32 devices in a mesh: dp: 4 (over x, core), seq: 8 (over z, y).
Axes of the slice: x: 2, y: 2, z: 4, core: 2. Of those that a mesh axis runs over, the one named last changes fastest.
Arguments:
- hidden: bfloat16 [4, 2048, 1024], P('dp', 'seq'), may hold values from -6 to 6
- group_sizes: int32 [4], P('dp'), may hold values from 4 to 16, as said below
- prefix_lens: int32 [4], P('dp'), may hold values from 128 to 1232, as said below
- sol_lens: int32 [4, 16], P('dp'), may hold values from 48 to 96, as said below
- ln1_gain: bfloat16 [1024], P(('dp', 'seq')), may hold values from 0.5 to 1.5
- ln1_shift: bfloat16 [1024], P(('dp', 'seq')), may hold values from -1 to 1
- qkv_weight: bfloat16 [1024, 3072], P(('dp', 'seq')), may hold values from -0.1875 to 0.1875
- qv_bias: bfloat16 [2048], P(('dp', 'seq')), may hold values from -1 to 1
- out_weight: bfloat16 [1024, 1024], P(('dp', 'seq')), may hold values from -2 to 2
- out_bias: bfloat16 [1024], P(('dp', 'seq')), may hold values from -1 to 1
- ln2_gain: bfloat16 [1024], P(('dp', 'seq')), may hold values from 0.5 to 1.5
- ln2_shift: bfloat16 [1024], P(('dp', 'seq')), may hold values from -1 to 1
- fc_weight: bfloat16 [1024, 4096], P(('dp', 'seq')), may hold values from -0.1875 to 0.1875
- fc_bias: bfloat16 [4096], P(('dp', 'seq')), may hold values from -1 to 1
- proj_weight: bfloat16 [4096, 1024], P(('dp', 'seq')), may hold values from -0.09375 to 0.09375
- proj_bias: bfloat16 [1024], P(('dp', 'seq')), may hold values from -1 to 1
- cotangent: bfloat16 [4, 2048, 1024], P('dp', 'seq'), may hold values from -6 to 6
Outputs:
- layer_out: bfloat16 [4, 2048, 1024], P('dp', 'seq')
- hidden_grad: bfloat16 [4, 2048, 1024], P('dp', 'seq')
- ln1_gain_grad: float32 [1024], P(('dp', 'seq'))
- ln1_shift_grad: float32 [1024], P(('dp', 'seq'))
- qkv_weight_grad: float32 [1024, 3072], P(('dp', 'seq'))
- qv_bias_grad: float32 [2048], P(('dp', 'seq'))
- out_weight_grad: float32 [1024, 1024], P(('dp', 'seq'))
- out_bias_grad: float32 [1024], P(('dp', 'seq'))
- ln2_gain_grad: float32 [1024], P(('dp', 'seq'))
- ln2_shift_grad: float32 [1024], P(('dp', 'seq'))
- fc_weight_grad: float32 [1024, 4096], P(('dp', 'seq'))
- fc_bias_grad: float32 [4096], P(('dp', 'seq'))
- proj_weight_grad: float32 [4096, 1024], P(('dp', 'seq'))
- proj_bias_grad: float32 [1024], P(('dp', 'seq'))
The draws below stay inside these ranges and needn't reach their ends.
Inputs may be any that keep to these rules, and one draw needn't show every extreme that they name: `group_sizes`: how many of the 16 solution slots a group uses; some group uses all 16, some group only 4. `prefix_lens`: positions of the shared prefix; a group's prefix and its used solutions fill at most 2048 positions, and one group of every draw fills exactly 2048. `sol_lens`: positions of each solution slot; slots at or beyond the group's size are unused.
All inputs are finite; a program needn't handle non-finite values.
Results may differ from the reference program's by a relative error of at most 0.012.
Values may be sent and summed in bfloat16 or wider, within the bound.
No kernel may reach another device: no remote copies, remote signals or barrier semaphores. Data moves between devices by JAX's collectives and lax.ppermute only.
A program may use at most 192 MiB of HBM per device.

```python
import jax
import jax.numpy as jnp
from jax import lax

D = 1024
H = 16
HD = 64
FF = 4096
SOLS = 16
GSLOT = 2048
QB = 512
GROUPS = 4


def plan_groups(key):
    base_key = jax.random.fold_in(key, 4242)
    key_size, key_lens, key_prefix, key_pick = jax.random.split(base_key, 4)
    longest = GSLOT * 3 // (4 * SOLS)
    shortest = longest // 2
    group_index = jnp.arange(GROUPS, dtype=jnp.int32)
    picked = jax.random.randint(key_pick, (), 0, GROUPS)
    opposite = (picked + GROUPS // 2) % GROUPS
    counts = jax.random.randint(key_size, (GROUPS,), 4, SOLS + 1)
    counts = jnp.where(group_index == picked, SOLS, jnp.where(group_index == opposite, 4, counts))
    lengths = jax.random.randint(key_lens, (GROUPS, SOLS), shortest, longest + 1)
    slot_ids = jnp.arange(SOLS, dtype=jnp.int32)
    picked_row = (group_index == picked)[:, None]
    lengths = jnp.where(picked_row, jnp.where(slot_ids[None, :] == 0, longest, shortest), lengths)
    in_use = (slot_ids[None, :] < counts[:, None]).astype(jnp.int32)
    spent = jnp.sum(lengths * in_use, axis=1)
    prefixes = jax.random.randint(key_prefix, (GROUPS,), GSLOT // 16, GSLOT // 4 + 1)
    prefixes = jnp.where(group_index == picked, GSLOT - spent, jnp.where(group_index == opposite, GSLOT // 16, prefixes))
    return (counts.astype(jnp.int32), prefixes.astype(jnp.int32), lengths.astype(jnp.int32))


def draw_group_sizes(key, part):
    return plan_groups(key)[0]


def draw_prefix_lens(key, part):
    return plan_groups(key)[1]


def draw_sol_lens(key, part):
    return plan_groups(key)[2]


def spiked(array, own_key, source, target, blocks, factor):
    owner, partner = [(jnp.arange(array.shape[axis_at]) // (array.shape[axis_at] // blocks)).reshape([-1 if axis == axis_at else 1 for axis in range(array.ndim)]) for axis_at in (source, target)]
    chosen = jax.random.permutation(own_key, blocks)[partner]
    strong = (owner == chosen) | (owner == (partner + blocks // 2) % blocks)
    return jnp.where(strong, factor * array, array)


def block_scale(own_key, shape, cuts, least, high):
    loudness, own = 1.0, jax.random.fold_in(own_key, 6)
    for dim, parts in cuts:
        steps = jnp.exp(jax.random.uniform(jax.random.fold_in(own, dim), (parts,), jnp.float32, least / len(cuts), high / len(cuts)))
        loudness = loudness * jnp.repeat(steps, shape[dim] // parts).reshape([-1 if axis == dim else 1 for axis in range(len(shape))])
    return loudness


def bell_draw(key, dims, spread, most, pieces=(), kind=jnp.bfloat16):
    array = spread * jax.random.normal(key, dims, jnp.float32)
    if pieces:
        array = array * block_scale(key, dims, pieces, -0.22, 0.18)
    return jnp.clip(array, -most, most).astype(kind)


def gaussian_with(stream_key, dims, width, most, pieces, heavy, held_as=jnp.bfloat16):
    array = width * jax.random.normal(stream_key, dims, jnp.float32)
    if pieces:
        array = array * block_scale(stream_key, dims, pieces, -0.22, 0.18)
    return jnp.clip(spiked(array, jax.random.fold_in(stream_key, 3), *heavy), -most, most).astype(held_as)


def setup_inputs(seed: int = 0) -> dict:
    key_of = jax.random.split(jax.random.key(seed), 18)
    return {
        "hidden": bell_draw(key_of[0], (GROUPS, GSLOT, D), 1.0, 6.0, ((0, 4), (1, 8))),
        "group_sizes": draw_group_sizes(jax.random.fold_in(key_of[17], 71), 0),
        "prefix_lens": draw_prefix_lens(jax.random.fold_in(key_of[17], 71), 0),
        "sol_lens": draw_sol_lens(jax.random.fold_in(key_of[17], 71), 0),
        "ln1_gain": jnp.clip(1.0 + 0.1 * jax.random.normal(key_of[4], (D,), jnp.float32), 0.5, 1.5).astype(jnp.bfloat16),
        "ln1_shift": bell_draw(key_of[5], (D,), 0.2, 1.0, ((0, 32),)),
        "qkv_weight": bell_draw(key_of[6], (D, 3 * D), D ** -0.5, 0.1875, ((0, 32),)),
        "qv_bias": bell_draw(key_of[7], (2 * D,), 0.2, 1.0, ((0, 32),)),
        "out_weight": bell_draw(key_of[8], (D, D), (D * 16 // GSLOT) ** -0.5, 2.0, ((0, 32),)),
        "out_bias": bell_draw(key_of[9], (D,), 0.2, 1.0, ((0, 32),)),
        "ln2_gain": jnp.clip(1.0 + 0.1 * jax.random.normal(key_of[10], (D,), jnp.float32), 0.5, 1.5).astype(jnp.bfloat16),
        "ln2_shift": bell_draw(key_of[11], (D,), 0.2, 1.0, ((0, 32),)),
        "fc_weight": bell_draw(key_of[12], (D, FF), D ** -0.5, 0.1875, ((0, 32),)),
        "fc_bias": bell_draw(key_of[13], (FF,), 0.2, 1.0, ((0, 32),)),
        "proj_weight": bell_draw(key_of[14], (FF, D), FF ** -0.5, 0.09375, ((0, 32),)),
        "proj_bias": bell_draw(key_of[15], (D,), 0.2, 1.0, ((0, 32),)),
        "cotangent": gaussian_with(key_of[16], (GROUPS, GSLOT, D), 1.0, 6.0, ((0, 4), (1, 8)), (1, 2, 8, 2.0)),
    }


@jax.custom_vjp
def low(v):
    return lax.optimization_barrier(v.astype(jnp.bfloat16)).astype(jnp.float32)

@jax.custom_vjp
def low_back(v):
    return v

def low_keep(v):
    return (low(v), None)

def low_pass(kept, grad):
    return (grad,)

def back_keep(v):
    return (v, None)

def back_low(kept, grad):
    return (low(grad),)
low.defvjp(low_keep, low_pass)
low_back.defvjp(back_keep, back_low)
EPSILON = 1e-05
MASK_FILL = -1e+30
HIGHEST_PREC = lax.Precision.HIGHEST

def product(left, right):
    return jnp.dot(left, right, precision=HIGHEST_PREC, preferred_element_type=jnp.float32)

def segment_table(group_sizes, prefix_lens, sol_lens, positions):
    slot_ids = jnp.arange(sol_lens.shape[1], dtype=jnp.int32)
    in_use = (slot_ids[None, :] < group_sizes[:, None]).astype(jnp.int32)
    seg_ends = prefix_lens[:, None] + jnp.cumsum(sol_lens * in_use, axis=1).astype(jnp.int32)
    passed = lax.optimization_barrier(jnp.sum((positions[None, :, None] >= seg_ends[:, None, :]).astype(jnp.int32), axis=2)).astype(jnp.int32)
    inside = positions[None, :] < seg_ends[:, -1:]
    after_pref = jnp.where(inside, passed + 1, -1)
    return jnp.where(positions[None, :] < prefix_lens[:, None], 0, after_pref).astype(jnp.int32)

def layer_norm(row_block, gain_vec, shift_vec):
    centred = row_block - lax.optimization_barrier(jnp.mean(row_block, axis=-1, keepdims=True))
    inverse = lax.rsqrt(lax.optimization_barrier(jnp.mean(centred * centred, axis=-1, keepdims=True)) + EPSILON)
    return centred * inverse * gain_vec + shift_vec

def attend(query_tok, key_tok, value_tok, seg_row):
    query_heads = query_tok.reshape(GSLOT, H, HD)
    key_heads = key_tok.reshape(GSLOT, H, HD)
    value_heads = value_tok.reshape(GSLOT, H, HD)
    positions = jnp.arange(GSLOT, dtype=jnp.int32)

    def one_block(row_start):
        row_block = lax.dynamic_slice_in_dim(query_heads, row_start, QB, 0)
        query_seg = lax.dynamic_slice_in_dim(seg_row, row_start, QB, 0)
        query_pos = row_start + jnp.arange(QB, dtype=jnp.int32)
        scores = low_back(jnp.einsum('qhd,khd->hqk', row_block, key_heads, precision=HIGHEST_PREC) * HD ** (-0.5))
        allowed = (positions[None, :] <= query_pos[:, None]) & ((seg_row[None, :] == 0) | (seg_row[None, :] == query_seg[:, None]))
        prob_low = low(jax.nn.softmax(jnp.where(allowed[None, :, :], scores, MASK_FILL), axis=-1))
        return jnp.einsum('hqk,khd->qhd', prob_low, value_heads, precision=HIGHEST_PREC)
    starts = jnp.arange(GSLOT // QB, dtype=jnp.int32) * QB
    return lax.map(jax.checkpoint(one_block), starts).reshape(GSLOT, D)

def gelu_tanh(pre_act):
    return jax.nn.gelu(pre_act, approximate=True)

def group_layer(weights, inputs, seg_row):
    ln1_gain, ln1_shift, qkv_weight, qv_bias, out_weight, out_bias, ln2_gain, ln2_shift, fc_weight, fc_bias, proj_weight, proj_bias = weights
    valid_rows = (seg_row >= 0).astype(jnp.float32)[:, None]
    first = low(layer_norm(inputs, ln1_gain, ln1_shift))
    query_tok = low_back(low(product(first, qkv_weight[:, :D]) + qv_bias[:D]))
    key_tok = low_back(low(product(first, qkv_weight[:, D:2 * D])))
    value_tok = low_back(low(product(first, qkv_weight[:, 2 * D:]) + qv_bias[D:]))
    attended = low_back(low(attend(query_tok, key_tok, value_tok, seg_row)))
    resid = inputs + low_back(product(attended, out_weight)) + out_bias
    second = low(layer_norm(resid, ln2_gain, ln2_shift))
    pre_act = low_back(product(second, fc_weight) + fc_bias)
    activated = low(gelu_tanh(pre_act))
    return valid_rows * (resid + product(activated, proj_weight) + proj_bias)

def reference(hidden, group_sizes, prefix_lens, sol_lens, ln1_gain, ln1_shift, qkv_weight, qv_bias, out_weight, out_bias, ln2_gain, ln2_shift, fc_weight, fc_bias, proj_weight, proj_bias, cotangent):
    seg_all = segment_table(group_sizes, prefix_lens, sol_lens, jnp.arange(GSLOT, dtype=jnp.int32))
    params = tuple((tensor.astype(jnp.float32) for tensor in (ln1_gain, ln1_shift, qkv_weight, qv_bias, out_weight, out_bias, ln2_gain, ln2_shift, fc_weight, fc_bias, proj_weight, proj_bias)))
    inputs = hidden.astype(jnp.float32)

    def forward(weights, all_rows):

        def one_group(group_pair):
            return group_layer(weights, group_pair[0], group_pair[1])
        return lax.map(jax.checkpoint(one_group), (all_rows, seg_all))
    result, pull_back = jax.vjp(forward, params, inputs)
    gradients, d_hidden = pull_back(cotangent.astype(jnp.float32))
    return (result.astype(jnp.bfloat16), d_hidden.astype(jnp.bfloat16), gradients[0], gradients[1], gradients[2], gradients[3], gradients[4], gradients[5], gradients[6], gradients[7], gradients[8], gradients[9], gradients[10], gradients[11])
```

```python
import functools

import jax
import jax.numpy as jnp
from jax import lax
from jax.experimental import pallas as pl
from jax.experimental.pallas import tpu as pltpu
from jax.sharding import Mesh
from jax.sharding import PartitionSpec as P

HD = 64
EPSILON = 1e-05
BIG = 1e30
BLOCK = 256
F32 = jnp.float32
BF16 = jnp.bfloat16
ALL = ("x", "c", "z", "y")
SEQ = ("z", "y")
SWAP = [(0, 1), (1, 0)]


def dot_nt(a, b):
    return lax.dot_general(a, b, (((1,), (1,)), ((), ())), preferred_element_type=F32)


def dot_nn(a, b):
    return lax.dot_general(a, b, (((1,), (0,)), ((), ())), preferred_element_type=F32)


def dot_tn(a, b):
    return lax.dot_general(a, b, (((0,), (0,)), ((), ())), preferred_element_type=F32)


def segment_code(ends_ref, start, rows, lanes):
    pos = start + lax.broadcasted_iota(jnp.int32, (rows, lanes), 0)
    passed = jnp.ones((rows, lanes), jnp.int32)
    for t in range(16):
        passed = passed + jnp.where(pos >= ends_ref[1 + t], 1, 0)
    code = jnp.where(pos < ends_ref[16], passed, 17)
    return jnp.where(pos < ends_ref[0], 0, code)


def with_segments(keys, queries, ends_ref, start):
    rows, lanes = keys.shape
    code = segment_code(ends_ref, start, rows, lanes)
    lane = lax.broadcasted_iota(jnp.int32, (rows, lanes), 1)
    key_mark = jnp.where((code == lane) & (code > 0), 1.0, 0.0).astype(BF16)
    query_mark = jnp.where(code == lane, 0.0, -BIG).astype(BF16)
    return jnp.concatenate([keys, key_mark], axis=1), query_mark


def head_part(array, head, heads):
    if heads == 1:
        return array
    lane = lax.broadcasted_iota(jnp.int32, array.shape, 1)
    return jnp.where((lane >= head * HD) & (lane < (head + 1) * HD), array, jnp.zeros_like(array))


def merge_heads(parts):
    out = parts[0]
    if len(parts) > 1:
        lane = lax.broadcasted_iota(jnp.int32, out.shape, 1)
        for head in range(1, len(parts)):
            out = jnp.where(lane >= head * HD, parts[head], out)
    return out


def causal(rows, cols, transposed):
    row = lax.broadcasted_iota(jnp.int32, (rows, cols), 0)
    col = lax.broadcasted_iota(jnp.int32, (rows, cols), 1)
    return (row <= col) if transposed else (col <= row)


def attend_kernel(heads, ends_ref, qkv_ref, out_ref, wide_ref, lse_ref, keys, values, scores):
    i = pl.program_id(0)
    width = heads * HD
    start = pl.multiple_of(i * BLOCK, BLOCK)
    tagged, query_mark = with_segments(qkv_ref[:, width : 2 * width], None, ends_ref, start)
    keys[pl.ds(start, BLOCK), :] = tagged
    values[pl.ds(start, BLOCK), :] = qkv_ref[:, 2 * width :]
    scaled = qkv_ref[:, :width] * BF16(HD**-0.5)
    query = [
        jnp.concatenate([head_part(scaled, h, heads), query_mark], axis=1) for h in range(heads)
    ]

    def fold(array, op):
        out = array[:, :128]
        for at in range(128, BLOCK, 128):
            out = op(out, array[:, at : at + 128])
        return out

    def first(j, tops):
        block = keys[pl.ds(pl.multiple_of(j * BLOCK, BLOCK), BLOCK), :]
        new = []
        for h in range(heads):
            score = dot_nt(query[h], block)
            scores[h, j] = score
            new.append(jnp.maximum(tops[h], fold(score, jnp.maximum)))
        return tuple(new)

    tops = []
    for h in range(heads):
        score = jnp.where(causal(BLOCK, BLOCK, False), dot_nt(query[h], tagged), -BIG)
        scores[h, i] = score
        tops.append(fold(score, jnp.maximum))
    tops = lax.fori_loop(0, i, first, tuple(tops))
    tops = [jnp.max(t, axis=1, keepdims=True) for t in tops]

    def second(j, carry):
        sums, accs = carry
        block = values[pl.ds(pl.multiple_of(j * BLOCK, BLOCK), BLOCK), :]
        new_sums, new_accs = [], []
        for h in range(heads):
            expo = jnp.exp(scores[h, j] - tops[h])
            new_sums.append(sums[h] + fold(expo, jnp.add))
            new_accs.append(accs[h] + dot_nn(expo.astype(BF16), block))
        return tuple(new_sums), tuple(new_accs)

    zero = tuple(jnp.zeros((BLOCK, 128), F32) for _ in range(heads))
    zero_acc = tuple(jnp.zeros((BLOCK, width), F32) for _ in range(heads))
    sums, accs = lax.fori_loop(0, i + 1, second, (zero, zero_acc))
    sums = [jnp.sum(t, axis=1, keepdims=True) for t in sums]
    wide = merge_heads([accs[h] / sums[h] for h in range(heads)])
    wide_ref[...] = wide
    out_ref[...] = wide.astype(BF16)
    for h in range(heads):
        lse = jnp.broadcast_to(tops[h] + jnp.log(sums[h]), (BLOCK, 128))
        lse_ref[h : h + 1, :] = lse.T[0:1, :]


def attend(qkv, ends, heads):
    length, width = qkv.shape[0], heads * HD
    return pl.pallas_call(
        functools.partial(attend_kernel, heads),
        name="attend",
        grid=(length // BLOCK,),
        in_specs=[
            pl.BlockSpec(memory_space=pltpu.SMEM),
            pl.BlockSpec((BLOCK, 3 * width), lambda i: (i, 0)),
        ],
        out_specs=[
            pl.BlockSpec((BLOCK, width), lambda i: (i, 0)),
            pl.BlockSpec((BLOCK, width), lambda i: (i, 0)),
            pl.BlockSpec((8, BLOCK), lambda i: (0, i)),
        ],
        out_shape=[
            jax.ShapeDtypeStruct((length, width), BF16),
            jax.ShapeDtypeStruct((length, width), F32),
            jax.ShapeDtypeStruct((8, length), F32),
        ],
        scratch_shapes=[
            pltpu.VMEM((length, 2 * width), BF16),
            pltpu.VMEM((length, width), BF16),
            pltpu.VMEM((heads, length // BLOCK, BLOCK, BLOCK), F32),
        ],
        compiler_params=pltpu.CompilerParams(vmem_limit_bytes=32 << 20),
        cost_estimate=pl.CostEstimate(
            flops=heads * length * length * 512, bytes_accessed=4 << 20, transcendentals=heads * length * length // 2
        ),
    )(ends, qkv)


def attend_back_kernel(
    heads, ends_ref, qkv_ref, wide_ref, lse_ref, up_ref, out_ref, keys, values, key_acc, value_acc, query_acc
):
    i = pl.program_id(0)
    width = heads * HD
    start = pl.multiple_of(i * BLOCK, BLOCK)
    tagged, query_mark = with_segments(qkv_ref[:, width : 2 * width], None, ends_ref, start)
    keys[pl.ds(start, BLOCK), :] = tagged
    values[pl.ds(start, BLOCK), :] = qkv_ref[:, 2 * width :]
    key_acc[pl.ds(start, BLOCK), :] = jnp.zeros((BLOCK, width), F32)
    value_acc[pl.ds(start, BLOCK), :] = jnp.zeros((BLOCK, width), F32)
    scaled = qkv_ref[:, :width] * BF16(HD**-0.5)
    up = up_ref[...]
    part = [head_part(scaled, h, heads) for h in range(heads)]
    up_part = [head_part(up, h, heads) for h in range(heads)]
    query = [jnp.concatenate([part[h], query_mark], axis=1) for h in range(heads)]
    inner = (up.astype(F32) * wide_ref[...]).T
    inner = [jnp.sum(inner[h * HD : (h + 1) * HD, :], axis=0, keepdims=True) for h in range(heads)]
    lse = [lse_ref[h : h + 1, :] for h in range(heads)]
    part_all = jnp.concatenate(part, axis=0)
    up_all = jnp.concatenate(up_part, axis=0)
    for h in range(heads):
        query_acc[h] = jnp.zeros((BLOCK, width), F32)

    def step(j, diagonal):
        rows = pl.ds(pl.multiple_of(j * BLOCK, BLOCK), BLOCK)
        block, value = keys[rows, :], values[rows, :]
        probs, scores = [], []
        for h in range(heads):
            score = dot_nt(block, query[h])
            if diagonal:
                score = jnp.where(causal(BLOCK, BLOCK, True), score, -BIG)
            prob = jnp.exp(score - lse[h])
            d_prob = dot_nt(value, up_part[h])
            d_score = (prob * (d_prob - inner[h])).astype(BF16)
            probs.append(prob.astype(BF16))
            scores.append(d_score)
            query_acc[h] += dot_tn(d_score, block[:, :width])
        value_acc[rows, :] += dot_nn(jnp.concatenate(probs, axis=1), up_all)
        key_acc[rows, :] += dot_nn(jnp.concatenate(scores, axis=1), part_all)

    step(i, True)

    def body(j, carry):
        step(j, False)
        return carry

    lax.fori_loop(0, i, body, 0)
    d_query = merge_heads([query_acc[h] for h in range(heads)]) * HD**-0.5
    out_ref[pl.ds(start, BLOCK), :width] = d_query.astype(BF16)

    @pl.when(i == pl.num_programs(0) - 1)
    def _():
        out_ref[:, width : 2 * width] = key_acc[...].astype(BF16)
        out_ref[:, 2 * width :] = value_acc[...].astype(BF16)


def attend_back(qkv, wide, lse, up, ends, heads):
    length, width = qkv.shape[0], heads * HD
    return pl.pallas_call(
        functools.partial(attend_back_kernel, heads),
        name="attend_back",
        grid=(length // BLOCK,),
        in_specs=[
            pl.BlockSpec(memory_space=pltpu.SMEM),
            pl.BlockSpec((BLOCK, 3 * width), lambda i: (i, 0)),
            pl.BlockSpec((BLOCK, width), lambda i: (i, 0)),
            pl.BlockSpec((8, BLOCK), lambda i: (0, i)),
            pl.BlockSpec((BLOCK, width), lambda i: (i, 0)),
        ],
        out_specs=pl.BlockSpec((length, 3 * width), lambda i: (0, 0)),
        out_shape=jax.ShapeDtypeStruct((length, 3 * width), BF16),
        scratch_shapes=[
            pltpu.VMEM((length, 2 * width), BF16),
            pltpu.VMEM((length, width), BF16),
            pltpu.VMEM((length, width), F32),
            pltpu.VMEM((length, width), F32),
            pltpu.VMEM((heads, BLOCK, width), F32),
        ],
        compiler_params=pltpu.CompilerParams(vmem_limit_bytes=32 << 20),
        cost_estimate=pl.CostEstimate(
            flops=heads * length * length * 1280, bytes_accessed=6 << 20, transcendentals=heads * length * length // 2
        ),
    )(ends, qkv, wide, lse, up)


def layer_stats(rows):
    centred = rows - jnp.mean(rows, axis=-1, keepdims=True)
    inverse = lax.rsqrt(jnp.mean(centred * centred, axis=-1, keepdims=True) + EPSILON)
    return centred * inverse, inverse


def layer_back(upstream, normed, inverse, gain):
    scaled = upstream * gain
    return inverse * (
        scaled
        - jnp.mean(scaled, axis=-1, keepdims=True)
        - normed * jnp.mean(scaled * normed, axis=-1, keepdims=True)
    )


def gelu_tanh(pre):
    return jax.nn.gelu(pre, approximate=True)


def pick(array, index, dim):
    return lax.dynamic_index_in_dim(array, index, dim, keepdims=False)


def swap(array):
    return lax.ppermute(array, "c", SWAP)


def scatter_sum(array, axis, dim):
    size, me = array.shape[dim], lax.axis_index(axis)
    total = pick(array, me, dim).astype(F32)
    for k in range(1, size):
        sent = pick(array, (me + k) % size, dim)
        total = total + lax.ppermute(sent, axis, [(i, (i + k) % size) for i in range(size)]).astype(F32)
    return total


def per_device(sizes, *args):
    (
        hidden, group_sizes, prefix_lens, sol_lens, ln1_gain, ln1_shift, qkv_weight, qv_bias, out_weight, out_bias,
        ln2_gain, ln2_shift, fc_weight, fc_bias, proj_weight, proj_bias, cotangent,
    ) = args
    X, Z, Y = sizes
    S, ND = Z * Y, 2 * X * Z * Y
    _, T, D = hidden.shape
    FF = fc_weight.shape[1]
    per_core = D // HD // 2
    heads = 2 * per_core // S
    wd, chunks = heads * HD, S // 2
    half, ffh = D // 2, FF // 2
    c, place = lax.axis_index("c"), lax.axis_index(SEQ)
    x_at = lax.axis_index("x")

    small = (ln1_gain, ln1_shift, qv_bias, out_bias, ln2_gain, ln2_shift, fc_bias, proj_bias)
    cuts = [0]
    for part in small:
        cuts.append(cuts[-1] + part.shape[0])
    packed = jnp.broadcast_to(jnp.concatenate(small)[None, :], (ND, cuts[-1]))
    packed = lax.all_to_all(packed, ALL, split_axis=0, concat_axis=0, tiled=True).astype(F32)
    gain1, shift1, qv_all, out_b, gain2, shift2, fc_b, proj_b = (
        packed[:, cuts[n] : cuts[n + 1]].reshape(-1) for n in range(8)
    )

    qkv_full = lax.all_gather(qkv_weight, ALL, axis=0, tiled=True)
    narrow = jnp.concatenate(
        [fc_weight[:, at : at + D] for at in range(0, FF, D)] + [proj_weight, out_weight], axis=0
    )
    rest, _ = lax.optimization_barrier((narrow, qkv_full[0, 0]))
    rest = lax.all_gather(rest, ALL, axis=0, tiled=False)

    slot = jnp.arange(sol_lens.shape[1], dtype=jnp.int32)
    used = jnp.where(slot < group_sizes[0], sol_lens[0], 0)
    ends = prefix_lens[0] + jnp.sum(jnp.where(slot[None, :] <= slot[:, None], used[None, :], 0), axis=1)
    meta = jnp.concatenate([prefix_lens, ends, jnp.zeros((15,), jnp.int32)])
    metas = jnp.stack([meta, swap(meta)])
    meta_here = jnp.where(place < chunks, metas[0], metas[1])
    position = place * T + jnp.arange(T, dtype=jnp.int32)
    valid = (position[None, :] < metas[:, 16:17]).astype(F32).reshape(2 * T, 1)

    both = jnp.concatenate([hidden[0], swap(hidden[0])], axis=0).astype(F32)
    up_own = cotangent[0]
    d_out = valid * jnp.concatenate([up_own, swap(up_own)], axis=0).astype(F32)
    d_out_low = d_out.astype(BF16)

    norm1, inv1 = layer_stats(both)
    first = (norm1 * gain1 + shift1).astype(BF16)
    w_qkv = pick(qkv_full.reshape(D, 3, X, 2, half // X), c, 3)
    w_qkv = w_qkv.reshape(D, 3, chunks, wd).transpose(0, 2, 1, 3).reshape(D, 3 * half)
    qv_here = pick(qv_all.reshape(2, X, 2, half // X), c, 2).reshape(2, chunks, 1, wd)
    bias = jnp.concatenate([qv_here[0], jnp.zeros_like(qv_here[0]), qv_here[1]], axis=1).reshape(-1)
    joint = (jnp.dot(first, w_qkv, preferred_element_type=F32) + bias).astype(BF16)

    def to_heads(array):
        array = array.reshape(2, T, chunks, -1).transpose(0, 2, 1, 3).reshape(S, T, -1)
        out = lax.all_to_all(array, SEQ, split_axis=0, concat_axis=0, tiled=True)
        return out.reshape(S * T, -1)

    def to_rows(array):
        out = lax.all_to_all(array.reshape(S, T, -1), SEQ, split_axis=0, concat_axis=0, tiled=True)
        return out.reshape(2, chunks, T, -1).transpose(0, 2, 1, 3).reshape(2 * T, -1)

    qkv = to_heads(joint)
    att, att_wide, lse = attend(qkv, meta_here, heads)
    mine = to_rows(att)
    theirs = swap(mine)
    theirs = jnp.concatenate([theirs[T:], theirs[:T]], axis=0)

    rows = D // ND
    fc_rows = rows * (FF // D)
    fc_full = rest[:, :fc_rows].reshape(ND, FF // D, rows, D).transpose(0, 2, 1, 3).reshape(D, X, 2, ffh // X)
    w_fc = pick(fc_full, c, 2).reshape(D, ffh)
    w_proj = pick(rest[:, fc_rows : fc_rows + FF // ND].reshape(X, 2, S, FF // ND, D), c, 1).reshape(ffh, D)
    out_full = rest[:, fc_rows + FF // ND :].reshape(X, 2, half // X, D)
    w_out = pick(out_full, c, 1).reshape(half, D)
    w_out_other = pick(out_full, 1 - c, 1).reshape(half, D)

    resid = (
        both
        + jnp.dot(mine, w_out, preferred_element_type=F32)
        + jnp.dot(theirs, w_out_other, preferred_element_type=F32)
        + out_b
    )
    norm2, inv2 = layer_stats(resid)
    second = (norm2 * gain2 + shift2).astype(BF16)
    fc_b_here = pick(fc_b.reshape(X, 2, ffh // X), c, 1).reshape(-1)
    pre = jnp.dot(second, w_fc, preferred_element_type=F32) + fc_b_here
    act, gelu_pull = jax.vjp(gelu_tanh, pre)
    act = act.astype(BF16)
    part_out = jnp.dot(act, w_proj, preferred_element_type=F32)
    layer_out = valid[:T] * (
        resid[:T] + (part_out[:T] + swap(part_out[T:].astype(BF16)).astype(F32)) + proj_b
    )

    d_act = dot_nt(d_out_low, w_proj)
    d_pre = gelu_pull(d_act)[0].astype(BF16)
    part_second = dot_nt(d_pre, w_fc)
    other = swap(part_second.astype(BF16)).astype(F32)
    d_second = part_second + jnp.concatenate([other[T:], other[:T]], axis=0)
    d_resid = d_out + layer_back(d_second, norm2, inv2, gain2)
    d_resid_low = d_resid.astype(BF16)
    d_att = dot_nt(d_resid_low, w_out).astype(BF16)
    up = to_heads(d_att)

    fc_grad = dot_tn(second, d_pre).astype(BF16).reshape(X, 2, Z, Y, rows, ffh)
    proj_grad = dot_tn(act, d_out_low).astype(BF16).reshape(X, Z, Y, FF // ND, D)
    out_grad = dot_tn(mine, d_resid_low).astype(BF16).reshape(X, Z, Y, rows, D)
    fc_grad = scatter_sum(fc_grad, "x", 0).astype(BF16)
    proj_grad = scatter_sum(proj_grad, "y", 2).astype(BF16)
    fc_grad = scatter_sum(fc_grad, "y", 2).astype(BF16)
    proj_grad = scatter_sum(proj_grad, "x", 0).astype(BF16)
    fc_grad = scatter_sum(fc_grad, "z", 1)
    proj_grad = scatter_sum(proj_grad, "z", 0)
    out_grad = scatter_sum(out_grad, "x", 0).astype(BF16)
    out_grad = scatter_sum(out_grad, "y", 1).astype(BF16)
    out_grad = scatter_sum(out_grad, "z", 0)

    def both_halves(grad, blocks):
        kept = pick(grad, c, 0)
        got = swap(pick(grad, 1 - c, 0).astype(BF16)).astype(F32)
        shape = (kept.shape[0],) + blocks
        kept, got = kept.reshape(shape), got.reshape(shape)
        low = jnp.where(c == 0, kept, got)
        high = jnp.where(c == 0, got, kept)
        return jnp.stack([low, high], axis=-2).reshape(kept.shape[0], -1)

    fc_grad = both_halves(fc_grad, (X, ffh // X))

    d_qkv = to_rows(attend_back(qkv, att_wide, lse, up, meta_here, heads))
    qkv_grad = dot_tn(first, d_qkv).astype(BF16).reshape(X, 2, Z, Y, rows, 2, 3 * half // 2)
    part_first = dot_nt(d_qkv, w_qkv)
    d_first = part_first[:T] + swap(part_first[T:].astype(BF16)).astype(F32)
    own_norm, own_inv = norm1[:T], inv1[:T]
    hidden_grad = d_resid[:T] + layer_back(d_first, own_norm, own_inv, gain1)

    grad_a = scatter_sum(qkv_grad[..., 0, :], "x", 0).astype(BF16)
    grad_b = scatter_sum(qkv_grad[..., 1, :], "y", 3).astype(BF16)
    grad_a = scatter_sum(grad_a, "y", 2).astype(BF16)
    grad_b = scatter_sum(grad_b, "x", 0).astype(BF16)
    grad_a = scatter_sum(grad_a, "z", 1)
    grad_b = scatter_sum(grad_b, "z", 1)
    qkv_grad = jnp.concatenate([grad_a, grad_b], axis=-1)
    qkv_grad = qkv_grad.reshape(2, rows, chunks, 3, wd).transpose(0, 1, 3, 2, 4).reshape(2, rows, 3 * half)
    qkv_grad = both_halves(qkv_grad, (3, X, half // X))

    def own_columns(vector, lead):
        cut = vector.reshape(lead, X, 1, -1)
        at = lax.broadcasted_iota(jnp.int32, (lead, X, 2, cut.shape[-1]), 2)
        return jnp.where(at == c, cut, 0.0).reshape(-1)

    qkv_sum = jnp.sum(d_qkv.astype(F32), axis=0).reshape(chunks, 3, wd)
    qv_sum = jnp.stack([qkv_sum[:, 0], qkv_sum[:, 2]])
    sums = (
        jnp.sum(d_first * own_norm, axis=0),
        jnp.sum(d_first, axis=0),
        own_columns(qv_sum, 2),
        jnp.sum(d_resid[:T], axis=0),
        jnp.sum(d_second[:T] * norm2[:T], axis=0),
        jnp.sum(d_second[:T], axis=0),
        own_columns(jnp.sum(d_pre.astype(F32), axis=0), 1),
        jnp.sum(d_out[:T], axis=0),
    )
    packed = jnp.concatenate([v.reshape(ND, -1) for v in sums], axis=1)
    packed = jnp.sum(lax.all_to_all(packed, ALL, split_axis=0, concat_axis=0, tiled=True), axis=0)
    gain1_g, shift1_g, qv_g, out_b_g, gain2_g, shift2_g, fc_b_g, proj_b_g = (
        packed[cuts[n] : cuts[n + 1]] for n in range(8)
    )
    return (
        layer_out.astype(BF16)[None], hidden_grad.astype(BF16)[None], gain1_g, shift1_g, qkv_grad, qv_g, out_grad,
        out_b_g, gain2_g, shift2_g, fc_grad, fc_b_g, proj_grad, proj_b_g,
    )


def solution(mesh):
    Z = 4
    X, Y = mesh.shape["dp"] // 2, mesh.shape["seq"] // Z
    split = Mesh(mesh.devices.reshape(X, 2, Z, Y), ALL)
    group, wide, flat = P(("x", "c"), SEQ, None), P(ALL, None), P(ALL)
    dp = P(("x", "c"))
    return jax.shard_map(
        functools.partial(per_device, (X, Z, Y)),
        mesh=split,
        in_specs=(
            group, dp, dp, P(("x", "c"), None), flat, flat, wide, flat, wide, flat, flat, flat, wide, flat, wide, flat,
            group,
        ),
        out_specs=(
            group, group, flat, flat, wide, flat, wide, flat, flat, flat, wide, flat, wide, flat,
        ),
        check_vma=False,
    )
```

```python
import functools

import jax
import jax.numpy as jnp
from jax import lax
from jax.experimental import pallas as pl
from jax.experimental.pallas import tpu as pltpu
from jax.sharding import Mesh
from jax.sharding import PartitionSpec as P

HD = 64
EPSILON = 1e-05
BIG = 1e30
BLOCK = 256
F32 = jnp.float32
BF16 = jnp.bfloat16
ALL = ("x", "c", "z", "y")
SEQ = ("z", "y")
SWAP = [(0, 1), (1, 0)]


def dot_nt(a, b):
    return lax.dot_general(a, b, (((1,), (1,)), ((), ())), preferred_element_type=F32)


def dot_nn(a, b):
    return lax.dot_general(a, b, (((1,), (0,)), ((), ())), preferred_element_type=F32)


def dot_tn(a, b):
    return lax.dot_general(a, b, (((0,), (0,)), ((), ())), preferred_element_type=F32)


def segment_code(ends_ref, start, rows, lanes):
    pos = start + lax.broadcasted_iota(jnp.int32, (rows, lanes), 0)
    passed = jnp.ones((rows, lanes), jnp.int32)
    for t in range(16):
        passed = passed + jnp.where(pos >= ends_ref[1 + t], 1, 0)
    code = jnp.where(pos < ends_ref[16], passed, 17)
    return jnp.where(pos < ends_ref[0], 0, code)


def with_segments(keys, ends_ref, start):
    rows, lanes = keys.shape
    code = segment_code(ends_ref, start, rows, lanes)
    lane = lax.broadcasted_iota(jnp.int32, (rows, lanes), 1)
    key_mark = jnp.where((code == lane) & (code > 0), 1.0, 0.0).astype(BF16)
    query_mark = jnp.where(code == lane, 0.0, -BIG).astype(BF16)
    return jnp.concatenate([keys, key_mark], axis=1), query_mark


def head_part(array, head, heads):
    if heads == 1:
        return array
    lane = lax.broadcasted_iota(jnp.int32, array.shape, 1)
    return jnp.where((lane >= head * HD) & (lane < (head + 1) * HD), array, jnp.zeros_like(array))


def merge_heads(parts):
    out = parts[0]
    if len(parts) > 1:
        lane = lax.broadcasted_iota(jnp.int32, out.shape, 1)
        for head in range(1, len(parts)):
            out = jnp.where(lane >= head * HD, parts[head], out)
    return out


def causal(rows, cols, transposed):
    row = lax.broadcasted_iota(jnp.int32, (rows, cols), 0)
    col = lax.broadcasted_iota(jnp.int32, (rows, cols), 1)
    return (row <= col) if transposed else (col <= row)


def attend_kernel(heads, ends_ref, qkv_ref, out_ref, wide_ref, lse_ref, keys, values, scores):
    i = pl.program_id(0)
    width = heads * HD
    start = pl.multiple_of(i * BLOCK, BLOCK)
    query_in, keys_in, values_in = (qkv_ref[:, t].reshape(BLOCK, width) for t in range(3))
    tagged, query_mark = with_segments(keys_in, ends_ref, start)
    keys[pl.ds(start, BLOCK), :] = tagged
    values[pl.ds(start, BLOCK), :] = values_in
    scaled = query_in * BF16(HD**-0.5)
    query = [
        jnp.concatenate([head_part(scaled, h, heads), query_mark], axis=1) for h in range(heads)
    ]

    def fold(array, op):
        out = array[:, :128]
        for at in range(128, BLOCK, 128):
            out = op(out, array[:, at : at + 128])
        return out

    def first(j, tops):
        block = keys[pl.ds(pl.multiple_of(j * BLOCK, BLOCK), BLOCK), :]
        new = []
        for h in range(heads):
            score = dot_nt(query[h], block)
            scores[h, j] = score
            new.append(jnp.maximum(tops[h], fold(score, jnp.maximum)))
        return tuple(new)

    tops = []
    for h in range(heads):
        score = jnp.where(causal(BLOCK, BLOCK, False), dot_nt(query[h], tagged), -BIG)
        scores[h, i] = score
        tops.append(fold(score, jnp.maximum))
    tops = lax.fori_loop(0, i, first, tuple(tops))
    tops = [jnp.max(t, axis=1, keepdims=True) for t in tops]

    def second(j, carry):
        sums, accs = carry
        block = values[pl.ds(pl.multiple_of(j * BLOCK, BLOCK), BLOCK), :]
        new_sums, new_accs = [], []
        for h in range(heads):
            expo = jnp.exp(scores[h, j] - tops[h])
            new_sums.append(sums[h] + fold(expo, jnp.add))
            new_accs.append(accs[h] + dot_nn(expo.astype(BF16), block))
        return tuple(new_sums), tuple(new_accs)

    zero = tuple(jnp.zeros((BLOCK, 128), F32) for _ in range(heads))
    zero_acc = tuple(jnp.zeros((BLOCK, width), F32) for _ in range(heads))
    sums, accs = lax.fori_loop(0, i + 1, second, (zero, zero_acc))
    sums = [jnp.sum(t, axis=1, keepdims=True) for t in sums]
    wide = merge_heads([accs[h] / sums[h] for h in range(heads)])
    wide_ref[...] = wide
    out_ref[...] = wide.astype(BF16).reshape(out_ref.shape)
    for h in range(heads):
        lse = jnp.broadcast_to(tops[h] + jnp.log(sums[h]), (BLOCK, 128))
        lse_ref[h : h + 1, :] = lse.T[0:1, :]


def attend(qkv, ends, heads):
    length, width = qkv.shape[0] * qkv.shape[2], heads * HD
    T = qkv.shape[2]
    per = BLOCK // T
    return pl.pallas_call(
        functools.partial(attend_kernel, heads),
        name="attend",
        grid=(length // BLOCK,),
        in_specs=[
            pl.BlockSpec(memory_space=pltpu.SMEM),
            pl.BlockSpec((per, 3, T, width), lambda i: (i, 0, 0, 0)),
        ],
        out_specs=[
            pl.BlockSpec((per, T, width), lambda i: (i, 0, 0)),
            pl.BlockSpec((BLOCK, width), lambda i: (i, 0)),
            pl.BlockSpec((8, BLOCK), lambda i: (0, i)),
        ],
        out_shape=[
            jax.ShapeDtypeStruct((length // T, T, width), BF16),
            jax.ShapeDtypeStruct((length, width), F32),
            jax.ShapeDtypeStruct((8, length), F32),
        ],
        scratch_shapes=[
            pltpu.VMEM((length, 2 * width), BF16),
            pltpu.VMEM((length, width), BF16),
            pltpu.VMEM((heads, length // BLOCK, BLOCK, BLOCK), F32),
        ],
        compiler_params=pltpu.CompilerParams(vmem_limit_bytes=32 << 20),
        cost_estimate=pl.CostEstimate(
            flops=heads * length * length * 512, bytes_accessed=4 << 20, transcendentals=heads * length * length // 2
        ),
    )(ends, qkv)


def attend_back_kernel(
    heads, ends_ref, qkv_ref, wide_ref, lse_ref, up_ref, out_ref, keys, values, key_acc, value_acc, query_acc
):
    i = pl.program_id(0)
    width = heads * HD
    start = pl.multiple_of(i * BLOCK, BLOCK)
    query_in, keys_in, values_in = (qkv_ref[:, t].reshape(BLOCK, width) for t in range(3))
    tagged, query_mark = with_segments(keys_in, ends_ref, start)
    keys[pl.ds(start, BLOCK), :] = tagged
    values[pl.ds(start, BLOCK), :] = values_in
    key_acc[pl.ds(start, BLOCK), :] = jnp.zeros((BLOCK, width), F32)
    value_acc[pl.ds(start, BLOCK), :] = jnp.zeros((BLOCK, width), F32)
    scaled = query_in * BF16(HD**-0.5)
    up = up_ref[...].reshape(BLOCK, width)
    part = [head_part(scaled, h, heads) for h in range(heads)]
    up_part = [head_part(up, h, heads) for h in range(heads)]
    query = [jnp.concatenate([part[h], query_mark], axis=1) for h in range(heads)]
    inner = (up.astype(F32) * wide_ref[...]).T
    inner = [jnp.sum(inner[h * HD : (h + 1) * HD, :], axis=0, keepdims=True) for h in range(heads)]
    lse = [lse_ref[h : h + 1, :] for h in range(heads)]
    part_all = jnp.concatenate(part, axis=0)
    up_all = jnp.concatenate(up_part, axis=0)
    for h in range(heads):
        query_acc[h] = jnp.zeros((BLOCK, width), F32)

    def step(j, diagonal):
        rows = pl.ds(pl.multiple_of(j * BLOCK, BLOCK), BLOCK)
        block, value = keys[rows, :], values[rows, :]
        probs, scores = [], []
        for h in range(heads):
            score = dot_nt(block, query[h])
            if diagonal:
                score = jnp.where(causal(BLOCK, BLOCK, True), score, -BIG)
            prob = jnp.exp(score - lse[h])
            d_prob = dot_nt(value, up_part[h])
            d_score = (prob * (d_prob - inner[h])).astype(BF16)
            probs.append(prob.astype(BF16))
            scores.append(d_score)
            query_acc[h] += dot_tn(d_score, block[:, :width])
        value_acc[rows, :] += dot_nn(jnp.concatenate(probs, axis=1), up_all)
        key_acc[rows, :] += dot_nn(jnp.concatenate(scores, axis=1), part_all)

    step(i, True)

    def body(j, carry):
        step(j, False)
        return carry

    lax.fori_loop(0, i, body, 0)
    d_query = merge_heads([query_acc[h] for h in range(heads)]) * HD**-0.5
    T = out_ref.shape[2]
    per = BLOCK // T
    out_ref[pl.ds(i * per, per), 0] = d_query.astype(BF16).reshape(per, T, width)

    @pl.when(i == pl.num_programs(0) - 1)
    def _():
        for s in range(out_ref.shape[0]):
            out_ref[s, 1] = key_acc[s * T : (s + 1) * T, :].astype(BF16)
            out_ref[s, 2] = value_acc[s * T : (s + 1) * T, :].astype(BF16)


def attend_back(qkv, wide, lse, up, ends, heads):
    length, width = qkv.shape[0] * qkv.shape[2], heads * HD
    T = qkv.shape[2]
    per = BLOCK // T
    return pl.pallas_call(
        functools.partial(attend_back_kernel, heads),
        name="attend_back",
        grid=(length // BLOCK,),
        in_specs=[
            pl.BlockSpec(memory_space=pltpu.SMEM),
            pl.BlockSpec((per, 3, T, width), lambda i: (i, 0, 0, 0)),
            pl.BlockSpec((BLOCK, width), lambda i: (i, 0)),
            pl.BlockSpec((8, BLOCK), lambda i: (0, i)),
            pl.BlockSpec((per, T, width), lambda i: (i, 0, 0)),
        ],
        out_specs=pl.BlockSpec((length // T, 3, T, width), lambda i: (0, 0, 0, 0)),
        out_shape=jax.ShapeDtypeStruct((length // T, 3, T, width), BF16),
        scratch_shapes=[
            pltpu.VMEM((length, 2 * width), BF16),
            pltpu.VMEM((length, width), BF16),
            pltpu.VMEM((length, width), F32),
            pltpu.VMEM((length, width), F32),
            pltpu.VMEM((heads, BLOCK, width), F32),
        ],
        compiler_params=pltpu.CompilerParams(vmem_limit_bytes=32 << 20),
        cost_estimate=pl.CostEstimate(
            flops=heads * length * length * 1280, bytes_accessed=6 << 20, transcendentals=heads * length * length // 2
        ),
    )(ends, qkv, wide, lse, up)


def layer_stats(rows):
    centred = rows - jnp.mean(rows, axis=-1, keepdims=True)
    inverse = lax.rsqrt(jnp.mean(centred * centred, axis=-1, keepdims=True) + EPSILON)
    return centred * inverse, inverse


def layer_back(upstream, normed, inverse, gain):
    scaled = upstream * gain
    return inverse * (
        scaled
        - jnp.mean(scaled, axis=-1, keepdims=True)
        - normed * jnp.mean(scaled * normed, axis=-1, keepdims=True)
    )


def full(shape):
    return pl.BlockSpec(shape, lambda *_: (0,) * len(shape))


def vmem(mib):
    return pltpu.CompilerParams(vmem_limit_bytes=mib << 20)


def project_kernel(dims, at_ref, own_ref, peer_ref, gain_ref, shift_ref, bias_ref, a_ref, b_ref, msg_ref, w_ref, first_ref):
    X, Y, Z, T, chunks, wd = dims
    S, rows, part = Z * Y, a_ref.shape[-2], a_ref.shape[-1]
    width = w_ref.shape[1] // (3 * X)

    @pl.when((pl.program_id(0) == 0) & (pl.program_id(1) == 0))
    def _():
        x_me, c_me, z_me, y_me = (at_ref[n] for n in range(4))
        for ref, col, x_outer in ((a_ref, 0, False), (b_ref, part, True)):
            for k0 in range(ref.shape[0]):
                for k1 in range(ref.shape[1]):
                    kx, ky = (k0, k1) if x_outer else (k1, k0)
                    x, y = lax.rem(x_me - kx + X, X), lax.rem(y_me - ky + Y, Y)
                    for kz in range(Z):
                        z = lax.rem(z_me - kz + Z, Z)
                        for kc in range(2):
                            c = lax.rem(c_me + kc, 2)
                            row = (((x * 2 + c) * Z + z) * Y + y) * rows
                            row = pl.multiple_of(row, rows)
                            w_ref[pl.ds(row, rows), col : col + part] = ref[k0, k1, kz, kc]
        for r, ref in enumerate((own_ref, peer_ref)):
            normed, _ = layer_stats(ref[...].astype(F32))
            first_ref[r * T : (r + 1) * T, :] = (normed * gain_ref[...] + shift_ref[...]).astype(BF16)

    t, x = pl.program_id(0), pl.program_id(1)
    col = pl.multiple_of((t * X + x) * width, width)
    out = dot_nn(first_ref[...], w_ref[:, pl.ds(col, width)]) + bias_ref[:, pl.ds(col, width)]
    out = out.astype(BF16)
    per = width // wd
    for r in range(2):
        for k in range(per):
            msg_ref[r * chunks + x * per + k, t] = out[r * T : (r + 1) * T, k * wd : (k + 1) * wd]


def project(dims, at, own, peer, gain, shift, bias, a, b):
    X, Y, Z, T, chunks, wd = dims
    D = own.shape[1]
    cols = 2 * a.shape[-1]
    return pl.pallas_call(
        functools.partial(project_kernel, dims),
        name="project",
        grid=(3, X),
        in_specs=[pl.BlockSpec(memory_space=pltpu.SMEM)]
        + [full(v.shape) for v in (own, peer, gain, shift, bias, a, b)],
        out_specs=[full((2 * chunks, 3, T, wd)), full((D, cols)), full((2 * T, D))],
        out_shape=[
            jax.ShapeDtypeStruct((2 * chunks, 3, T, wd), BF16),
            jax.ShapeDtypeStruct((D, cols), BF16),
            jax.ShapeDtypeStruct((2 * T, D), BF16),
        ],
        compiler_params=vmem(60),
        cost_estimate=pl.CostEstimate(flops=4 * T * D * cols, bytes_accessed=8 << 20, transcendentals=0),
    )(at, own, peer, gain, shift, bias, a, b)


def origin(k, me, size):
    return lax.rem(me - k + size, size)


def at_rows(start, rows):
    return pl.ds(pl.multiple_of(start, rows), rows)


def expand_kernel(dims, at_ref, *refs):
    X, Y, Z, T, chunks, wd = dims
    own_ref, peer_ref, mine_ref, theirs_ref, out_b_ref, gain_ref, shift_ref, fc_b_ref = refs[:8]
    refs = refs[8:]
    own_w_refs, peer_w_refs, low_refs, refs = refs[:X], refs[X : 2 * X], refs[2 * X : 3 * X], refs[3 * X :]
    high_refs, (resid_ref, second_ref, pre_ref, w_own_ref, fc_ref, w_peer) = refs[:Y], refs[Y:]
    D = own_ref.shape[1]
    rows = own_w_refs[0].shape[2]
    f = pl.program_id(0)
    x_me, c_me, y_me = (at_ref[n] for n in (0, 1, 3))

    @pl.when(f == 0)
    def _():
        for kx in range(X):
            for ky in range(Y):
                for kz in range(Z):
                    x, y, z = origin(kx, x_me, X), origin(ky, y_me, Y), kz
                    spot = at_rows(((x * Z + z) * Y + y) * rows, rows)
                    w_own_ref[spot, :] = own_w_refs[kx][ky, kz]
                    w_peer[spot, :] = peer_w_refs[kx][ky, kz]
        per = chunks // X
        width = per * wd
        for r, x_ref in enumerate((own_ref, peer_ref)):
            resid = x_ref[...].astype(F32) + out_b_ref[...]
            for source, base, w in ((mine_ref, r, w_own_ref), (theirs_ref, 1 - r, w_peer)):
                for x in range(X):
                    parts = [source[base * chunks + x * per + k] for k in range(per)]
                    resid = resid + dot_nn(jnp.concatenate(parts, axis=1), w[x * width : (x + 1) * width, :])
            part = slice(r * T, (r + 1) * T)
            resid_ref[part, :] = resid
            normed, _ = layer_stats(resid)
            second_ref[part, :] = (normed * gain_ref[...] + shift_ref[...]).astype(BF16)

    def place(block, kx, ky, kz):
        x, y, z = origin(kx, x_me, X), origin(ky, y_me, Y), kz
        for kc in range(2):
            c = lax.rem(c_me + kc, 2)
            fc_ref[at_rows((((x * 2 + c) * Z + z) * Y + y) * rows, rows), :] = block[kc * rows : (kc + 1) * rows, :]

    steps = pl.num_programs(0)

    @pl.when(f * 2 < steps)
    def _():
        for kx in range(X):
            for ky in range(Y):
                for kz in range(Z):
                    place(low_refs[kx][ky, kz], kx, ky, kz)

    @pl.when(f * 2 >= steps)
    def _():
        for kx in range(X):
            for ky in range(Y):
                for kz in range(Z):
                    place(high_refs[ky][kx, kz], kx, ky, kz)

    pre_ref[...] = dot_nn(second_ref[...], fc_ref[...]) + fc_b_ref[...]


def expand(dims, at, inputs, fc_b, low, w_peer, high):
    X, Y, Z, T, chunks, wd = dims
    D = inputs[0].shape[1]
    half, ffh = D // 2, fc_b.shape[1]
    rows = half // (X * Y * Z)
    tile = ffh // (X * Z)
    per = X * Z // 2
    return pl.pallas_call(
        functools.partial(expand_kernel, dims),
        name="expand",
        grid_spec=pltpu.PrefetchScalarGridSpec(
            num_scalar_prefetch=1,
            grid=(X * Z,),
            in_specs=[full(v.shape) for v in inputs]
            + [pl.BlockSpec((1, tile), lambda f, at: (0, f))]
            + [pl.BlockSpec((Y, Z, rows, D), lambda f, at: (0, 0, 4, 0))] * X
            + [full((Y, Z, rows, D))] * X
            + [pl.BlockSpec((Y, Z, 2 * rows, tile), lambda f, at: (0, 0, 0, jnp.minimum(f, per - 1)))] * X
            + [pl.BlockSpec((X, Z, 2 * rows, tile), lambda f, at: (0, 0, 0, jnp.maximum(f - per, 0)))] * Y,
            out_specs=[
                full((2 * T, D)), full((2 * T, D)),
                pl.BlockSpec((2 * T, tile), lambda f, at: (0, f)),
                full((half, D)),
                pl.BlockSpec((D, tile), lambda f, at: (0, f)),
            ],
            scratch_shapes=[pltpu.VMEM((half, D), BF16)],
        ),
        out_shape=[
            jax.ShapeDtypeStruct((2 * T, D), F32),
            jax.ShapeDtypeStruct((2 * T, D), BF16),
            jax.ShapeDtypeStruct((2 * T, ffh), F32),
            jax.ShapeDtypeStruct((half, D), BF16),
            jax.ShapeDtypeStruct((D, ffh), BF16),
        ],
        compiler_params=vmem(60),
        cost_estimate=pl.CostEstimate(flops=4 * T * D * (D + ffh), bytes_accessed=20 << 20, transcendentals=0),
    )(at, *inputs, fc_b, *low, *w_peer, *low, *high)


def contract_kernel(dims, at_ref, *refs):
    X, Y, Z, T, chunks, wd = dims
    cot_own_ref, cot_peer_ref, second_ref, pre_ref, fc_ref = refs[:5]
    refs = refs[5:]
    low_refs, high_refs, refs = refs[:X], refs[X : X + Y], refs[X + Y :]
    own_ref, give_ref, back_ref, back_low_ref, dy_ref, fc_sum_ref = refs[:6]
    refs = refs[6:]
    a_refs, b_refs, (flipped, proj, tall, acc) = refs[:X], refs[X : X + Y], refs[X + Y :]
    D = cot_own_ref.shape[1]
    tile = pre_ref.shape[1]
    fr = tile // Y
    cut = fr // 2
    rows = a_refs[0].shape[2] // 4
    f = pl.program_id(0)
    x_me, y_me, place = at_ref[0], at_ref[3], at_ref[4]

    @pl.when(f == 0)
    def _():
        for r, cot_ref in enumerate((cot_own_ref, cot_peer_ref)):
            pos = place * T + lax.broadcasted_iota(jnp.int32, (T, D), 0)
            dy_ref[r * T : (r + 1) * T, :] = jnp.where(pos < at_ref[5 + r], cot_ref[...], BF16(0.0))
        flipped[...] = second_ref[...].T

    for ky in range(Y):
        y = origin(ky, y_me, Y) * fr
        for kx in range(X):

            @pl.when(origin(kx, x_me, X) == f // Z)
            def _():
                proj[at_rows(y, cut), :] = low_refs[kx][ky, 0]
                proj[at_rows(y + cut, cut), :] = high_refs[ky][kx, 0]

    pre = pre_ref[...]
    d_act = dot_nt(dy_ref[...], proj[...])
    k0, k1 = 0.7978845608028654, 0.044715
    square = pre * pre
    tanh = jnp.tanh(k0 * (pre + k1 * (square * pre)))
    left = 0.5 * (1.0 + tanh)
    act = (pre * left).astype(BF16)
    slope = left + 0.5 * pre * (1.0 - tanh * tanh) * (k0 * (1.0 + 3.0 * k1 * square))
    d_pre = (slope * d_act).astype(BF16)
    fc_sum_ref[...] = jnp.sum(d_pre.astype(F32), axis=0, keepdims=True)
    part = dot_nn(act, proj[...])
    back = dot_nt(d_pre, fc_ref[...])
    tall[...] = dot_tn(act, dy_ref[...]).astype(BF16)
    for k in range(Y):
        y = lax.rem(y_me + k, Y)
        b_refs[k][f // Z, lax.rem(f, Z)] = tall[at_rows(y * fr, fr), :]
    grad = dot_nn(flipped[...], d_pre).astype(BF16)
    block = D // (2 * X)
    n, lane = (f * tile) // D, pl.multiple_of(lax.rem(f * tile, D), tile)
    for x in range(X):
        for k in range(X):

            @pl.when(x == lax.rem(x_me + k, X))
            def _():
                for c in range(2):
                    value = grad[(x * 2 + c) * block : (x * 2 + c + 1) * block, :].reshape(Z, Y, rows, tile)
                    a_refs[k][:, :, at_rows((c * 2 + n) * rows, rows), pl.ds(lane, tile)] = value

    @pl.when(f == 0)
    def _():
        acc[...] = part
        back_ref[...] = back

    @pl.when(f > 0)
    def _():
        acc[...] += part
        back_ref[...] += back

    @pl.when(f == pl.num_programs(0) - 1)
    def _():
        own_ref[...] = acc[:T, :]
        give_ref[...] = acc[T:, :].astype(BF16)
        back_low_ref[:T, :] = back_ref[T:, :].astype(BF16)
        back_low_ref[T:, :] = back_ref[:T, :].astype(BF16)


def contract(dims, at, cot_own, cot_peer, second, pre, fc, low, high):
    X, Y, Z, T, chunks, wd = dims
    D, ffh = fc.shape
    tile = ffh // (X * Z)
    cut = tile // (2 * Y)
    rows = D // (2 * X * Y * Z)
    a_shape, b_shape = (Z, Y, 5 * rows, D), (X, Z, tile // Y, D)

    def block(f, at):
        return (0, f % Z, 1, 0)

    return pl.pallas_call(
        functools.partial(contract_kernel, dims),
        name="contract",
        grid_spec=pltpu.PrefetchScalarGridSpec(
            num_scalar_prefetch=1,
            grid=(X * Z,),
            in_specs=[full(v.shape) for v in (cot_own, cot_peer, second)]
            + [
                pl.BlockSpec((2 * T, tile), lambda f, at: (0, f)),
                pl.BlockSpec((D, tile), lambda f, at: (0, f)),
            ]
            + [pl.BlockSpec((Y, 1, cut, D), block)] * X
            + [pl.BlockSpec((X, 1, cut, D), block)] * Y,
            out_specs=[
                full((T, D)), full((T, D)), full((2 * T, D)), full((2 * T, D)), full((2 * T, D)),
                pl.BlockSpec((1, tile), lambda f, at: (0, f)),
            ]
            + [pl.BlockSpec((Z, Y, 4 * rows, D), lambda f, at: (0, 0, 0, 0))] * X
            + [full(b_shape)] * Y,
            scratch_shapes=[
                pltpu.VMEM((D, 2 * T), BF16),
                pltpu.VMEM((tile, D), BF16),
                pltpu.VMEM((tile, D), BF16),
                pltpu.VMEM((2 * T, D), F32),
            ],
        ),
        out_shape=[
            jax.ShapeDtypeStruct((T, D), F32),
            jax.ShapeDtypeStruct((T, D), BF16),
            jax.ShapeDtypeStruct((2 * T, D), F32),
            jax.ShapeDtypeStruct((2 * T, D), BF16),
            jax.ShapeDtypeStruct((2 * T, D), BF16),
            jax.ShapeDtypeStruct((1, ffh), F32),
        ]
        + [jax.ShapeDtypeStruct(a_shape, BF16)] * X
        + [jax.ShapeDtypeStruct(b_shape, BF16)] * Y,
        compiler_params=vmem(60),
        cost_estimate=pl.CostEstimate(
            flops=20 * T * D * ffh, bytes_accessed=30 << 20, transcendentals=2 * T * ffh
        ),
    )(at, cot_own, cot_peer, second, pre, fc, *low, *high)


def middle_kernel(dims, at_ref, back_ref, got_ref, resid_ref, dy_ref, gain_ref, w_ref, mine_ref, *refs):
    X, Y, Z, T, chunks, wd = dims
    low_ref, wide_ref, msg_ref, sums_ref = refs[X : X + 4]
    a_refs, all_low = refs[X + 4 : -1], refs[-1]
    b = pl.program_id(0)
    rows, D = back_ref.shape
    steps = T // rows
    normed, inverse = layer_stats(resid_ref[...])
    d_second = back_ref[...] + got_ref[...].astype(F32)
    dy = dy_ref[...].astype(F32)
    d_resid = dy + layer_back(d_second, normed, inverse, gain_ref[...])
    low = d_resid.astype(BF16)
    low_ref[...] = low
    wide_ref[...] = d_resid
    all_low[at_rows(b * rows, rows), :] = low
    per = chunks // X
    start = pl.multiple_of(lax.rem(b, steps) * rows, rows)
    for x in range(X):
        out = dot_nt(low, w_ref[x * per * wd : (x + 1) * per * wd, :]).astype(BF16)
        for k in range(per):
            msg_ref[(b // steps) * chunks + x * per + k, pl.ds(start, rows), :] = out[:, k * wd : (k + 1) * wd]

    @pl.when(b == 0)
    def _():
        sums_ref[...] = jnp.zeros_like(sums_ref)

    @pl.when(b < steps)
    def _():
        for n, value in enumerate((d_resid, d_second * normed, d_second, dy)):
            sums_ref[n : n + 1, :] += jnp.sum(value, axis=0, keepdims=True)

    @pl.when(b == pl.num_programs(0) - 1)
    def _():
        for k in range(X):
            x = lax.rem(at_ref[0] + k, X)
            left = [
                jnp.concatenate([mine_ref[r * chunks + x * per + j] for r in range(2)], axis=0) for j in range(per)
            ]
            value = dot_tn(jnp.concatenate(left, axis=1), all_low[...]).astype(BF16)
            a_refs[k][...] = value.reshape(a_refs[k].shape)


def middle(dims, at, back, got, resid, dy, gain, w_own, mine, part_a):
    X, Y, Z, T, chunks, wd = dims
    D = back.shape[1]
    block = min(128, T)
    row = pl.BlockSpec((block, D), lambda b: (b, 0))
    rows = D // (2 * X * Y * Z)
    last = part_a[0].shape[2] // rows - 1
    return pl.pallas_call(
        functools.partial(middle_kernel, dims),
        name="middle",
        grid=(2 * T // block,),
        in_specs=[pl.BlockSpec(memory_space=pltpu.SMEM), row, row, row, row]
        + [full(v.shape) for v in (gain, w_own, mine)]
        + [pl.BlockSpec(memory_space=pl.ANY)] * X,
        out_specs=[row, row, full((2 * chunks, T, wd)), full((8, D))]
        + [pl.BlockSpec((Z, Y, rows, D), lambda b: (0, 0, last, 0))] * X,
        out_shape=[
            jax.ShapeDtypeStruct((2 * T, D), BF16),
            jax.ShapeDtypeStruct((2 * T, D), F32),
            jax.ShapeDtypeStruct((2 * chunks, T, wd), BF16),
            jax.ShapeDtypeStruct((8, D), F32),
        ]
        + [jax.ShapeDtypeStruct(v.shape, v.dtype) for v in part_a],
        input_output_aliases={8 + k: 4 + k for k in range(X)},
        scratch_shapes=[pltpu.VMEM((2 * T, D), BF16)],
        compiler_params=vmem(60),
        cost_estimate=pl.CostEstimate(flops=4 * T * D * D, bytes_accessed=14 << 20, transcendentals=0),
    )(at, back, got, resid, dy, gain, w_own, mine, *part_a)


def project_back_kernel(dims, at_ref, d_ref, w_ref, first_ref, own_ref, give_ref, sum_ref, *refs):
    X, Y, Z, T, chunks, wd = dims
    a_refs, b_refs, (joint, block) = refs[:X], refs[X : X + Y], refs[X + Y :]
    g = pl.program_id(0)
    x, c = g // 2, pl.multiple_of(lax.rem(g, 2), 1)
    half = chunks * wd

    @pl.when(g == 0)
    def _():
        for r in range(2):
            for t in range(3):
                for h in range(chunks):
                    at = t * half + h * wd
                    joint[r * T : (r + 1) * T, at : at + wd] = d_ref[r * chunks + h, t]
        sum_ref[...] = jnp.sum(joint[...].astype(F32), axis=0, keepdims=True)

    part = dot_nt(joint[...], w_ref[...])
    own_ref[...] = part[:T, :]
    give_ref[...] = part[T:, :].astype(BF16)
    block[...] = dot_tn(first_ref[...], joint[...]).astype(BF16)
    cols = block.shape[1] // 2
    rows = block.shape[0] // (Z * Y)
    for k in range(X):

        @pl.when(x == lax.rem(at_ref[0] + k, X))
        def _():
            a_refs[k][:, :, pl.ds(c * rows, rows), :] = block[:, :cols].reshape(Z, Y, rows, cols)

    for k in range(Y):
        y = lax.rem(at_ref[3] + k, Y)
        for z in range(Z):
            start = pl.multiple_of((z * Y + y) * rows, rows)
            b_refs[k][x, z, pl.ds(c * rows, rows), :] = block[pl.ds(start, rows), cols:]


def project_back(dims, at, d_msg, w, first):
    X, Y, Z, T, chunks, wd = dims
    D, cols = w.shape
    block = D // (2 * X)
    rows = block // (Z * Y)
    a_shape, b_shape = (Z, Y, 2 * rows, cols // 2), (X, Z, 2 * rows, cols // 2)
    return pl.pallas_call(
        functools.partial(project_back_kernel, dims),
        name="project_back",
        grid=(2 * X,),
        in_specs=[
            pl.BlockSpec(memory_space=pltpu.SMEM),
            full(d_msg.shape),
            pl.BlockSpec((block, cols), lambda g: (g, 0)),
            pl.BlockSpec((2 * T, block), lambda g: (0, g)),
        ],
        out_specs=[
            pl.BlockSpec((T, block), lambda g: (0, g)),
            pl.BlockSpec((T, block), lambda g: (0, g)),
            full((1, cols)),
        ]
        + [full(a_shape)] * X
        + [full(b_shape)] * Y,
        out_shape=[
            jax.ShapeDtypeStruct((T, D), F32),
            jax.ShapeDtypeStruct((T, D), BF16),
            jax.ShapeDtypeStruct((1, cols), F32),
        ]
        + [jax.ShapeDtypeStruct(a_shape, BF16)] * X
        + [jax.ShapeDtypeStruct(b_shape, BF16)] * Y,
        scratch_shapes=[pltpu.VMEM((2 * T, cols), BF16), pltpu.VMEM((block, cols), BF16)],
        compiler_params=vmem(60),
        cost_estimate=pl.CostEstimate(flops=8 * T * D * cols, bytes_accessed=12 << 20, transcendentals=0),
    )(at, d_msg, w, first)


def combine_kernel(axis, counts, wide, at_ref, *refs):
    groups = []
    for count in counts:
        groups.append(refs[:count])
        refs = refs[count:]
    step = pl.program_id(0)
    for k, out_ref in enumerate(refs):

        @pl.when(step == k)
        def _():
            start = 0
            for group in groups:
                total = group[0][...].astype(F32)
                for ref in group[1:]:
                    total = total + ref[...].astype(F32)
                total = total.reshape(out_ref.shape[:-2] + total.shape[-2:]).astype(out_ref.dtype)
                out_ref[..., start : start + total.shape[-2], :] = total
                start += total.shape[-2]


def join_kernel(counts, *refs):
    start, out_ref = 0, refs[-1]
    for count in counts:
        total = refs[0][...].astype(F32)
        for ref in refs[1:count]:
            total = total + ref[...].astype(F32)
        out_ref[:, start : start + total.shape[1], :] = total.astype(BF16)
        start += total.shape[1]
        refs = refs[count:]


def join(groups):
    size, columns = groups[0][0].shape[0], groups[0][0].shape[2]
    rows = sum(g[0].shape[1] for g in groups)
    return pl.pallas_call(
        functools.partial(join_kernel, tuple(len(g) for g in groups)),
        name="join",
        grid=(size,),
        in_specs=[pl.BlockSpec((1,) + v.shape[1:], lambda n: (n, 0, 0)) for g in groups for v in g],
        out_specs=pl.BlockSpec((1, rows, columns), lambda n: (n, 0, 0)),
        out_shape=jax.ShapeDtypeStruct((size, rows, columns), BF16),
        compiler_params=vmem(60),
        cost_estimate=pl.CostEstimate(
            flops=0, bytes_accessed=sum(2 * v.size for g in groups for v in g), transcendentals=0
        ),
    )(*[v for g in groups for v in g])


def combine(at, axis, dim, groups, wide):
    shapes = [group[0].shape for group in groups]
    size = shapes[0][dim]
    rest = tuple(n for d, n in enumerate(shapes[0]) if d != dim)
    out = rest[:-2] + (sum(s[-2] for s in shapes), rest[-1])

    def spec(shape):
        return pl.BlockSpec(
            tuple(1 if d == dim else n for d, n in enumerate(shape)),
            lambda k, at: tuple(lax.rem(at[axis] + k, size) if d == dim else 0 for d in range(len(shape))),
        )

    kinds = [F32 if wide and k == 0 else BF16 for k in range(size)]
    return pl.pallas_call(
        functools.partial(combine_kernel, axis, tuple(len(g) for g in groups), wide),
        name="combine",
        grid_spec=pltpu.PrefetchScalarGridSpec(
            num_scalar_prefetch=1,
            grid=(size,),
            in_specs=[spec(v.shape) for g in groups for v in g],
            out_specs=[full(out)] * size,
        ),
        out_shape=[jax.ShapeDtypeStruct(out, kind) for kind in kinds],
        compiler_params=vmem(60),
        cost_estimate=pl.CostEstimate(
            flops=0, bytes_accessed=sum(2 * v.size for g in groups for v in g), transcendentals=0
        ),
    )(at, *[v for g in groups for v in g])


def pick(array, index, dim):
    return lax.dynamic_index_in_dim(array, index, dim, keepdims=False)


def swap(array):
    return lax.ppermute(array, "c", SWAP)


def shift(array, axis, size, k):
    return lax.ppermute(array, axis, [(i, (i + k) % size) for i in range(size)])


def spread(array, axis, size):
    return jnp.stack([array] + [shift(array, axis, size, k) for k in range(1, size)])


def sent(parts, axis):
    return [parts[0]] + [shift(parts[k], axis, len(parts), k) for k in range(1, len(parts))]


def scatter_sum(array, axis, dim):
    size, me = array.shape[dim], lax.axis_index(axis)
    return sum(sent([pick(array, (me + k) % size, dim) for k in range(size)], axis))


def per_device(sizes, *args):
    (
        hidden, group_sizes, prefix_lens, sol_lens, ln1_gain, ln1_shift, qkv_weight, qv_bias, out_weight, out_bias,
        ln2_gain, ln2_shift, fc_weight, fc_bias, proj_weight, proj_bias, cotangent,
    ) = args
    X, Z, Y = sizes
    S, ND = Z * Y, 2 * X * Z * Y
    _, T, D = hidden.shape
    FF = fc_weight.shape[1]
    heads = D // HD // S
    wd, chunks = heads * HD, S // 2
    half, ffh = D // 2, FF // 2
    rows = D // ND
    dims = (X, Y, Z, T, chunks, wd)
    c, place = lax.axis_index("c"), lax.axis_index(SEQ)

    local = qkv_weight.reshape(rows, 3, X, 2, half // X)
    kept = pick(local, c, 3).reshape(rows, 3 * half)
    given = pick(local, 1 - c, 3).reshape(rows, 3 * half)
    piece = jnp.stack([kept, swap(given)])
    cut = 3 * half // 2
    piece_a, piece_b = spread(piece[..., :cut], "z", Z), spread(piece[..., cut:], "z", Z)

    local = fc_weight.reshape(rows, X, 2, ffh // X)
    kept, given = (pick(local, n, 2).reshape(rows, ffh) for n in (c, 1 - c))
    wide = [slice(n, n + D) for n in range(0, ffh, D)]
    got = swap(jnp.concatenate([given[:, n] for n in wide], axis=0))
    fr = FF // ND
    later = jnp.concatenate(
        [kept[:, wide[0]], got[:rows], proj_weight[: fr // 2], out_weight]
        + [kept[:, wide[1]], got[rows:], proj_weight[fr // 2 :]],
        axis=0,
    )
    later = lax.all_gather(later, "z", axis=0, tiled=False)
    low, high = later[:, : fr + rows], later[:, fr + rows :]
    piece_a = spread(spread(piece_a, "x", X), "y", Y)
    piece_b = spread(spread(piece_b, "y", Y), "x", X)

    small = (ln1_gain, ln1_shift, qv_bias, out_bias, ln2_gain, ln2_shift, fc_bias, proj_bias)
    cuts = [0]
    for part in small:
        cuts.append(cuts[-1] + part.shape[0])
    packed = jnp.broadcast_to(jnp.concatenate(small)[None, :], (ND, cuts[-1]))
    packed = lax.all_to_all(packed, ALL, split_axis=0, concat_axis=0, tiled=True).astype(F32)
    gain1, shift1, qv_all, out_b, gain2, shift2, fc_b, proj_b = (
        packed[:, cuts[n] : cuts[n + 1]].reshape(1, -1) for n in range(8)
    )

    slot = jnp.arange(sol_lens.shape[1], dtype=jnp.int32)
    used = jnp.where(slot < group_sizes[0], sol_lens[0], 0)
    ends = prefix_lens[0] + jnp.sum(jnp.where(slot[None, :] <= slot[:, None], used[None, :], 0), axis=1)
    meta = jnp.concatenate([prefix_lens, ends, jnp.zeros((15,), jnp.int32)])
    meta_peer = swap(meta)
    meta_here = jnp.where(place < chunks, meta, meta_peer)
    where = [lax.axis_index("x"), c, lax.axis_index("z"), lax.axis_index("y"), place, meta[16], meta_peer[16]]
    at = jnp.stack(where).astype(jnp.int32)

    own, cot = hidden[0], cotangent[0]
    peer, cot_peer = swap(own), swap(cot)

    qv_here = pick(qv_all.reshape(2, X, 2, half // X), c, 2).reshape(2, half)
    bias = jnp.concatenate([qv_here[:1], jnp.zeros_like(qv_here[:1]), qv_here[1:]], axis=1)
    msg, w_qkv, first = project(dims, at, own, peer, gain1, shift1, bias, piece_a, piece_b)

    def exchange(array):
        return lax.all_to_all(array, SEQ, split_axis=0, concat_axis=0, tiled=True)

    msg, low, high = lax.optimization_barrier((msg, low, high))
    qkv = exchange(msg)
    low, high = spread(low, "y", Y), spread(high, "x", X)
    low = [low] + [shift(low, "x", X, k) for k in range(1, X)]
    high = [high] + [shift(high, "y", Y, k) for k in range(1, Y)]
    att, att_wide, lse = attend(qkv, meta_here, heads)
    w_peer = [swap(v[:, :, fr :]) for v in low]
    mine = exchange(att)
    theirs = swap(mine)

    fc_b_here = pick(fc_b.reshape(X, 2, ffh // X), c, 1).reshape(1, ffh)
    resid, second, pre, w_own, w_fc = expand(
        dims, at, [own, peer, mine, theirs, out_b, gain2, shift2], fc_b_here, low, w_peer, high
    )
    out = contract(dims, at, cot, cot_peer, second, pre, w_fc, low, high)
    ahead, give, back, back_low, dy, fc_sum = out[:6]
    d_low, d_wide, d_msg, sums_mid, *part_a = middle(
        dims, at, back, swap(back_low), resid, dy, gain2, w_own, mine, out[6 : 6 + X]
    )
    part_a, part_b = sent(part_a, "x"), sent(out[6 + X :], "y")
    up = exchange(d_msg)
    position = place * T + jnp.arange(T, dtype=jnp.int32)
    valid = (position < meta[16]).astype(F32)[:, None]
    layer_out = valid * (resid[:T] + (ahead + swap(give).astype(F32)) + proj_b)

    d_msg = attend_back(qkv, att_wide, lse, up, meta_here, heads)
    part_a, part_b = combine(at, 3, 1, [part_a], False), combine(at, 0, 0, [part_b], False)
    part_a, part_b = sent(part_a, "y"), sent(part_b, "x")
    d_qkv = exchange(d_msg)
    d_qkv, part_a, part_b = lax.optimization_barrier((d_qkv, part_a, part_b))
    total = lax.psum_scatter(join([part_a, part_b]), "z", scatter_dimension=0, tiled=True)[0].astype(F32)
    def both_halves(grad, blocks):
        kept = pick(grad, c, 0)
        got = swap(pick(grad, 1 - c, 0).astype(BF16)).astype(F32)
        shape = (kept.shape[0],) + blocks
        kept, got = kept.reshape(shape), got.reshape(shape)
        low = jnp.where(c == 0, kept, got)
        high = jnp.where(c == 0, got, kept)
        return jnp.stack([low, high], axis=-2).reshape(kept.shape[0], -1)

    out = project_back(dims, at, d_qkv, w_qkv, first)
    part, part_peer, qkv_sum = out[:3]
    part_a, part_b = sent(out[3 : 3 + X], "x"), sent(out[3 + X :], "y")
    d_first = part + swap(part_peer).astype(F32)
    norm, inverse = layer_stats(own.astype(F32))
    hidden_grad = d_wide[:T] + layer_back(d_first, norm, inverse, gain1)
    def small_grads():
        def own_columns(vector, lead):
            cut = vector.reshape(lead, X, 1, -1)
            spot = lax.broadcasted_iota(jnp.int32, (lead, X, 2, cut.shape[-1]), 2)
            return jnp.where(spot == c, cut, 0.0).reshape(-1)

        qv_sum = jnp.concatenate([qkv_sum[0, :half], qkv_sum[0, 2 * half :]])
        sums = (
            jnp.sum(d_first * norm, axis=0),
            jnp.sum(d_first, axis=0),
            own_columns(qv_sum, 2),
            sums_mid[0],
            sums_mid[1],
            sums_mid[2],
            own_columns(fc_sum, 1),
            sums_mid[3],
        )
        return jnp.concatenate([v.reshape(ND, -1) for v in sums], axis=1)

    part_a, part_b = combine(at, 3, 1, [part_a], False), combine(at, 0, 0, [part_b], False)
    part_a, part_b = sent(part_a, "y"), sent(part_b, "x")
    fc_rows = 2 * ffh // D * rows
    fc_grad = total[:fc_rows].reshape(2, ffh // D, rows, D).transpose(0, 2, 1, 3).reshape(2, rows, ffh)
    out_grad, proj_grad = total[fc_rows : fc_rows + rows], total[fc_rows + rows :]
    fc_grad = both_halves(fc_grad, (X, ffh // X))
    last = sent(combine(at, 2, 0, [part_a, part_b], True), "z")
    qkv_grad = sum(v.astype(F32) for v in last)
    qkv_grad = qkv_grad.reshape(2, 2, rows, cut).transpose(1, 2, 0, 3).reshape(2, rows, 2 * cut)
    qkv_grad = both_halves(qkv_grad, (3, X, half // X))

    packed = small_grads().reshape(X, 2, Z, Y, -1)
    for axis, dim in (("x", 0), ("y", 2), ("c", 0), ("z", 0)):
        packed = scatter_sum(packed, axis, dim)
    gain1_g, shift1_g, qv_g, out_b_g, gain2_g, shift2_g, fc_b_g, proj_b_g = (
        packed[cuts[n] : cuts[n + 1]] for n in range(8)
    )
    return (
        layer_out.astype(BF16)[None], hidden_grad.astype(BF16)[None], gain1_g, shift1_g, qkv_grad, qv_g, out_grad,
        out_b_g, gain2_g, shift2_g, fc_grad, fc_b_g, proj_grad, proj_b_g,
    )


def solution(mesh):
    Z = 4
    X, Y = mesh.shape["dp"] // 2, mesh.shape["seq"] // Z
    split = Mesh(mesh.devices.reshape(X, 2, Z, Y), ALL)
    group, wide, flat = P(("x", "c"), SEQ, None), P(ALL, None), P(ALL)
    dp = P(("x", "c"))
    return jax.shard_map(
        functools.partial(per_device, (X, Z, Y)),
        mesh=split,
        in_specs=(
            group, dp, dp, P(("x", "c"), None), flat, flat, wide, flat, wide, flat, flat, flat, wide, flat, wide, flat,
            group,
        ),
        out_specs=(
            group, group, flat, flat, wide, flat, wide, flat, flat, flat, wide, flat, wide, flat,
        ),
        check_vma=False,
    )
```

```python
import functools

import jax
import jax.numpy as jnp
from jax import lax
from jax.experimental import pallas as pl
from jax.experimental.pallas import tpu as pltpu
from jax.sharding import Mesh
from jax.sharding import PartitionSpec as P

HD = 64
EPSILON = 1e-05
BIG = 1e30
BLOCK = 256
F32 = jnp.float32
LONG = pl.CostEstimate(flops=10**11, bytes_accessed=1, transcendentals=0)
TINY = pl.CostEstimate(flops=1, bytes_accessed=1, transcendentals=0)
BF16 = jnp.bfloat16
ALL = ("x", "c", "z", "y")
SEQ = ("z", "y")
SWAP = [(0, 1), (1, 0)]


def dot_nt(a, b):
    return lax.dot_general(a, b, (((1,), (1,)), ((), ())), preferred_element_type=F32)


def dot_nn(a, b):
    return lax.dot_general(a, b, (((1,), (0,)), ((), ())), preferred_element_type=F32)


def dot_tn(a, b):
    return lax.dot_general(a, b, (((0,), (0,)), ((), ())), preferred_element_type=F32)


def segment_code(ends_ref, start, rows, lanes):
    pos = start + lax.broadcasted_iota(jnp.int32, (rows, lanes), 0)
    passed = jnp.ones((rows, lanes), jnp.int32)
    for t in range(16):
        passed = passed + jnp.where(pos >= ends_ref[1 + t], 1, 0)
    code = jnp.where(pos < ends_ref[16], passed, 17)
    return jnp.where(pos < ends_ref[0], 0, code)


def with_segments(keys, ends_ref, start):
    rows, lanes = keys.shape
    code = segment_code(ends_ref, start, rows, lanes)
    lane = lax.broadcasted_iota(jnp.int32, (rows, lanes), 1)
    key_mark = jnp.where((code == lane) & (code > 0), 1.0, 0.0).astype(BF16)
    query_mark = jnp.where(code == lane, 0.0, -BIG).astype(BF16)
    return jnp.concatenate([keys, key_mark], axis=1), query_mark


def head_part(array, head, heads):
    if heads == 1:
        return array
    lane = lax.broadcasted_iota(jnp.int32, array.shape, 1)
    return jnp.where((lane >= head * HD) & (lane < (head + 1) * HD), array, jnp.zeros_like(array))


def merge_heads(parts):
    out = parts[0]
    if len(parts) > 1:
        lane = lax.broadcasted_iota(jnp.int32, out.shape, 1)
        for head in range(1, len(parts)):
            out = jnp.where(lane >= head * HD, parts[head], out)
    return out


def causal(rows, cols, transposed):
    row = lax.broadcasted_iota(jnp.int32, (rows, cols), 0)
    col = lax.broadcasted_iota(jnp.int32, (rows, cols), 1)
    return (row <= col) if transposed else (col <= row)


def attend_kernel(heads, ends_ref, qkv_ref, out_ref, wide_ref, lse_ref, keys, values, scores):
    i = pl.program_id(0)
    width = heads * HD
    start = pl.multiple_of(i * BLOCK, BLOCK)
    query_in, keys_in, values_in = (qkv_ref[:, t].reshape(BLOCK, width) for t in range(3))
    tagged, query_mark = with_segments(keys_in, ends_ref, start)
    keys[pl.ds(start, BLOCK), :] = tagged
    values[pl.ds(start, BLOCK), :] = values_in
    scaled = query_in * BF16(HD**-0.5)
    query = [
        jnp.concatenate([head_part(scaled, h, heads), query_mark], axis=1) for h in range(heads)
    ]

    def fold(array, op):
        out = array[:, :128]
        for at in range(128, BLOCK, 128):
            out = op(out, array[:, at : at + 128])
        return out

    def first(j, tops):
        block = keys[pl.ds(pl.multiple_of(j * BLOCK, BLOCK), BLOCK), :]
        new = []
        for h in range(heads):
            score = dot_nt(query[h], block)
            scores[h, j] = score
            new.append(jnp.maximum(tops[h], fold(score, jnp.maximum)))
        return tuple(new)

    tops = []
    for h in range(heads):
        score = jnp.where(causal(BLOCK, BLOCK, False), dot_nt(query[h], tagged), -BIG)
        scores[h, i] = score
        tops.append(fold(score, jnp.maximum))
    tops = lax.fori_loop(0, i, first, tuple(tops))
    tops = [jnp.max(t, axis=1, keepdims=True) for t in tops]

    def second(j, carry):
        sums, accs = carry
        block = values[pl.ds(pl.multiple_of(j * BLOCK, BLOCK), BLOCK), :]
        new_sums, new_accs = [], []
        for h in range(heads):
            expo = jnp.exp(scores[h, j] - tops[h])
            new_sums.append(sums[h] + fold(expo, jnp.add))
            new_accs.append(accs[h] + dot_nn(expo.astype(BF16), block))
        return tuple(new_sums), tuple(new_accs)

    zero = tuple(jnp.zeros((BLOCK, 128), F32) for _ in range(heads))
    zero_acc = tuple(jnp.zeros((BLOCK, width), F32) for _ in range(heads))
    sums, accs = lax.fori_loop(0, i + 1, second, (zero, zero_acc))
    sums = [jnp.sum(t, axis=1, keepdims=True) for t in sums]
    wide = merge_heads([accs[h] / sums[h] for h in range(heads)])
    wide_ref[...] = wide
    out_ref[...] = wide.astype(BF16).reshape(out_ref.shape)
    for h in range(heads):
        lse = jnp.broadcast_to(tops[h] + jnp.log(sums[h]), (BLOCK, 128))
        lse_ref[h : h + 1, :] = lse.T[0:1, :]


def attend(qkv, ends, heads):
    length, width = qkv.shape[0] * qkv.shape[2], heads * HD
    T = qkv.shape[2]
    per = BLOCK // T
    return pl.pallas_call(
        functools.partial(attend_kernel, heads),
        name="attend",
        grid=(length // BLOCK,),
        in_specs=[
            pl.BlockSpec(memory_space=pltpu.SMEM),
            pl.BlockSpec((per, 3, T, width), lambda i: (i, 0, 0, 0)),
        ],
        out_specs=[
            pl.BlockSpec((per, T, width), lambda i: (i, 0, 0)),
            pl.BlockSpec((BLOCK, width), lambda i: (i, 0)),
            pl.BlockSpec((8, BLOCK), lambda i: (0, i)),
        ],
        out_shape=[
            jax.ShapeDtypeStruct((length // T, T, width), BF16),
            jax.ShapeDtypeStruct((length, width), F32),
            jax.ShapeDtypeStruct((8, length), F32),
        ],
        scratch_shapes=[
            pltpu.VMEM((length, 2 * width), BF16),
            pltpu.VMEM((length, width), BF16),
            pltpu.VMEM((heads, length // BLOCK, BLOCK, BLOCK), F32),
        ],
        compiler_params=pltpu.CompilerParams(vmem_limit_bytes=32 << 20),
        cost_estimate=TINY,
    )(ends, qkv)


def attend_back_kernel(
    heads, ends_ref, qkv_ref, wide_ref, lse_ref, up_ref, out_ref, keys, values, key_acc, value_acc, query_acc
):
    i = pl.program_id(0)
    width = heads * HD
    start = pl.multiple_of(i * BLOCK, BLOCK)
    query_in, keys_in, values_in = (qkv_ref[:, t].reshape(BLOCK, width) for t in range(3))
    tagged, query_mark = with_segments(keys_in, ends_ref, start)
    keys[pl.ds(start, BLOCK), :] = tagged
    values[pl.ds(start, BLOCK), :] = values_in
    key_acc[pl.ds(start, BLOCK), :] = jnp.zeros((BLOCK, width), F32)
    value_acc[pl.ds(start, BLOCK), :] = jnp.zeros((BLOCK, width), F32)
    scaled = query_in * BF16(HD**-0.5)
    up = up_ref[...].reshape(BLOCK, width)
    part = [head_part(scaled, h, heads) for h in range(heads)]
    up_part = [head_part(up, h, heads) for h in range(heads)]
    query = [jnp.concatenate([part[h], query_mark], axis=1) for h in range(heads)]
    inner = (up.astype(F32) * wide_ref[...]).T
    inner = [jnp.sum(inner[h * HD : (h + 1) * HD, :], axis=0, keepdims=True) for h in range(heads)]
    lse = [lse_ref[h : h + 1, :] for h in range(heads)]
    part_all = jnp.concatenate(part, axis=0)
    up_all = jnp.concatenate(up_part, axis=0)
    for h in range(heads):
        query_acc[h] = jnp.zeros((BLOCK, width), F32)

    def step(j, diagonal):
        rows = pl.ds(pl.multiple_of(j * BLOCK, BLOCK), BLOCK)
        block, value = keys[rows, :], values[rows, :]
        probs, scores = [], []
        for h in range(heads):
            score = dot_nt(block, query[h])
            if diagonal:
                score = jnp.where(causal(BLOCK, BLOCK, True), score, -BIG)
            prob = jnp.exp(score - lse[h])
            d_prob = dot_nt(value, up_part[h])
            d_score = (prob * (d_prob - inner[h])).astype(BF16)
            probs.append(prob.astype(BF16))
            scores.append(d_score)
            query_acc[h] += dot_tn(d_score, block[:, :width])
        value_acc[rows, :] += dot_nn(jnp.concatenate(probs, axis=1), up_all)
        key_acc[rows, :] += dot_nn(jnp.concatenate(scores, axis=1), part_all)

    step(i, True)

    def body(j, carry):
        step(j, False)
        return carry

    lax.fori_loop(0, i, body, 0)
    d_query = merge_heads([query_acc[h] for h in range(heads)]) * HD**-0.5
    T = out_ref.shape[2]
    per = BLOCK // T
    out_ref[pl.ds(i * per, per), 0] = d_query.astype(BF16).reshape(per, T, width)

    @pl.when(i == pl.num_programs(0) - 1)
    def _():
        for s in range(out_ref.shape[0]):
            out_ref[s, 1] = key_acc[s * T : (s + 1) * T, :].astype(BF16)
            out_ref[s, 2] = value_acc[s * T : (s + 1) * T, :].astype(BF16)


def attend_back(qkv, wide, lse, up, ends, heads):
    length, width = qkv.shape[0] * qkv.shape[2], heads * HD
    T = qkv.shape[2]
    per = BLOCK // T
    return pl.pallas_call(
        functools.partial(attend_back_kernel, heads),
        name="attend_back",
        grid=(length // BLOCK,),
        in_specs=[
            pl.BlockSpec(memory_space=pltpu.SMEM),
            pl.BlockSpec((per, 3, T, width), lambda i: (i, 0, 0, 0)),
            pl.BlockSpec((BLOCK, width), lambda i: (i, 0)),
            pl.BlockSpec((8, BLOCK), lambda i: (0, i)),
            pl.BlockSpec((per, T, width), lambda i: (i, 0, 0)),
        ],
        out_specs=pl.BlockSpec((length // T, 3, T, width), lambda i: (0, 0, 0, 0)),
        out_shape=jax.ShapeDtypeStruct((length // T, 3, T, width), BF16),
        scratch_shapes=[
            pltpu.VMEM((length, 2 * width), BF16),
            pltpu.VMEM((length, width), BF16),
            pltpu.VMEM((length, width), F32),
            pltpu.VMEM((length, width), F32),
            pltpu.VMEM((heads, BLOCK, width), F32),
        ],
        compiler_params=pltpu.CompilerParams(vmem_limit_bytes=32 << 20),
        cost_estimate=TINY,
    )(ends, qkv, wide, lse, up)


def layer_stats(rows):
    centred = rows - jnp.mean(rows, axis=-1, keepdims=True)
    inverse = lax.rsqrt(jnp.mean(centred * centred, axis=-1, keepdims=True) + EPSILON)
    return centred * inverse, inverse


def layer_back(upstream, normed, inverse, gain):
    scaled = upstream * gain
    return inverse * (
        scaled
        - jnp.mean(scaled, axis=-1, keepdims=True)
        - normed * jnp.mean(scaled * normed, axis=-1, keepdims=True)
    )


def full(shape):
    return pl.BlockSpec(shape, lambda *_: (0,) * len(shape))


def vmem(mib):
    return pltpu.CompilerParams(vmem_limit_bytes=mib << 20)


def origin(k, me, size):
    return lax.rem(me - k + size, size)


def at_rows(start, rows):
    return pl.ds(pl.multiple_of(start, rows), rows)


def project_kernel(dims, at_ref, own_ref, peer_ref, gain_ref, shift_ref, bias_ref, *refs):
    X, Y, Z, T, chunks, wd = dims
    a_refs, b_refs, refs = refs[: X * Y], refs[X * Y : 2 * X * Y], refs[2 * X * Y :]
    msg_ref, w_ref, first_ref, norm_ref = refs
    rows, part = a_refs[0].shape[-2:]
    width = w_ref.shape[1] // (3 * X)

    @pl.when((pl.program_id(0) == 0) & (pl.program_id(1) == 0))
    def _():
        x_me, c_me, z_me, y_me = (at_ref[n] for n in range(4))
        for kx in range(X):
            for ky in range(Y):
                x, y = origin(kx, x_me, X), origin(ky, y_me, Y)
                for kz in range(Z):
                    z = origin(kz, z_me, Z)
                    for kc in range(2):
                        c = lax.rem(c_me + kc, 2)
                        spot = at_rows((((x * 2 + c) * Z + z) * Y + y) * rows, rows)
                        w_ref[spot, :part] = a_refs[ky * X + kx][kz, kc]
                        w_ref[spot, part:] = b_refs[kx * Y + ky][kz, kc]
        for r, ref in enumerate((own_ref, peer_ref)):
            normed, _ = layer_stats(ref[...].astype(F32))
            norm_ref[r * T : (r + 1) * T, :] = normed
            first_ref[r * T : (r + 1) * T, :] = (normed * gain_ref[...] + shift_ref[...]).astype(BF16)

    t, x = pl.program_id(0), pl.program_id(1)
    col = pl.multiple_of((t * X + x) * width, width)
    out = dot_nn(first_ref[...], w_ref[:, pl.ds(col, width)]) + bias_ref[:, pl.ds(col, width)]
    out = out.astype(BF16)
    per = width // wd
    for r in range(2):
        for k in range(per):
            msg_ref[r * chunks + x * per + k, t] = out[r * T : (r + 1) * T, k * wd : (k + 1) * wd]


def project(dims, at, own, peer, gain, shift, bias, pieces):
    X, Y, Z, T, chunks, wd = dims
    D = own.shape[1]
    cols = 2 * pieces[0].shape[-1]
    return pl.pallas_call(
        functools.partial(project_kernel, dims),
        name="project",
        grid=(3, X),
        in_specs=[pl.BlockSpec(memory_space=pltpu.SMEM)]
        + [full(v.shape) for v in (own, peer, gain, shift, bias, *pieces)],
        out_specs=[full((2 * chunks, 3, T, wd)), full((D, cols)), full((2 * T, D)), full((2 * T, D))],
        out_shape=[
            jax.ShapeDtypeStruct((2 * chunks, 3, T, wd), BF16),
            jax.ShapeDtypeStruct((D, cols), BF16),
            jax.ShapeDtypeStruct((2 * T, D), BF16),
            jax.ShapeDtypeStruct((2 * T, D), F32),
        ],
        compiler_params=vmem(60),
        cost_estimate=TINY,
    )(at, own, peer, gain, shift, bias, *pieces)


def expand_kernel(dims, at_ref, *refs):
    X, Y, Z, T, chunks, wd = dims
    own_ref, peer_ref, mine_ref, theirs_ref, out_b_ref, gain_ref, shift_ref, fc_b_ref = refs[:8]
    refs = refs[8:]
    n = X * Y
    own_w_refs, low_refs, high_refs, refs = refs[:n], refs[n : 2 * n], refs[2 * n : 3 * n], refs[3 * n :]
    peer_w_ref, resid_ref, second_ref, pre_ref, w_own_ref, fc_ref, w_peer = refs
    D = own_ref.shape[1]
    rows = own_w_refs[0].shape[1]
    f = pl.program_id(0)
    x_me, c_me, y_me = (at_ref[n] for n in (0, 1, 3))

    @pl.when(f == 0)
    def _():
        for kx in range(X):
            for ky in range(Y):
                for kz in range(Z):
                    x, y, z = origin(kx, x_me, X), origin(ky, y_me, Y), kz
                    spot = at_rows(((x * Z + z) * Y + y) * rows, rows)
                    w_own_ref[spot, :] = own_w_refs[kx * Y + ky][kz]
                    w_peer[spot, :] = peer_w_ref[kx * Y + ky, kz]
        per = chunks // X
        width = per * wd
        for r, x_ref in enumerate((own_ref, peer_ref)):
            resid = x_ref[...].astype(F32) + out_b_ref[...]
            for source, base, w in ((mine_ref, r, w_own_ref), (theirs_ref, 1 - r, w_peer)):
                for x in range(X):
                    parts = [source[base * chunks + x * per + k] for k in range(per)]
                    resid = resid + dot_nn(jnp.concatenate(parts, axis=1), w[x * width : (x + 1) * width, :])
            part = slice(r * T, (r + 1) * T)
            resid_ref[part, :] = resid
            normed, _ = layer_stats(resid)
            second_ref[part, :] = (normed * gain_ref[...] + shift_ref[...]).astype(BF16)

    def place(block, kx, ky, kz):
        x, y, z = origin(kx, x_me, X), origin(ky, y_me, Y), kz
        for kc in range(2):
            c = lax.rem(c_me + kc, 2)
            fc_ref[at_rows((((x * 2 + c) * Z + z) * Y + y) * rows, rows), :] = block[kc * rows : (kc + 1) * rows, :]

    steps = pl.num_programs(0)

    @pl.when(f * 2 < steps)
    def _():
        for kx in range(X):
            for ky in range(Y):
                for kz in range(Z):
                    place(low_refs[kx * Y + ky][kz], kx, ky, kz)

    @pl.when(f * 2 >= steps)
    def _():
        for kx in range(X):
            for ky in range(Y):
                for kz in range(Z):
                    place(high_refs[ky * X + kx][kz], kx, ky, kz)

    pre_ref[...] = dot_nn(second_ref[...], fc_ref[...]) + fc_b_ref[...]


def expand(dims, at, inputs, fc_b, low, w_peer, high):
    X, Y, Z, T, chunks, wd = dims
    D = inputs[0].shape[1]
    half, ffh = D // 2, fc_b.shape[1]
    rows = half // (X * Y * Z)
    tile = ffh // (X * Z)
    per = X * Z // 2
    return pl.pallas_call(
        functools.partial(expand_kernel, dims),
        name="expand",
        grid_spec=pltpu.PrefetchScalarGridSpec(
            num_scalar_prefetch=1,
            grid=(X * Z,),
            in_specs=[full(v.shape) for v in inputs]
            + [pl.BlockSpec((1, tile), lambda f, at: (0, f))]
            + [pl.BlockSpec((Z, rows, D), lambda f, at: (0, 4, 0))] * (X * Y)
            + [pl.BlockSpec((Z, 2 * rows, tile), lambda f, at: (0, 0, jnp.minimum(f, per - 1)))] * (X * Y)
            + [pl.BlockSpec((Z, 2 * rows, tile), lambda f, at: (0, 0, jnp.maximum(f - per, 0)))] * (X * Y)
            + [full(w_peer.shape)],
            out_specs=[
                full((2 * T, D)), full((2 * T, D)),
                pl.BlockSpec((2 * T, tile), lambda f, at: (0, f)),
                full((half, D)),
                pl.BlockSpec((D, tile), lambda f, at: (0, f)),
            ],
            scratch_shapes=[pltpu.VMEM((half, D), BF16)],
        ),
        out_shape=[
            jax.ShapeDtypeStruct((2 * T, D), F32),
            jax.ShapeDtypeStruct((2 * T, D), BF16),
            jax.ShapeDtypeStruct((2 * T, ffh), F32),
            jax.ShapeDtypeStruct((half, D), BF16),
            jax.ShapeDtypeStruct((D, ffh), BF16),
        ],
        compiler_params=vmem(60),
        cost_estimate=TINY,
    )(at, *inputs, fc_b, *low, *low, *high, w_peer)


def contract_kernel(dims, at_ref, *refs):
    X, Y, Z, T, chunks, wd = dims
    cot_own_ref, cot_peer_ref, second_ref, pre_ref, fc_ref = refs[:5]
    refs = refs[5:]
    low_refs, high_refs, refs = refs[: X * Y], refs[X * Y : 2 * X * Y], refs[2 * X * Y :]
    own_ref, give_ref, back_ref, back_low_ref, dy_ref, fc_sum_ref = refs[:6]
    refs = refs[6:]
    grad_ref, flipped, proj, grad, acc = refs
    D = cot_own_ref.shape[1]
    tile = pre_ref.shape[1]
    fr = tile // Y
    cut = fr // 2
    rows = grad_ref.shape[3] // 8
    f = pl.program_id(0)
    x_me, y_me, place = at_ref[0], at_ref[3], at_ref[4]

    @pl.when(f == 0)
    def _():
        for r, cot_ref in enumerate((cot_own_ref, cot_peer_ref)):
            pos = place * T + lax.broadcasted_iota(jnp.int32, (T, D), 0)
            dy_ref[r * T : (r + 1) * T, :] = jnp.where(pos < at_ref[5 + r], cot_ref[...], BF16(0.0))
        flipped[...] = second_ref[...].T

    for ky in range(Y):
        y = origin(ky, y_me, Y) * fr
        for kx in range(X):

            @pl.when(origin(kx, x_me, X) == f // Z)
            def _():
                proj[at_rows(y, cut), :] = low_refs[kx * Y + ky][0]
                proj[at_rows(y + cut, cut), :] = high_refs[ky * X + kx][0]

    pre = pre_ref[...]
    d_act = dot_nt(dy_ref[...], proj[...])
    k0, k1 = 0.7978845608028654, 0.044715
    square = pre * pre
    tanh = jnp.tanh(k0 * (pre + k1 * (square * pre)))
    left = 0.5 * (1.0 + tanh)
    act = (pre * left).astype(BF16)
    slope = left + 0.5 * pre * (1.0 - tanh * tanh) * (k0 * (1.0 + 3.0 * k1 * square))
    d_pre = (slope * d_act).astype(BF16)
    fc_sum_ref[...] = jnp.sum(d_pre.astype(F32), axis=0, keepdims=True)
    part = dot_nn(act, proj[...])
    back = dot_nt(d_pre, fc_ref[...])
    tall = dot_tn(act, dy_ref[...]).astype(BF16)
    for y in range(Y):
        grad_ref[f // Z, y, lax.rem(f, Z), 4 * rows :, :] = tall[y * fr : (y + 1) * fr, :]
    grad[...] = dot_nn(flipped[...], d_pre).astype(BF16)
    n, lane = (f * tile) // D, pl.multiple_of(lax.rem(f * tile, D), tile)
    for x in range(X):
        for c in range(2):
            for z in range(Z):
                for y in range(Y):
                    start = (((x * 2 + c) * Z + z) * Y + y) * rows
                    value = grad[start : start + rows, :]
                    grad_ref[x, y, z, at_rows((c * 2 + n) * rows, rows), pl.ds(lane, tile)] = value

    @pl.when(f == 0)
    def _():
        acc[...] = part
        back_ref[...] = back

    @pl.when(f > 0)
    def _():
        acc[...] += part
        back_ref[...] += back

    @pl.when(f == pl.num_programs(0) - 1)
    def _():
        own_ref[...] = acc[:T, :]
        give_ref[...] = acc[T:, :].astype(BF16)
        back_low_ref[:T, :] = back_ref[T:, :].astype(BF16)
        back_low_ref[T:, :] = back_ref[:T, :].astype(BF16)


def contract(dims, at, cot_own, cot_peer, second, pre, fc, low, high):
    X, Y, Z, T, chunks, wd = dims
    D, ffh = fc.shape
    tile = ffh // (X * Z)
    cut = tile // (2 * Y)
    rows = D // (2 * X * Y * Z)

    def block(f, at):
        return (f % Z, 1, 0)

    return pl.pallas_call(
        functools.partial(contract_kernel, dims),
        name="contract",
        grid_spec=pltpu.PrefetchScalarGridSpec(
            num_scalar_prefetch=1,
            grid=(X * Z,),
            in_specs=[full(v.shape) for v in (cot_own, cot_peer, second)]
            + [
                pl.BlockSpec((2 * T, tile), lambda f, at: (0, f)),
                pl.BlockSpec((D, tile), lambda f, at: (0, f)),
            ]
            + [pl.BlockSpec((1, cut, D), block)] * (2 * X * Y),
            out_specs=[
                full((T, D)), full((T, D)), full((2 * T, D)), full((2 * T, D)), full((2 * T, D)),
                pl.BlockSpec((1, tile), lambda f, at: (0, f)),
            ]
            + [full((X, Y, Z, 8 * rows, D))],
            scratch_shapes=[
                pltpu.VMEM((D, 2 * T), BF16),
                pltpu.VMEM((tile, D), BF16),
                pltpu.VMEM((D, tile), BF16),
                pltpu.VMEM((2 * T, D), F32),
            ],
        ),
        out_shape=[
            jax.ShapeDtypeStruct((T, D), F32),
            jax.ShapeDtypeStruct((T, D), BF16),
            jax.ShapeDtypeStruct((2 * T, D), F32),
            jax.ShapeDtypeStruct((2 * T, D), BF16),
            jax.ShapeDtypeStruct((2 * T, D), BF16),
            jax.ShapeDtypeStruct((1, ffh), F32),
        ]
        + [jax.ShapeDtypeStruct((X, Y, Z, 8 * rows, D), BF16)],
        compiler_params=vmem(60),
        cost_estimate=TINY,
    )(at, cot_own, cot_peer, second, pre, fc, *low, *high)


def middle_kernel(
    dims, back_ref, got_ref, resid_ref, dy_ref, gain_ref, w_ref, low_ref, wide_ref, msg_ref, sums_ref
):
    X, Y, Z, T, chunks, wd = dims
    b = pl.program_id(0)
    rows, D = back_ref.shape
    steps = T // rows
    normed, inverse = layer_stats(resid_ref[...])
    d_second = back_ref[...] + got_ref[...].astype(F32)
    dy = dy_ref[...].astype(F32)
    d_resid = dy + layer_back(d_second, normed, inverse, gain_ref[...])
    low = d_resid.astype(BF16)
    low_ref[...] = low
    wide_ref[...] = d_resid
    per = chunks // X
    start = pl.multiple_of(lax.rem(b, steps) * rows, rows)
    for x in range(X):
        out = dot_nt(low, w_ref[x * per * wd : (x + 1) * per * wd, :]).astype(BF16)
        for k in range(per):
            msg_ref[(b // steps) * chunks + x * per + k, pl.ds(start, rows), :] = out[:, k * wd : (k + 1) * wd]

    @pl.when(b == 0)
    def _():
        sums_ref[...] = jnp.zeros_like(sums_ref)

    @pl.when(b < steps)
    def _():
        for n, value in enumerate((d_resid, d_second * normed, d_second, dy)):
            sums_ref[n : n + 1, :] += jnp.sum(value, axis=0, keepdims=True)


def middle(dims, back, got, resid, dy, gain, w_own):
    X, Y, Z, T, chunks, wd = dims
    D = back.shape[1]
    block = min(128, T)
    row = pl.BlockSpec((block, D), lambda b: (b, 0))
    return pl.pallas_call(
        functools.partial(middle_kernel, dims),
        name="middle",
        grid=(2 * T // block,),
        in_specs=[row, row, row, row, full(gain.shape), full(w_own.shape)],
        out_specs=[row, row, full((2 * chunks, T, wd)), full((8, D))],
        out_shape=[
            jax.ShapeDtypeStruct((2 * T, D), BF16),
            jax.ShapeDtypeStruct((2 * T, D), F32),
            jax.ShapeDtypeStruct((2 * chunks, T, wd), BF16),
            jax.ShapeDtypeStruct((8, D), F32),
        ],
        compiler_params=vmem(60),
        cost_estimate=TINY,
    )(back, got, resid, dy, gain, w_own)


def project_back_kernel(
    dims, at_ref, d_ref, w_ref, first_ref, norm_ref, mine_ref, low_ref, own_ref, give_ref, sum_ref, sums_ref, *refs
):
    X, Y, Z, T, chunks, wd = dims
    a_refs, b_refs, (joint, block) = refs[:X], refs[X : X + Y], refs[X + Y :]
    g = pl.program_id(0)
    x, c = g // 2, pl.multiple_of(lax.rem(g, 2), 1)
    half = chunks * wd

    @pl.when(g == 0)
    def _():
        for r in range(2):
            for t in range(3):
                for h in range(chunks):
                    at = t * half + h * wd
                    joint[r * T : (r + 1) * T, at : at + wd] = d_ref[r * chunks + h, t]
        sum_ref[...] = jnp.sum(joint[...].astype(F32), axis=0, keepdims=True)

    part = dot_nt(joint[...], w_ref[...])
    own_ref[...] = part[:T, :]
    give_ref[...] = part[T:, :].astype(BF16)
    sums_ref[0:1, :] = jnp.sum(part * norm_ref[...], axis=0, keepdims=True)
    sums_ref[1:2, :] = jnp.sum(part, axis=0, keepdims=True)
    block[...] = dot_tn(first_ref[...], joint[...]).astype(BF16)
    rows = block.shape[0] // (Z * Y)
    for k in range(X):

        @pl.when(x == lax.rem(at_ref[0] + k, X))
        def _():
            a_refs[k][:, :, at_rows(c * rows, rows), :] = block[:, : 2 * half].reshape(Z, Y, rows, 2 * half)

    def spots(k):
        y = lax.rem(at_ref[3] + k, Y)
        return [(z, at_rows((z * Y + y) * rows, rows)) for z in range(Z)]

    for k in range(Y):
        for z, spot in spots(k):
            b_refs[k][x, z, :rows, at_rows(c * half, half)] = block[spot, 2 * half :]

    @pl.when(c == 0)
    def _():
        per = chunks // X
        left = [jnp.concatenate([mine_ref[r * chunks + x * per + j] for r in range(2)], axis=0) for j in range(per)]
        block[:, : 2 * half] = dot_tn(jnp.concatenate(left, axis=1), low_ref[...]).astype(BF16)
        for k in range(Y):
            for z, spot in spots(k):
                b_refs[k][x, z, rows:, :] = block[spot, : 2 * half]


def project_back(dims, at, d_msg, w, first, norm, mine, low):
    X, Y, Z, T, chunks, wd = dims
    D, cols = w.shape
    block = D // (2 * X)
    rows = block // (Z * Y)
    a_shape, b_shape = (Z, Y, 2 * rows, D), (X, Z, 2 * rows, D)
    return pl.pallas_call(
        functools.partial(project_back_kernel, dims),
        name="project_back",
        grid=(2 * X,),
        in_specs=[
            pl.BlockSpec(memory_space=pltpu.SMEM),
            full(d_msg.shape),
            pl.BlockSpec((block, cols), lambda g: (g, 0)),
            pl.BlockSpec((2 * T, block), lambda g: (0, g)),
            pl.BlockSpec((2 * T, block), lambda g: (0, g)),
            full(mine.shape), full(low.shape),
        ],
        out_specs=[
            pl.BlockSpec((T, block), lambda g: (0, g)),
            pl.BlockSpec((T, block), lambda g: (0, g)),
            full((1, cols)),
            pl.BlockSpec((8, block), lambda g: (0, g)),
        ]
        + [full(a_shape)] * X
        + [full(b_shape)] * Y,
        out_shape=[
            jax.ShapeDtypeStruct((T, D), F32),
            jax.ShapeDtypeStruct((T, D), BF16),
            jax.ShapeDtypeStruct((1, cols), F32),
            jax.ShapeDtypeStruct((8, D), F32),
        ]
        + [jax.ShapeDtypeStruct(a_shape, BF16)] * X
        + [jax.ShapeDtypeStruct(b_shape, BF16)] * Y,
        scratch_shapes=[pltpu.VMEM((2 * T, cols), BF16), pltpu.VMEM((block, cols), BF16)],
        compiler_params=vmem(60),
        cost_estimate=TINY,
    )(at, d_msg, w, first, norm, mine, low)


def combine_kernel(streams, at_ref, *refs):
    step, taken = pl.program_id(0), []
    for counts in streams:
        groups = []
        for count in counts:
            groups.append(refs[:count])
            refs = refs[count:]
        taken.append(groups)
    size = len(refs) // len(streams)
    for n, groups in enumerate(taken):
        for k, out_ref in enumerate(refs[n * size : (n + 1) * size]):

            @pl.when(step == k)
            def _():
                start = 0
                for group in groups:
                    total = group[0][...].astype(F32)
                    for ref in group[1:]:
                        total = total + ref[...].astype(F32)
                    total = total.reshape(out_ref.shape[:-2] + total.shape[-2:]).astype(out_ref.dtype)
                    out_ref[..., start : start + total.shape[-2], :] = total
                    start += total.shape[-2]


def combine(at, *streams, wide=False, cost=None):
    specs, outs, values, out_specs, counts = [], [], [], [], []
    size = streams[0][2][0][0].shape[streams[0][1]]
    for axis, dim, groups in streams:
        shape = groups[0][0].shape
        rest = tuple(n for d, n in enumerate(shape) if d != dim)
        out = rest[:-2] + (sum(g[0].shape[-2] for g in groups), rest[-1])

        def spec(shape, axis=axis, dim=dim):
            return pl.BlockSpec(
                tuple(1 if d == dim else n for d, n in enumerate(shape)),
                lambda k, at: tuple(lax.rem(at[axis] + k, size) if d == dim else 0 for d in range(len(shape))),
            )

        specs += [spec(v.shape) for g in groups for v in g]
        values += [v for g in groups for v in g]
        out_specs += [full(out)] * size
        outs += [jax.ShapeDtypeStruct(out, F32 if wide and k == 0 else BF16) for k in range(size)]
        counts.append(tuple(len(g) for g in groups))
    out = pl.pallas_call(
        functools.partial(combine_kernel, tuple(counts)),
        name="combine",
        grid_spec=pltpu.PrefetchScalarGridSpec(
            num_scalar_prefetch=1, grid=(size,), in_specs=specs, out_specs=out_specs
        ),
        out_shape=outs,
        compiler_params=vmem(60),
        cost_estimate=cost or TINY,
    )(at, *values)
    return [out[n * size : (n + 1) * size] for n in range(len(streams))]


def pick(array, index, dim):
    return lax.dynamic_index_in_dim(array, index, dim, keepdims=False)


def swap(array):
    return lax.ppermute(array, "c", SWAP)


def shift(array, axis, size, k):
    return lax.ppermute(array, axis, [(i, (i + k) % size) for i in range(size)])


def spread(array, axis, size):
    return jnp.stack([array] + [shift(array, axis, size, k) for k in range(1, size)])


def gather(array, first, first_size, second, second_size):
    base = [array] + [shift(array, first, first_size, k) for k in range(1, first_size)]
    return base + [shift(v, second, second_size, j) for j in range(1, second_size) for v in base]


def sent(parts, axis):
    return [parts[0]] + [shift(parts[k], axis, len(parts), k) for k in range(1, len(parts))]


def scatter_sum(array, axis, dim):
    size, me = array.shape[dim], lax.axis_index(axis)
    return sum(sent([pick(array, (me + k) % size, dim) for k in range(size)], axis))


def per_device(sizes, *args):
    (
        hidden, group_sizes, prefix_lens, sol_lens, ln1_gain, ln1_shift, qkv_weight, qv_bias, out_weight, out_bias,
        ln2_gain, ln2_shift, fc_weight, fc_bias, proj_weight, proj_bias, cotangent,
    ) = args
    X, Z, Y = sizes
    S, ND = Z * Y, 2 * X * Z * Y
    _, T, D = hidden.shape
    FF = fc_weight.shape[1]
    heads = D // HD // S
    wd, chunks = heads * HD, S // 2
    half, ffh = D // 2, FF // 2
    rows = D // ND
    dims = (X, Y, Z, T, chunks, wd)
    c, place = lax.axis_index("c"), lax.axis_index(SEQ)

    local = qkv_weight.reshape(rows, 3, X, 2, half // X)
    kept = pick(local, c, 3).reshape(rows, 3 * half)
    given = pick(local, 1 - c, 3).reshape(rows, 3 * half)
    piece = jnp.stack([kept, swap(given)])
    cut = 3 * half // 2
    piece_a, piece_b = spread(piece[..., :cut], "z", Z), spread(piece[..., cut:], "z", Z)

    local = fc_weight.reshape(rows, X, 2, ffh // X)
    kept, given = (pick(local, n, 2).reshape(rows, ffh) for n in (c, 1 - c))
    wide = [slice(n, n + D) for n in range(0, ffh, D)]
    got = swap(jnp.concatenate([given[:, n] for n in wide], axis=0))
    fr = FF // ND
    low = jnp.concatenate([kept[:, wide[0]], got[:rows], proj_weight[: fr // 2], out_weight], axis=0)
    high = jnp.concatenate([kept[:, wide[1]], got[rows:], proj_weight[fr // 2 :]], axis=0)
    low, high, piece_a, piece_b = lax.optimization_barrier((low, high, piece_a, piece_b))
    low, high = (lax.all_gather(v, "z", axis=0, tiled=False) for v in (low, high))
    pieces = gather(piece_a, "x", X, "y", Y) + gather(piece_b, "y", Y, "x", X)

    small = (ln1_gain, ln1_shift, qv_bias, out_bias, ln2_gain, ln2_shift, fc_bias, proj_bias)
    cuts = [0]
    for part in small:
        cuts.append(cuts[-1] + part.shape[0])
    packed = jnp.broadcast_to(jnp.concatenate(small)[None, :], (ND, cuts[-1]))
    packed = lax.all_to_all(packed, ALL, split_axis=0, concat_axis=0, tiled=True).astype(F32)
    gain1, shift1, qv_all, out_b, gain2, shift2, fc_b, proj_b = (
        packed[:, cuts[n] : cuts[n + 1]].reshape(1, -1) for n in range(8)
    )

    slot = jnp.arange(sol_lens.shape[1], dtype=jnp.int32)
    used = jnp.where(slot < group_sizes[0], sol_lens[0], 0)
    ends = prefix_lens[0] + jnp.sum(jnp.where(slot[None, :] <= slot[:, None], used[None, :], 0), axis=1)
    meta = jnp.concatenate([prefix_lens, ends, jnp.zeros((15,), jnp.int32)])
    meta_peer = swap(meta)
    meta_here = jnp.where(place < chunks, meta, meta_peer)
    where = [lax.axis_index("x"), c, lax.axis_index("z"), lax.axis_index("y"), place, meta[16], meta_peer[16]]
    at = jnp.stack(where).astype(jnp.int32)

    own, cot = hidden[0], cotangent[0]
    peer, cot_peer = swap(own), swap(cot)

    qv_here = pick(qv_all.reshape(2, X, 2, half // X), c, 2).reshape(2, half)
    bias = jnp.concatenate([qv_here[:1], jnp.zeros_like(qv_here[:1]), qv_here[1:]], axis=1)
    msg, w_qkv, first, norm = project(dims, at, own, peer, gain1, shift1, bias, pieces)

    def exchange(array):
        return lax.all_to_all(array, SEQ, split_axis=0, concat_axis=0, tiled=True)

    qkv = exchange(msg)
    low, high = gather(low, "y", Y, "x", X), gather(high, "x", X, "y", Y)
    att, att_wide, lse = attend(qkv, meta_here, heads)
    w_peer = swap(jnp.stack([v[:, fr:] for v in low]))
    mine = exchange(att)
    theirs = swap(mine)

    fc_b_here = pick(fc_b.reshape(X, 2, ffh // X), c, 1).reshape(1, ffh)
    resid, second, pre, w_own, w_fc = expand(
        dims, at, [own, peer, mine, theirs, out_b, gain2, shift2], fc_b_here, low, w_peer, high
    )
    out = contract(dims, at, cot, cot_peer, second, pre, w_fc, low, high)
    ahead, give, back, back_low, dy, fc_sum = out[:6]
    grads = lax.psum_scatter(out[6].reshape(X * Y, Z, -1, D), ("x", "y"), scatter_dimension=0, tiled=True)
    d_low, d_wide, d_msg, sums_mid = middle(dims, back, swap(back_low), resid, dy, gain2, w_own)
    up = exchange(d_msg)
    position = place * T + jnp.arange(T, dtype=jnp.int32)
    valid = (position < meta[16]).astype(F32)[:, None]
    layer_out = valid * (resid[:T] + (ahead + swap(give).astype(F32)) + proj_b)

    d_msg = attend_back(qkv, att_wide, lse, up, meta_here, heads)
    d_qkv = exchange(d_msg)
    out = list(project_back(dims, at, d_qkv, w_qkv, first, norm, mine, d_low))
    part, part_peer, qkv_sum, sums_first = out[:4]
    given = swap(part_peer)
    part_a, part_b = sent(out[4 : 4 + X], "x"), sent(out[4 + X :], "y")

    grads, _ = lax.optimization_barrier((grads, part))
    grads = lax.psum_scatter(grads[0], "z", scatter_dimension=0, tiled=True)[0].astype(F32)

    def both_halves(grad, blocks):
        kept = pick(grad, c, 0)
        got = swap(pick(grad, 1 - c, 0).astype(BF16)).astype(F32)
        shape = (kept.shape[0],) + blocks
        kept, got = kept.reshape(shape), got.reshape(shape)
        low = jnp.where(c == 0, kept, got)
        high = jnp.where(c == 0, got, kept)
        return jnp.stack([low, high], axis=-2).reshape(kept.shape[0], -1)

    fc_rows = 2 * ffh // D * rows
    fc_grad = grads[:fc_rows].reshape(2, ffh // D, rows, D).transpose(0, 2, 1, 3).reshape(2, rows, ffh)
    proj_grad = grads[fc_rows:]
    fc_grad = both_halves(fc_grad, (X, ffh // X))

    def own_columns(vector, lead):
        cut = vector.reshape(lead, X, 1, -1)
        spot = lax.broadcasted_iota(jnp.int32, (lead, X, 2, cut.shape[-1]), 2)
        return jnp.where(spot == c, cut, 0.0).reshape(-1)

    qv_sum = jnp.concatenate([qkv_sum[0, :half], qkv_sum[0, 2 * half :]])
    sums = (
        sums_first[0],
        sums_first[1],
        own_columns(qv_sum, 2),
        sums_mid[0],
        sums_mid[1],
        sums_mid[2],
        own_columns(fc_sum, 1),
        sums_mid[3],
    )
    packed = jnp.concatenate([v.reshape(ND, -1) for v in sums], axis=1).reshape(X, 2, Z, Y, -1)
    packed = scatter_sum(packed, "x", 0)

    part_a, part_b = combine(at, (3, 1, [part_a]), (0, 0, [part_b]))
    packed, *_ = lax.optimization_barrier((packed, *part_a, *part_b))
    part_a, part_b, packed = sent(part_a, "y"), sent(part_b, "x"), scatter_sum(packed, "y", 2)
    fc_grad, proj_grad, *ordered = lax.optimization_barrier((fc_grad, proj_grad, *part_a, *part_b))
    last = combine(at, (2, 0, [ordered[:Y], ordered[Y:]]), wide=True)[0]
    packed, *_ = lax.optimization_barrier((scatter_sum(packed, "c", 0), *last))
    packed = scatter_sum(packed, "z", 0)
    last = sent(last, "z")
    last = sum(v.astype(F32) for v in last)
    value = last[2 * rows : 3 * rows].reshape(rows, 2, half).transpose(1, 0, 2)
    qkv_grad = jnp.concatenate([last[: 2 * rows].reshape(2, rows, D), value], axis=2)
    out_grad = last[3 * rows :]
    qkv_grad = both_halves(qkv_grad, (3, X, half // X))

    d_first = part + given.astype(F32)
    norm, inverse = layer_stats(own.astype(F32))
    hidden_grad = d_wide[:T] + layer_back(d_first, norm, inverse, gain1)

    gain1_g, shift1_g, qv_g, out_b_g, gain2_g, shift2_g, fc_b_g, proj_b_g = (
        packed[cuts[n] : cuts[n + 1]] for n in range(8)
    )
    return (
        layer_out.astype(BF16)[None], hidden_grad.astype(BF16)[None], gain1_g, shift1_g, qkv_grad, qv_g, out_grad,
        out_b_g, gain2_g, shift2_g, fc_grad, fc_b_g, proj_grad, proj_b_g,
    )


def solution(mesh):
    Z = 4
    X, Y = mesh.shape["dp"] // 2, mesh.shape["seq"] // Z
    split = Mesh(mesh.devices.reshape(X, 2, Z, Y), ALL)
    group, wide, flat = P(("x", "c"), SEQ, None), P(ALL, None), P(ALL)
    dp = P(("x", "c"))
    return jax.shard_map(
        functools.partial(per_device, (X, Z, Y)),
        mesh=split,
        in_specs=(
            group, dp, dp, P(("x", "c"), None), flat, flat, wide, flat, wide, flat, flat, flat, wide, flat, wide, flat,
            group,
        ),
        out_specs=(
            group, group, flat, flat, wide, flat, wide, flat, flat, flat, wide, flat, wide, flat,
        ),
        check_vma=False,
    )
```

```python
import functools

import jax
import jax.numpy as jnp
from jax import lax
from jax.experimental import pallas as pl
from jax.experimental.pallas import tpu as pltpu
from jax.sharding import Mesh
from jax.sharding import PartitionSpec as P

HD = 64
EPSILON = 1e-05
BIG = 1e30
BLOCK = 256
DEPTH = 2
F32 = jnp.float32
LONG = pl.CostEstimate(flops=10**11, bytes_accessed=1, transcendentals=0)
TINY = pl.CostEstimate(flops=1, bytes_accessed=1, transcendentals=0)
BF16 = jnp.bfloat16
ALL = ("x", "c", "z", "y")
SEQ = ("z", "y")
SWAP = [(0, 1), (1, 0)]


def dot_nt(a, b):
    return lax.dot_general(a, b, (((1,), (1,)), ((), ())), preferred_element_type=F32)


def dot_nn(a, b):
    return lax.dot_general(a, b, (((1,), (0,)), ((), ())), preferred_element_type=F32)


def dot_tn(a, b):
    return lax.dot_general(a, b, (((0,), (0,)), ((), ())), preferred_element_type=F32)


def segment_code(ends_ref, start, rows, lanes):
    pos = start + lax.broadcasted_iota(jnp.int32, (rows, lanes), 0)
    passed = jnp.ones((rows, lanes), jnp.int32)
    for t in range(16):
        passed = passed + jnp.where(pos >= ends_ref[1 + t], 1, 0)
    code = jnp.where(pos < ends_ref[16], passed, 17)
    return jnp.where(pos < ends_ref[0], 0, code)


def with_segments(keys, ends_ref, start):
    rows, lanes = keys.shape
    code = segment_code(ends_ref, start, rows, lanes)
    lane = lax.broadcasted_iota(jnp.int32, (rows, lanes), 1)
    key_mark = jnp.where((code == lane) & (code > 0), 1.0, 0.0).astype(BF16)
    query_mark = jnp.where(code == lane, 0.0, -BIG).astype(BF16)
    return jnp.concatenate([keys, key_mark], axis=1), query_mark


def head_part(array, head, heads):
    if heads == 1:
        return array
    lane = lax.broadcasted_iota(jnp.int32, array.shape, 1)
    return jnp.where((lane >= head * HD) & (lane < (head + 1) * HD), array, jnp.zeros_like(array))


def causal(rows, cols, transposed):
    row = lax.broadcasted_iota(jnp.int32, (rows, cols), 0)
    col = lax.broadcasted_iota(jnp.int32, (rows, cols), 1)
    return (row <= col) if transposed else (col <= row)


def attend_kernel(heads, ends_ref, qkv_ref, out_ref, wide_ref, lse_ref, keys, values):
    i = pl.program_id(0)
    width = heads * HD
    start = pl.multiple_of(i * BLOCK, BLOCK)
    query_in, keys_in, values_in = (qkv_ref[:, t].reshape(BLOCK, width) for t in range(3))
    tagged, query_mark = with_segments(keys_in, ends_ref, start)
    keys[pl.ds(start, BLOCK), :] = tagged
    values[pl.ds(start, BLOCK), :] = values_in
    scaled = query_in * BF16(HD**-0.5)
    for n in range(keys.shape[0] // BLOCK):

        @pl.when(i == n)
        def _():
            before = n * BLOCK

            def one_head(h, wide):
                query = jnp.concatenate([head_part(scaled, h, heads), query_mark], axis=1)
                score = jnp.where(causal(BLOCK, BLOCK, False), dot_nt(query, tagged), -BIG)
                top = jnp.max(score, axis=1, keepdims=True)
                if n:
                    wide_score = dot_nt(query, keys[:before, :])
                    top = jnp.maximum(top, jnp.max(wide_score, axis=1, keepdims=True))
                expo = jnp.exp(score - top)
                total = jnp.sum(expo, axis=1, keepdims=True)
                acc = dot_nn(expo.astype(BF16), values_in)
                if n:
                    expo = jnp.exp(wide_score - top)
                    total = total + jnp.sum(expo, axis=1, keepdims=True)
                    acc = acc + dot_nn(expo.astype(BF16), values[:before, :])
                lse = jnp.broadcast_to(top + jnp.log(total), (BLOCK, 128))
                lse_ref[pl.ds(h, 1), :] = lse.T[0:1, :]
                return head_part(acc / total, h, heads) + wide

            wide_ref[...] = lax.fori_loop(0, heads, one_head, jnp.zeros((BLOCK, width), F32))

    out_ref[...] = wide_ref[...].astype(BF16).reshape(out_ref.shape)


def attend(qkv, ends, heads):
    length, width = qkv.shape[0] * qkv.shape[2], heads * HD
    T = qkv.shape[2]
    per = BLOCK // T
    return pl.pallas_call(
        functools.partial(attend_kernel, heads),
        name="attend",
        grid=(length // BLOCK,),
        in_specs=[
            pl.BlockSpec(memory_space=pltpu.SMEM),
            pl.BlockSpec((per, 3, T, width), lambda i: (i, 0, 0, 0)),
        ],
        out_specs=[
            pl.BlockSpec((per, T, width), lambda i: (i, 0, 0)),
            pl.BlockSpec((BLOCK, width), lambda i: (i, 0)),
            pl.BlockSpec((8, BLOCK), lambda i: (0, i)),
        ],
        out_shape=[
            jax.ShapeDtypeStruct((length // T, T, width), BF16),
            jax.ShapeDtypeStruct((length, width), F32),
            jax.ShapeDtypeStruct((8, length), F32),
        ],
        scratch_shapes=[
            pltpu.VMEM((length, 2 * width), BF16),
            pltpu.VMEM((length, width), BF16),
        ],
        compiler_params=pltpu.CompilerParams(vmem_limit_bytes=32 << 20),
        cost_estimate=TINY,
    )(ends, qkv)


def attend_back_kernel(
    heads, ends_ref, qkv_ref, wide_ref, lse_ref, up_ref, out_ref, keys, values, key_acc, value_acc, query_acc, inner_all
):
    i = pl.program_id(0)
    width = heads * HD
    start = pl.multiple_of(i * BLOCK, BLOCK)
    query_in, keys_in, values_in = (qkv_ref[:, t].reshape(BLOCK, width) for t in range(3))
    tagged, query_mark = with_segments(keys_in, ends_ref, start)
    keys[pl.ds(start, BLOCK), :] = tagged
    values[pl.ds(start, BLOCK), :] = values_in
    key_acc[pl.ds(start, BLOCK), :] = jnp.zeros((BLOCK, width), F32)
    value_acc[pl.ds(start, BLOCK), :] = jnp.zeros((BLOCK, width), F32)
    scaled = query_in * BF16(HD**-0.5)
    up = up_ref[...].reshape(BLOCK, width)
    inner_all[...] = (up.astype(F32) * wide_ref[...]).T
    query_acc[...] = jnp.zeros((BLOCK, width), F32)

    def step(h, first, rows, diagonal):
        spot = slice(first, first + rows)
        block, value = keys[spot, :], values[spot, :]
        part, up_part = head_part(scaled, h, heads), head_part(up, h, heads)
        score = dot_nt(block, jnp.concatenate([part, query_mark], axis=1))
        if diagonal:
            score = jnp.where(causal(BLOCK, BLOCK, True), score, -BIG)
        inner = jnp.sum(inner_all[pl.ds(pl.multiple_of(h * HD, HD), HD), :], axis=0, keepdims=True)
        prob = jnp.exp(score - lse_ref[pl.ds(h, 1), :])
        d_prob = dot_nt(value, up_part)
        d_score = (prob * (d_prob - inner)).astype(BF16)
        value_acc[spot, :] += dot_nn(prob.astype(BF16), up_part)
        key_acc[spot, :] += dot_nn(d_score, part)
        query_acc[...] += head_part(dot_tn(d_score, block[:, :width]), h, heads)

    for n in range(keys.shape[0] // BLOCK):

        @pl.when(i == n)
        def _():
            def one_head(h, carry):
                step(h, n * BLOCK, BLOCK, True)
                if n:
                    step(h, 0, n * BLOCK, False)
                return carry

            lax.fori_loop(0, heads, one_head, 0)

    d_query = query_acc[...] * HD**-0.5
    T = out_ref.shape[2]
    per = BLOCK // T
    out_ref[pl.ds(i * per, per), 0] = d_query.astype(BF16).reshape(per, T, width)

    @pl.when(i == pl.num_programs(0) - 1)
    def _():
        for s in range(out_ref.shape[0]):
            out_ref[s, 1] = key_acc[s * T : (s + 1) * T, :].astype(BF16)
            out_ref[s, 2] = value_acc[s * T : (s + 1) * T, :].astype(BF16)


def attend_back(qkv, wide, lse, up, ends, heads):
    length, width = qkv.shape[0] * qkv.shape[2], heads * HD
    T = qkv.shape[2]
    per = BLOCK // T
    return pl.pallas_call(
        functools.partial(attend_back_kernel, heads),
        name="attend_back",
        grid=(length // BLOCK,),
        in_specs=[
            pl.BlockSpec(memory_space=pltpu.SMEM),
            pl.BlockSpec((per, 3, T, width), lambda i: (i, 0, 0, 0)),
            pl.BlockSpec((BLOCK, width), lambda i: (i, 0)),
            pl.BlockSpec((8, BLOCK), lambda i: (0, i)),
            pl.BlockSpec((per, T, width), lambda i: (i, 0, 0)),
        ],
        out_specs=pl.BlockSpec((length // T, 3, T, width), lambda i: (0, 0, 0, 0)),
        out_shape=jax.ShapeDtypeStruct((length // T, 3, T, width), BF16),
        scratch_shapes=[
            pltpu.VMEM((length, 2 * width), BF16),
            pltpu.VMEM((length, width), BF16),
            pltpu.VMEM((length, width), F32),
            pltpu.VMEM((length, width), F32),
            pltpu.VMEM((BLOCK, width), F32),
            pltpu.VMEM((width, BLOCK), F32),
        ],
        compiler_params=pltpu.CompilerParams(vmem_limit_bytes=32 << 20),
        cost_estimate=TINY,
    )(ends, qkv, wide, lse, up)


def layer_stats(rows):
    centred = rows - jnp.mean(rows, axis=-1, keepdims=True)
    inverse = lax.rsqrt(jnp.mean(centred * centred, axis=-1, keepdims=True) + EPSILON)
    return centred * inverse, inverse


def layer_back(upstream, normed, inverse, gain):
    scaled = upstream * gain
    return inverse * (
        scaled
        - jnp.mean(scaled, axis=-1, keepdims=True)
        - normed * jnp.mean(scaled * normed, axis=-1, keepdims=True)
    )


def full(shape):
    return pl.BlockSpec(shape, lambda *_: (0,) * len(shape))


def vmem(mib):
    return pltpu.CompilerParams(vmem_limit_bytes=mib << 20)


def origin(k, me, size):
    return lax.rem(me - k + size, size)


def at_rows(start, rows):
    return pl.ds(pl.multiple_of(start, rows), rows)


def project_kernel(dims, at_ref, own_ref, peer_ref, gain_ref, shift_ref, bias_ref, *refs):
    X, Y, Z, T, chunks, wd = dims
    a_refs, b_refs, refs = refs[: X * Y], refs[X * Y : 2 * X * Y], refs[2 * X * Y :]
    msg_ref, w_out_ref, first_ref, norm_ref, w_ref = refs
    rows, part = a_refs[0].shape[-2:]
    width = w_ref.shape[1] // (3 * X)

    @pl.when((pl.program_id(0) == 0) & (pl.program_id(1) == 0))
    def _():
        x_me, c_me, z_me, y_me = (at_ref[n] for n in range(4))
        for kx in range(X):
            for ky in range(Y):
                x, y = origin(kx, x_me, X), origin(ky, y_me, Y)
                for kz in range(Z):
                    z = origin(kz, z_me, Z)
                    for kc in range(2):
                        c = lax.rem(c_me + kc, 2)
                        spot = at_rows((((x * 2 + c) * Z + z) * Y + y) * rows, rows)
                        w_ref[spot, :part] = a_refs[ky * X + kx][kz, kc]
                        w_ref[spot, part:] = b_refs[kx * Y + ky][kz, kc]
        for r, ref in enumerate((own_ref, peer_ref)):
            normed, _ = layer_stats(ref[...].astype(F32))
            norm_ref[r * T : (r + 1) * T, :] = normed.astype(BF16)
            first_ref[r * T : (r + 1) * T, :] = (normed * gain_ref[...] + shift_ref[...]).astype(BF16)

    t, x = pl.program_id(0), pl.program_id(1)
    col = pl.multiple_of((t * X + x) * width, width)
    w = w_ref[:, pl.ds(col, width)]
    w_out_ref[...] = w
    out = dot_nn(first_ref[...], w) + bias_ref[:, pl.ds(col, width)]
    out = out.astype(BF16)
    per = width // wd
    for r in range(2):
        for k in range(per):
            msg_ref[r * chunks + x * per + k, 0] = out[r * T : (r + 1) * T, k * wd : (k + 1) * wd]


def project(dims, at, own, peer, gain, shift, bias, pieces):
    X, Y, Z, T, chunks, wd = dims
    D = own.shape[1]
    cols = 2 * pieces[0].shape[-1]
    return pl.pallas_call(
        functools.partial(project_kernel, dims),
        name="project",
        grid=(3, X),
        in_specs=[pl.BlockSpec(memory_space=pltpu.SMEM)]
        + [full(v.shape) for v in (own, peer, gain, shift, bias, *pieces)],
        out_specs=[
            pl.BlockSpec((2 * chunks, 1, T, wd), lambda t, x: (0, t, 0, 0)),
            pl.BlockSpec((D, cols // (3 * X)), lambda t, x: (0, t * X + x)),
            full((2 * T, D)), full((2 * T, D)),
        ],
        scratch_shapes=[pltpu.VMEM((D, cols), BF16)],
        out_shape=[
            jax.ShapeDtypeStruct((2 * chunks, 3, T, wd), BF16),
            jax.ShapeDtypeStruct((D, cols), BF16),
            jax.ShapeDtypeStruct((2 * T, D), BF16),
            jax.ShapeDtypeStruct((2 * T, D), BF16),
        ],
        compiler_params=vmem(60),
        cost_estimate=TINY,
    )(at, own, peer, gain, shift, bias, *pieces)


def expand_kernel(dims, at_ref, *refs):
    X, Y, Z, T, chunks, wd = dims
    own_ref, peer_ref, mine_ref, theirs_ref, out_b_ref, gain_ref, shift_ref, fc_b_ref = refs[:8]
    refs = refs[8:]
    n = X * Y
    own_w_refs, low_refs, high_refs, refs = refs[:n], refs[n : 2 * n], refs[2 * n : 3 * n], refs[3 * n :]
    peer_w_ref, resid_ref, second_ref, pre_ref, w_own_ref, fc_ref, w_peer = refs
    D = own_ref.shape[1]
    rows = own_w_refs[0].shape[1]
    f = pl.program_id(0)
    x_me, c_me, y_me = (at_ref[n] for n in (0, 1, 3))

    @pl.when(f == 0)
    def _():
        for kx in range(X):
            for ky in range(Y):
                for kz in range(Z):
                    x, y, z = origin(kx, x_me, X), origin(ky, y_me, Y), kz
                    spot = at_rows(((x * Z + z) * Y + y) * rows, rows)
                    w_own_ref[spot, :] = own_w_refs[kx * Y + ky][kz]
                    w_peer[spot, :] = peer_w_ref[kx * Y + ky, kz]
        per = chunks // X
        width = per * wd
        for r, x_ref in enumerate((own_ref, peer_ref)):
            resid = x_ref[...].astype(F32) + out_b_ref[...]
            for source, base, w in ((mine_ref, r, w_own_ref), (theirs_ref, 1 - r, w_peer)):
                for x in range(X):
                    parts = [source[base * chunks + x * per + k] for k in range(per)]
                    resid = resid + dot_nn(jnp.concatenate(parts, axis=1), w[x * width : (x + 1) * width, :])
            part = slice(r * T, (r + 1) * T)
            resid_ref[part, :] = resid
            normed, _ = layer_stats(resid)
            second_ref[part, :] = (normed * gain_ref[...] + shift_ref[...]).astype(BF16)

    def place(block, kx, ky, kz):
        x, y, z = origin(kx, x_me, X), origin(ky, y_me, Y), kz
        for kc in range(2):
            c = lax.rem(c_me + kc, 2)
            fc_ref[at_rows((((x * 2 + c) * Z + z) * Y + y) * rows, rows), :] = block[kc * rows : (kc + 1) * rows, :]

    steps = pl.num_programs(0)

    @pl.when(f * 2 < steps)
    def _():
        for kx in range(X):
            for ky in range(Y):
                for kz in range(Z):
                    place(low_refs[kx * Y + ky][kz], kx, ky, kz)

    @pl.when(f * 2 >= steps)
    def _():
        for kx in range(X):
            for ky in range(Y):
                for kz in range(Z):
                    place(high_refs[ky * X + kx][kz], kx, ky, kz)

    pre_ref[...] = dot_nn(second_ref[...], fc_ref[...]) + fc_b_ref[...]


def expand(dims, at, inputs, fc_b, low, w_peer, high):
    X, Y, Z, T, chunks, wd = dims
    D = inputs[0].shape[1]
    half, ffh = D // 2, fc_b.shape[1]
    rows = half // (X * Y * Z)
    steps = X * Z // DEPTH
    tile, per = ffh // steps, steps // 2
    return pl.pallas_call(
        functools.partial(expand_kernel, dims),
        name="expand",
        grid_spec=pltpu.PrefetchScalarGridSpec(
            num_scalar_prefetch=1,
            grid=(steps,),
            in_specs=[full(v.shape) for v in inputs]
            + [pl.BlockSpec((1, tile), lambda f, at: (0, f))]
            + [pl.BlockSpec((Z, rows, D), lambda f, at: (0, 4, 0))] * (X * Y)
            + [pl.BlockSpec((Z, 2 * rows, tile), lambda f, at: (0, 0, jnp.minimum(f, per - 1)))] * (X * Y)
            + [pl.BlockSpec((Z, 2 * rows, tile), lambda f, at: (0, 0, jnp.maximum(f - per, 0)))] * (X * Y)
            + [full(w_peer.shape)],
            out_specs=[
                full((2 * T, D)), full((2 * T, D)),
                pl.BlockSpec((2 * T, tile), lambda f, at: (0, f)),
                full((half, D)),
                pl.BlockSpec((D, tile), lambda f, at: (0, f)),
            ],
            scratch_shapes=[pltpu.VMEM((half, D), BF16)],
        ),
        out_shape=[
            jax.ShapeDtypeStruct((2 * T, D), F32),
            jax.ShapeDtypeStruct((2 * T, D), BF16),
            jax.ShapeDtypeStruct((2 * T, ffh), F32),
            jax.ShapeDtypeStruct((half, D), BF16),
            jax.ShapeDtypeStruct((D, ffh), BF16),
        ],
        compiler_params=vmem(60),
        cost_estimate=TINY,
    )(at, *inputs, fc_b, *low, *low, *high, w_peer)


def contract_kernel(dims, at_ref, *refs):
    X, Y, Z, T, chunks, wd = dims
    cot_own_ref, cot_peer_ref, second_ref, pre_ref, fc_ref = refs[:5]
    refs = refs[5:]
    low_refs, high_refs, refs = refs[: X * Y], refs[X * Y : 2 * X * Y], refs[2 * X * Y :]
    own_ref, give_ref, back_ref, back_low_ref, dy_ref, fc_sum_ref = refs[:6]
    refs = refs[6:]
    grad_ref, flipped, proj, grad, acc = refs
    D = cot_own_ref.shape[1]
    tile = pre_ref.shape[1]
    fr = tile // (Y * DEPTH)
    zs = Z // DEPTH
    cut = fr // 2
    rows = grad_ref.shape[3] // 8
    f = pl.program_id(0)
    x_me, y_me, place = at_ref[0], at_ref[3], at_ref[4]

    @pl.when(f == 0)
    def _():
        for r, cot_ref in enumerate((cot_own_ref, cot_peer_ref)):
            pos = place * T + lax.broadcasted_iota(jnp.int32, (T, D), 0)
            dy_ref[r * T : (r + 1) * T, :] = jnp.where(pos < at_ref[5 + r], cot_ref[...], BF16(0.0))
        flipped[...] = second_ref[...].T

    for ky in range(Y):
        for kx in range(X):

            @pl.when(origin(kx, x_me, X) == f // zs)
            def _():
                for z in range(DEPTH):
                    start = (z * Y + origin(ky, y_me, Y)) * fr
                    proj[at_rows(start, cut), :] = low_refs[kx * Y + ky][z]
                    proj[at_rows(start + cut, cut), :] = high_refs[ky * X + kx][z]

    pre = pre_ref[...]
    d_act = dot_nt(dy_ref[...], proj[...])
    k0, k1 = 0.7978845608028654, 0.044715
    square = pre * pre
    tanh = jnp.tanh(k0 * (pre + k1 * (square * pre)))
    left = 0.5 * (1.0 + tanh)
    act = (pre * left).astype(BF16)
    slope = left + 0.5 * pre * (1.0 - tanh * tanh) * (k0 * (1.0 + 3.0 * k1 * square))
    d_pre = (slope * d_act).astype(BF16)
    fc_sum_ref[...] = jnp.sum(d_pre.astype(F32), axis=0, keepdims=True)
    part = dot_nn(act, proj[...])
    back = dot_nt(d_pre, fc_ref[...])
    tall = dot_tn(act, dy_ref[...]).astype(BF16)
    for z in range(DEPTH):
        for y in range(Y):
            start = (z * Y + y) * fr
            grad_ref[f // zs, y, lax.rem(f, zs) * DEPTH + z, 4 * rows :, :] = tall[start : start + fr, :]
    grad[...] = dot_nn(flipped[...], d_pre).astype(BF16)
    n, lane = (f * tile) // D, pl.multiple_of(lax.rem(f * tile, D), tile)
    for x in range(X):
        for c in range(2):
            for z in range(Z):
                for y in range(Y):
                    start = (((x * 2 + c) * Z + z) * Y + y) * rows
                    value = grad[start : start + rows, :]
                    grad_ref[x, y, z, at_rows((c * 2 + n) * rows, rows), pl.ds(lane, tile)] = value

    @pl.when(f == 0)
    def _():
        acc[...] = part
        back_ref[...] = back

    @pl.when(f > 0)
    def _():
        acc[...] += part
        back_ref[...] += back

    @pl.when(f == pl.num_programs(0) - 1)
    def _():
        own_ref[...] = acc[:T, :]
        give_ref[...] = acc[T:, :].astype(BF16)
        back_low_ref[:T, :] = back_ref[T:, :].astype(BF16)
        back_low_ref[T:, :] = back_ref[:T, :].astype(BF16)


def contract(dims, at, cot_own, cot_peer, second, pre, fc, low, high):
    X, Y, Z, T, chunks, wd = dims
    D, ffh = fc.shape
    steps = X * Z // DEPTH
    tile = ffh // steps
    cut = tile // (2 * Y * DEPTH)
    rows = D // (2 * X * Y * Z)

    def block(f, at):
        return (f % (Z // DEPTH), 1, 0)

    return pl.pallas_call(
        functools.partial(contract_kernel, dims),
        name="contract",
        grid_spec=pltpu.PrefetchScalarGridSpec(
            num_scalar_prefetch=1,
            grid=(steps,),
            in_specs=[full(v.shape) for v in (cot_own, cot_peer, second)]
            + [
                pl.BlockSpec((2 * T, tile), lambda f, at: (0, f)),
                pl.BlockSpec((D, tile), lambda f, at: (0, f)),
            ]
            + [pl.BlockSpec((DEPTH, cut, D), block)] * (2 * X * Y),
            out_specs=[
                full((T, D)), full((T, D)), full((2 * T, D)), full((2 * T, D)), full((2 * T, D)),
                pl.BlockSpec((1, tile), lambda f, at: (0, f)),
            ]
            + [full((X, Y, Z, 8 * rows, D))],
            scratch_shapes=[
                pltpu.VMEM((D, 2 * T), BF16),
                pltpu.VMEM((tile, D), BF16),
                pltpu.VMEM((D, tile), BF16),
                pltpu.VMEM((2 * T, D), F32),
            ],
        ),
        out_shape=[
            jax.ShapeDtypeStruct((T, D), F32),
            jax.ShapeDtypeStruct((T, D), BF16),
            jax.ShapeDtypeStruct((2 * T, D), F32),
            jax.ShapeDtypeStruct((2 * T, D), BF16),
            jax.ShapeDtypeStruct((2 * T, D), BF16),
            jax.ShapeDtypeStruct((1, ffh), F32),
        ]
        + [jax.ShapeDtypeStruct((X, Y, Z, 8 * rows, D), BF16)],
        compiler_params=vmem(60),
        cost_estimate=TINY,
    )(at, cot_own, cot_peer, second, pre, fc, *low, *high)


def middle_kernel(
    dims, back_ref, got_ref, resid_ref, dy_ref, gain_ref, w_ref, low_ref, wide_ref, msg_ref, sums_ref
):
    X, Y, Z, T, chunks, wd = dims
    b = pl.program_id(0)
    rows, D = back_ref.shape
    steps = T // rows
    normed, inverse = layer_stats(resid_ref[...])
    d_second = back_ref[...] + got_ref[...].astype(F32)
    dy = dy_ref[...].astype(F32)
    d_resid = dy + layer_back(d_second, normed, inverse, gain_ref[...])
    low = d_resid.astype(BF16)
    low_ref[...] = low
    wide_ref[...] = d_resid
    per = chunks // X
    start = pl.multiple_of(lax.rem(b, steps) * rows, rows)
    for x in range(X):
        out = dot_nt(low, w_ref[x * per * wd : (x + 1) * per * wd, :]).astype(BF16)
        for k in range(per):
            msg_ref[(b // steps) * chunks + x * per + k, pl.ds(start, rows), :] = out[:, k * wd : (k + 1) * wd]

    @pl.when(b == 0)
    def _():
        sums_ref[...] = jnp.zeros_like(sums_ref)

    @pl.when(b < steps)
    def _():
        for n, value in enumerate((d_resid, d_second * normed, d_second, dy)):
            sums_ref[n : n + 1, :] += jnp.sum(value, axis=0, keepdims=True)


def middle(dims, back, got, resid, dy, gain, w_own):
    X, Y, Z, T, chunks, wd = dims
    D = back.shape[1]
    block = min(128, T)
    row = pl.BlockSpec((block, D), lambda b: (b, 0))
    return pl.pallas_call(
        functools.partial(middle_kernel, dims),
        name="middle",
        grid=(2 * T // block,),
        in_specs=[row, row, row, row, full(gain.shape), full(w_own.shape)],
        out_specs=[row, row, full((2 * chunks, T, wd)), full((8, D))],
        out_shape=[
            jax.ShapeDtypeStruct((2 * T, D), BF16),
            jax.ShapeDtypeStruct((2 * T, D), F32),
            jax.ShapeDtypeStruct((2 * chunks, T, wd), BF16),
            jax.ShapeDtypeStruct((8, D), F32),
        ],
        compiler_params=vmem(60),
        cost_estimate=TINY,
    )(back, got, resid, dy, gain, w_own)


def project_back_kernel(
    dims, at_ref, d_ref, w_ref, first_ref, norm_ref, mine_ref, low_ref, own_ref, give_ref, sum_ref, sums_ref, *refs
):
    X, Y, Z, T, chunks, wd = dims
    a_refs, b_refs, (joint, block) = refs[:X], refs[X : X + Y], refs[X + Y :]
    g = pl.program_id(0)
    x, c = g // 2, pl.multiple_of(lax.rem(g, 2), 1)
    half = chunks * wd

    @pl.when(g == 0)
    def _():
        for r in range(2):
            for t in range(3):
                for h in range(chunks):
                    at = t * half + h * wd
                    joint[r * T : (r + 1) * T, at : at + wd] = d_ref[r * chunks + h, t]
        sum_ref[...] = jnp.sum(joint[...].astype(F32), axis=0, keepdims=True)

    part = dot_nt(joint[...], w_ref[...])
    own_ref[...] = part[:T, :]
    give_ref[...] = part[T:, :].astype(BF16)
    sums_ref[0:1, :] = jnp.sum(part * norm_ref[...].astype(F32), axis=0, keepdims=True)
    sums_ref[1:2, :] = jnp.sum(part, axis=0, keepdims=True)
    block[...] = dot_tn(first_ref[...], joint[...]).astype(BF16)
    rows = block.shape[0] // (Z * Y)
    for k in range(X):

        @pl.when(x == lax.rem(at_ref[0] + k, X))
        def _():
            a_refs[k][:, :, at_rows(c * rows, rows), :] = block[:, : 2 * half].reshape(Z, Y, rows, 2 * half)

    def spots(k):
        y = lax.rem(at_ref[3] + k, Y)
        return [(z, at_rows((z * Y + y) * rows, rows)) for z in range(Z)]

    for k in range(Y):
        for z, spot in spots(k):
            b_refs[k][x, z, :rows, at_rows(c * half, half)] = block[spot, 2 * half :]

    @pl.when(c == 0)
    def _():
        per = chunks // X
        left = [jnp.concatenate([mine_ref[r * chunks + x * per + j] for r in range(2)], axis=0) for j in range(per)]
        block[:, : 2 * half] = dot_tn(jnp.concatenate(left, axis=1), low_ref[...]).astype(BF16)
        for k in range(Y):
            for z, spot in spots(k):
                b_refs[k][x, z, rows:, :] = block[spot, : 2 * half]


def project_back(dims, at, d_msg, w, first, norm, mine, low):
    X, Y, Z, T, chunks, wd = dims
    D, cols = w.shape
    block = D // (2 * X)
    rows = block // (Z * Y)
    a_shape, b_shape = (Z, Y, 2 * rows, D), (X, Z, 2 * rows, D)
    return pl.pallas_call(
        functools.partial(project_back_kernel, dims),
        name="project_back",
        grid=(2 * X,),
        in_specs=[
            pl.BlockSpec(memory_space=pltpu.SMEM),
            full(d_msg.shape),
            pl.BlockSpec((block, cols), lambda g: (g, 0)),
            pl.BlockSpec((2 * T, block), lambda g: (0, g)),
            pl.BlockSpec((2 * T, block), lambda g: (0, g)),
            full(mine.shape), full(low.shape),
        ],
        out_specs=[
            pl.BlockSpec((T, block), lambda g: (0, g)),
            pl.BlockSpec((T, block), lambda g: (0, g)),
            full((1, cols)),
            pl.BlockSpec((8, block), lambda g: (0, g)),
        ]
        + [full(a_shape)] * X
        + [full(b_shape)] * Y,
        out_shape=[
            jax.ShapeDtypeStruct((T, D), F32),
            jax.ShapeDtypeStruct((T, D), BF16),
            jax.ShapeDtypeStruct((1, cols), F32),
            jax.ShapeDtypeStruct((8, D), F32),
        ]
        + [jax.ShapeDtypeStruct(a_shape, BF16)] * X
        + [jax.ShapeDtypeStruct(b_shape, BF16)] * Y,
        scratch_shapes=[pltpu.VMEM((2 * T, cols), BF16), pltpu.VMEM((block, cols), BF16)],
        compiler_params=vmem(60),
        cost_estimate=TINY,
    )(at, d_msg, w, first, norm, mine, low)


def combine_kernel(streams, at_ref, *refs):
    step, taken = pl.program_id(0), []
    for counts in streams:
        groups = []
        for count in counts:
            groups.append(refs[:count])
            refs = refs[count:]
        taken.append(groups)
    size = len(refs) // len(streams)
    for n, groups in enumerate(taken):
        for k, out_ref in enumerate(refs[n * size : (n + 1) * size]):

            @pl.when(step == k)
            def _():
                start = 0
                for group in groups:
                    total = group[0][...].astype(F32)
                    for ref in group[1:]:
                        total = total + ref[...].astype(F32)
                    total = total.reshape(out_ref.shape[:-2] + total.shape[-2:]).astype(out_ref.dtype)
                    out_ref[..., start : start + total.shape[-2], :] = total
                    start += total.shape[-2]


def combine(at, *streams, wide=False, cost=None):
    specs, outs, values, out_specs, counts = [], [], [], [], []
    size = streams[0][2][0][0].shape[streams[0][1]]
    for axis, dim, groups in streams:
        shape = groups[0][0].shape
        rest = tuple(n for d, n in enumerate(shape) if d != dim)
        out = rest[:-2] + (sum(g[0].shape[-2] for g in groups), rest[-1])

        def spec(shape, axis=axis, dim=dim):
            return pl.BlockSpec(
                tuple(1 if d == dim else n for d, n in enumerate(shape)),
                lambda k, at: tuple(lax.rem(at[axis] + k, size) if d == dim else 0 for d in range(len(shape))),
            )

        specs += [spec(v.shape) for g in groups for v in g]
        values += [v for g in groups for v in g]
        out_specs += [full(out)] * size
        outs += [jax.ShapeDtypeStruct(out, F32 if wide and k == 0 else BF16) for k in range(size)]
        counts.append(tuple(len(g) for g in groups))
    out = pl.pallas_call(
        functools.partial(combine_kernel, tuple(counts)),
        name="combine",
        grid_spec=pltpu.PrefetchScalarGridSpec(
            num_scalar_prefetch=1, grid=(size,), in_specs=specs, out_specs=out_specs
        ),
        out_shape=outs,
        compiler_params=vmem(60),
        cost_estimate=cost or TINY,
    )(at, *values)
    return [out[n * size : (n + 1) * size] for n in range(len(streams))]


def pick(array, index, dim):
    return lax.dynamic_index_in_dim(array, index, dim, keepdims=False)


def swap(array):
    return lax.ppermute(array, "c", SWAP)


def shift(array, axis, size, k):
    return lax.ppermute(array, axis, [(i, (i + k) % size) for i in range(size)])


def spread(array, axis, size):
    return jnp.stack([array] + [shift(array, axis, size, k) for k in range(1, size)])


def gather(array, first, first_size, second, second_size):
    base = [array] + [shift(array, first, first_size, k) for k in range(1, first_size)]
    return base + [shift(v, second, second_size, j) for j in range(1, second_size) for v in base]


def sent(parts, axis):
    return [parts[0]] + [shift(parts[k], axis, len(parts), k) for k in range(1, len(parts))]


def scatter_sum(array, axis, dim):
    size, me = array.shape[dim], lax.axis_index(axis)
    return sum(sent([pick(array, (me + k) % size, dim) for k in range(size)], axis))


def per_device(sizes, *args):
    (
        hidden, group_sizes, prefix_lens, sol_lens, ln1_gain, ln1_shift, qkv_weight, qv_bias, out_weight, out_bias,
        ln2_gain, ln2_shift, fc_weight, fc_bias, proj_weight, proj_bias, cotangent,
    ) = args
    X, Z, Y = sizes
    S, ND = Z * Y, 2 * X * Z * Y
    _, T, D = hidden.shape
    FF = fc_weight.shape[1]
    heads = D // HD // S
    wd, chunks = heads * HD, S // 2
    half, ffh = D // 2, FF // 2
    rows = D // ND
    dims = (X, Y, Z, T, chunks, wd)
    c, place = lax.axis_index("c"), lax.axis_index(SEQ)

    local = qkv_weight.reshape(rows, 3, X, 2, half // X)
    kept = pick(local, c, 3).reshape(rows, 3 * half)
    given = pick(local, 1 - c, 3).reshape(rows, 3 * half)
    piece = jnp.stack([kept, swap(given)])
    cut = 3 * half // 2
    piece_a, piece_b = spread(piece[..., :cut], "z", Z), spread(piece[..., cut:], "z", Z)

    local = fc_weight.reshape(rows, X, 2, ffh // X)
    kept, given = (pick(local, n, 2).reshape(rows, ffh) for n in (c, 1 - c))
    wide = [slice(n, n + D) for n in range(0, ffh, D)]
    got = swap(jnp.concatenate([given[:, n] for n in wide], axis=0))
    fr = FF // ND
    low = jnp.concatenate([kept[:, wide[0]], got[:rows], proj_weight[: fr // 2], out_weight], axis=0)
    high = jnp.concatenate([kept[:, wide[1]], got[rows:], proj_weight[fr // 2 :]], axis=0)
    low, high, piece_a, piece_b = lax.optimization_barrier((low, high, piece_a, piece_b))
    low, high = (lax.all_gather(v, "z", axis=0, tiled=False) for v in (low, high))
    pieces = gather(piece_a, "x", X, "y", Y) + gather(piece_b, "y", Y, "x", X)

    small = (ln1_gain, ln1_shift, qv_bias, out_bias, ln2_gain, ln2_shift, fc_bias, proj_bias)
    cuts = [0]
    for part in small:
        cuts.append(cuts[-1] + part.shape[0])
    packed = jnp.broadcast_to(jnp.concatenate(small)[None, :], (ND, cuts[-1]))
    packed = lax.all_to_all(packed, ALL, split_axis=0, concat_axis=0, tiled=True).astype(F32)
    gain1, shift1, qv_all, out_b, gain2, shift2, fc_b, proj_b = (
        packed[:, cuts[n] : cuts[n + 1]].reshape(1, -1) for n in range(8)
    )

    slot = jnp.arange(sol_lens.shape[1], dtype=jnp.int32)
    used = jnp.where(slot < group_sizes[0], sol_lens[0], 0)
    ends = prefix_lens[0] + jnp.sum(jnp.where(slot[None, :] <= slot[:, None], used[None, :], 0), axis=1)
    meta = jnp.concatenate([prefix_lens, ends, jnp.zeros((15,), jnp.int32)])
    meta_peer = swap(meta)
    meta_here = jnp.where(place < chunks, meta, meta_peer)
    where = [lax.axis_index("x"), c, lax.axis_index("z"), lax.axis_index("y"), place, meta[16], meta_peer[16]]
    at = jnp.stack(where).astype(jnp.int32)

    own, cot = hidden[0], cotangent[0]
    peer, cot_peer = swap(own), swap(cot)

    qv_here = pick(qv_all.reshape(2, X, 2, half // X), c, 2).reshape(2, half)
    bias = jnp.concatenate([qv_here[:1], jnp.zeros_like(qv_here[:1]), qv_here[1:]], axis=1)
    msg, w_qkv, first, norm = project(dims, at, own, peer, gain1, shift1, bias, pieces)

    def exchange(array):
        return lax.all_to_all(array, SEQ, split_axis=0, concat_axis=0, tiled=True)

    qkv = exchange(msg)
    low, high = gather(low, "y", Y, "x", X), gather(high, "x", X, "y", Y)
    att, att_wide, lse = attend(qkv, meta_here, heads)
    w_peer = swap(jnp.stack([v[:, fr:] for v in low]))
    mine = exchange(att)
    theirs = swap(mine)

    fc_b_here = pick(fc_b.reshape(X, 2, ffh // X), c, 1).reshape(1, ffh)
    resid, second, pre, w_own, w_fc = expand(
        dims, at, [own, peer, mine, theirs, out_b, gain2, shift2], fc_b_here, low, w_peer, high
    )
    out = contract(dims, at, cot, cot_peer, second, pre, w_fc, low, high)
    ahead, give, back, back_low, dy, fc_sum = out[:6]
    grads = lax.psum_scatter(out[6].reshape(X * Y, Z, -1, D), ("x", "y"), scatter_dimension=0, tiled=True)
    d_low, d_wide, d_msg, sums_mid = middle(dims, back, swap(back_low), resid, dy, gain2, w_own)
    up = exchange(d_msg)
    position = place * T + jnp.arange(T, dtype=jnp.int32)
    valid = (position < meta[16]).astype(F32)[:, None]
    layer_out = valid * (resid[:T] + (ahead + swap(give).astype(F32)) + proj_b)

    d_msg = attend_back(qkv, att_wide, lse, up, meta_here, heads)
    d_qkv = exchange(d_msg)
    out = list(project_back(dims, at, d_qkv, w_qkv, first, norm, mine, d_low))
    part, part_peer, qkv_sum, sums_first = out[:4]
    given = swap(part_peer)
    part_a, part_b = sent(out[4 : 4 + X], "x"), sent(out[4 + X :], "y")

    grads, _ = lax.optimization_barrier((grads, part))
    grads = lax.psum_scatter(grads[0], "z", scatter_dimension=0, tiled=True)[0].astype(F32)

    def both_halves(grad, blocks):
        kept = pick(grad, c, 0)
        got = swap(pick(grad, 1 - c, 0).astype(BF16)).astype(F32)
        shape = (kept.shape[0],) + blocks
        kept, got = kept.reshape(shape), got.reshape(shape)
        low = jnp.where(c == 0, kept, got)
        high = jnp.where(c == 0, got, kept)
        return jnp.stack([low, high], axis=-2).reshape(kept.shape[0], -1)

    fc_rows = 2 * ffh // D * rows
    fc_grad = grads[:fc_rows].reshape(2, ffh // D, rows, D).transpose(0, 2, 1, 3).reshape(2, rows, ffh)
    proj_grad = grads[fc_rows:]
    fc_grad = both_halves(fc_grad, (X, ffh // X))

    def own_columns(vector, lead):
        cut = vector.reshape(lead, X, 1, -1)
        spot = lax.broadcasted_iota(jnp.int32, (lead, X, 2, cut.shape[-1]), 2)
        return jnp.where(spot == c, cut, 0.0).reshape(-1)

    qv_sum = jnp.concatenate([qkv_sum[0, :half], qkv_sum[0, 2 * half :]])
    sums = (
        sums_first[0],
        sums_first[1],
        own_columns(qv_sum, 2),
        sums_mid[0],
        sums_mid[1],
        sums_mid[2],
        own_columns(fc_sum, 1),
        sums_mid[3],
    )
    packed = jnp.concatenate([v.reshape(ND, -1) for v in sums], axis=1).reshape(X, 2, Z, Y, -1)
    packed = scatter_sum(packed, "x", 0)

    part_a, part_b = combine(at, (3, 1, [part_a]), (0, 0, [part_b]))
    packed, *_ = lax.optimization_barrier((packed, *part_a, *part_b))
    part_a, part_b, packed = sent(part_a, "y"), sent(part_b, "x"), scatter_sum(packed, "y", 2)
    packed = scatter_sum(scatter_sum(packed, "c", 0), "z", 0)
    d_first = part + given.astype(F32)
    norm, inverse = layer_stats(own.astype(F32))
    hidden_grad = d_wide[:T] + layer_back(d_first, norm, inverse, gain1)
    hidden_grad, layer_out = hidden_grad.astype(BF16), layer_out.astype(BF16)
    hidden_grad, layer_out, packed, fc_grad, proj_grad, *ordered = lax.optimization_barrier(
        (hidden_grad, layer_out, packed, fc_grad, proj_grad, *part_a, *part_b)
    )
    last = combine(at, (2, 0, [ordered[:Y], ordered[Y:]]), wide=True)[0]
    last = sent(last, "z")
    last = sum(v.astype(F32) for v in last)
    value = last[2 * rows : 3 * rows].reshape(rows, 2, half).transpose(1, 0, 2)
    qkv_grad = jnp.concatenate([last[: 2 * rows].reshape(2, rows, D), value], axis=2)
    out_grad = last[3 * rows :]
    qkv_grad = both_halves(qkv_grad, (3, X, half // X))

    gain1_g, shift1_g, qv_g, out_b_g, gain2_g, shift2_g, fc_b_g, proj_b_g = (
        packed[cuts[n] : cuts[n + 1]] for n in range(8)
    )
    return (
        layer_out[None], hidden_grad[None], gain1_g, shift1_g, qkv_grad, qv_g, out_grad,
        out_b_g, gain2_g, shift2_g, fc_grad, fc_b_g, proj_grad, proj_b_g,
    )


def solution(mesh):
    Z = 4
    X, Y = mesh.shape["dp"] // 2, mesh.shape["seq"] // Z
    split = Mesh(mesh.devices.reshape(X, 2, Z, Y), ALL)
    group, wide, flat = P(("x", "c"), SEQ, None), P(ALL, None), P(ALL)
    dp = P(("x", "c"))
    return jax.shard_map(
        functools.partial(per_device, (X, Z, Y)),
        mesh=split,
        in_specs=(
            group, dp, dp, P(("x", "c"), None), flat, flat, wide, flat, wide, flat, flat, flat, wide, flat, wide, flat,
            group,
        ),
        out_specs=(
            group, group, flat, flat, wide, flat, wide, flat, flat, flat, wide, flat, wide, flat,
        ),
        check_vma=False,
    )
```

```python
import functools

import jax
import jax.numpy as jnp
from jax import lax
from jax.experimental import pallas as pl
from jax.experimental.pallas import tpu as pltpu
from jax.sharding import Mesh
from jax.sharding import PartitionSpec as P

HD = 64
EPSILON = 1e-05
BIG = 1e30
BLOCK = 256
DEPTH = 2
F32 = jnp.float32
LONG = pl.CostEstimate(flops=10**11, bytes_accessed=1, transcendentals=0)
TINY = pl.CostEstimate(flops=1, bytes_accessed=1, transcendentals=0)
BF16 = jnp.bfloat16
ALL = ("x", "c", "z", "y")
SEQ = ("z", "y")
SWAP = [(0, 1), (1, 0)]


def dot_nt(a, b):
    return lax.dot_general(a, b, (((1,), (1,)), ((), ())), preferred_element_type=F32)


def dot_nn(a, b):
    return lax.dot_general(a, b, (((1,), (0,)), ((), ())), preferred_element_type=F32)


def dot_tn(a, b):
    return lax.dot_general(a, b, (((0,), (0,)), ((), ())), preferred_element_type=F32)


def segment_code(ends_ref, start, rows, lanes):
    pos = start + lax.broadcasted_iota(jnp.int32, (rows, lanes), 0)
    passed = jnp.ones((rows, lanes), jnp.int32)
    for t in range(16):
        passed = passed + jnp.where(pos >= ends_ref[1 + t], 1, 0)
    code = jnp.where(pos < ends_ref[16], passed, 17)
    return jnp.where(pos < ends_ref[0], 0, code)


def with_segments(keys, ends_ref, start):
    rows, lanes = keys.shape
    code = segment_code(ends_ref, start, rows, lanes)
    lane = lax.broadcasted_iota(jnp.int32, (rows, lanes), 1)
    key_mark = jnp.where((code == lane) & (code > 0), 1.0, 0.0).astype(BF16)
    query_mark = jnp.where(code == lane, 0.0, -BIG).astype(BF16)
    return jnp.concatenate([keys, key_mark], axis=1), query_mark


def head_part(array, head, heads):
    if heads == 1:
        return array
    lane = lax.broadcasted_iota(jnp.int32, array.shape, 1)
    return jnp.where((lane >= head * HD) & (lane < (head + 1) * HD), array, jnp.zeros_like(array))


def causal(rows, cols, transposed):
    row = lax.broadcasted_iota(jnp.int32, (rows, cols), 0)
    col = lax.broadcasted_iota(jnp.int32, (rows, cols), 1)
    return (row <= col) if transposed else (col <= row)


def attend_kernel(heads, ends_ref, qkv_ref, out_ref, wide_ref, lse_ref, keys, values):
    i = pl.program_id(0)
    width = heads * HD
    start = pl.multiple_of(i * BLOCK, BLOCK)
    query_in, keys_in, values_in = (qkv_ref[:, t].reshape(BLOCK, width) for t in range(3))
    tagged, query_mark = with_segments(keys_in, ends_ref, start)
    keys[pl.ds(start, BLOCK), :] = tagged
    values[pl.ds(start, BLOCK), :] = values_in
    scaled = query_in * BF16(HD**-0.5)
    for n in range(keys.shape[0] // BLOCK):

        @pl.when(i == n)
        def _():
            before = n * BLOCK

            def one_head(h, wide):
                query = jnp.concatenate([head_part(scaled, h, heads), query_mark], axis=1)
                score = jnp.where(causal(BLOCK, BLOCK, False), dot_nt(query, tagged), -BIG)
                top = jnp.max(score, axis=1, keepdims=True)
                if n:
                    wide_score = dot_nt(query, keys[:before, :])
                    top = jnp.maximum(top, jnp.max(wide_score, axis=1, keepdims=True))
                expo = jnp.exp(score - top)
                total = jnp.sum(expo, axis=1, keepdims=True)
                acc = dot_nn(expo.astype(BF16), values_in)
                if n:
                    expo = jnp.exp(wide_score - top)
                    total = total + jnp.sum(expo, axis=1, keepdims=True)
                    acc = acc + dot_nn(expo.astype(BF16), values[:before, :])
                lse = jnp.broadcast_to(top + jnp.log(total), (BLOCK, 128))
                lse_ref[pl.ds(h, 1), :] = lse.T[0:1, :]
                return head_part(acc / total, h, heads) + wide

            wide_ref[...] = lax.fori_loop(0, heads, one_head, jnp.zeros((BLOCK, width), F32))

    out_ref[...] = wide_ref[...].astype(BF16).reshape(out_ref.shape)


def attend(qkv, ends, heads):
    length, width = qkv.shape[0] * qkv.shape[2], heads * HD
    T = qkv.shape[2]
    per = BLOCK // T
    return pl.pallas_call(
        functools.partial(attend_kernel, heads),
        name="attend",
        grid=(length // BLOCK,),
        in_specs=[
            pl.BlockSpec(memory_space=pltpu.SMEM),
            pl.BlockSpec((per, 3, T, width), lambda i: (i, 0, 0, 0)),
        ],
        out_specs=[
            pl.BlockSpec((per, T, width), lambda i: (i, 0, 0)),
            pl.BlockSpec((BLOCK, width), lambda i: (i, 0)),
            pl.BlockSpec((8, BLOCK), lambda i: (0, i)),
        ],
        out_shape=[
            jax.ShapeDtypeStruct((length // T, T, width), BF16),
            jax.ShapeDtypeStruct((length, width), F32),
            jax.ShapeDtypeStruct((8, length), F32),
        ],
        scratch_shapes=[
            pltpu.VMEM((length, 2 * width), BF16),
            pltpu.VMEM((length, width), BF16),
        ],
        compiler_params=pltpu.CompilerParams(vmem_limit_bytes=32 << 20),
        cost_estimate=TINY,
    )(ends, qkv)


def attend_back_kernel(
    heads, ends_ref, qkv_ref, wide_ref, lse_ref, up_ref, out_ref, keys, values, key_acc, value_acc, query_acc, inner_all
):
    i = pl.program_id(0)
    width = heads * HD
    start = pl.multiple_of(i * BLOCK, BLOCK)
    query_in, keys_in, values_in = (qkv_ref[:, t].reshape(BLOCK, width) for t in range(3))
    tagged, query_mark = with_segments(keys_in, ends_ref, start)
    keys[pl.ds(start, BLOCK), :] = tagged
    values[pl.ds(start, BLOCK), :] = values_in
    key_acc[pl.ds(start, BLOCK), :] = jnp.zeros((BLOCK, width), F32)
    value_acc[pl.ds(start, BLOCK), :] = jnp.zeros((BLOCK, width), F32)
    scaled = query_in * BF16(HD**-0.5)
    up = up_ref[...].reshape(BLOCK, width)
    inner_all[...] = (up.astype(F32) * wide_ref[...]).T
    query_acc[...] = jnp.zeros((BLOCK, width), F32)

    def step(h, first, rows, diagonal):
        spot = slice(first, first + rows)
        block, value = keys[spot, :], values[spot, :]
        part, up_part = head_part(scaled, h, heads), head_part(up, h, heads)
        score = dot_nt(block, jnp.concatenate([part, query_mark], axis=1))
        if diagonal:
            score = jnp.where(causal(BLOCK, BLOCK, True), score, -BIG)
        inner = jnp.sum(inner_all[pl.ds(pl.multiple_of(h * HD, HD), HD), :], axis=0, keepdims=True)
        prob = jnp.exp(score - lse_ref[pl.ds(h, 1), :])
        d_prob = dot_nt(value, up_part)
        d_score = (prob * (d_prob - inner)).astype(BF16)
        value_acc[spot, :] += dot_nn(prob.astype(BF16), up_part)
        key_acc[spot, :] += dot_nn(d_score, part)
        query_acc[...] += head_part(dot_tn(d_score, block[:, :width]), h, heads)

    for n in range(keys.shape[0] // BLOCK):

        @pl.when(i == n)
        def _():
            def one_head(h, carry):
                step(h, n * BLOCK, BLOCK, True)
                if n:
                    step(h, 0, n * BLOCK, False)
                return carry

            lax.fori_loop(0, heads, one_head, 0)

    d_query = query_acc[...] * HD**-0.5
    T = out_ref.shape[2]
    per = BLOCK // T
    out_ref[pl.ds(i * per, per), 0] = d_query.astype(BF16).reshape(per, T, width)

    @pl.when(i == pl.num_programs(0) - 1)
    def _():
        for s in range(out_ref.shape[0]):
            out_ref[s, 1] = key_acc[s * T : (s + 1) * T, :].astype(BF16)
            out_ref[s, 2] = value_acc[s * T : (s + 1) * T, :].astype(BF16)


def attend_back(qkv, wide, lse, up, ends, heads):
    length, width = qkv.shape[0] * qkv.shape[2], heads * HD
    T = qkv.shape[2]
    per = BLOCK // T
    return pl.pallas_call(
        functools.partial(attend_back_kernel, heads),
        name="attend_back",
        grid=(length // BLOCK,),
        in_specs=[
            pl.BlockSpec(memory_space=pltpu.SMEM),
            pl.BlockSpec((per, 3, T, width), lambda i: (i, 0, 0, 0)),
            pl.BlockSpec((BLOCK, width), lambda i: (i, 0)),
            pl.BlockSpec((8, BLOCK), lambda i: (0, i)),
            pl.BlockSpec((per, T, width), lambda i: (i, 0, 0)),
        ],
        out_specs=pl.BlockSpec((length // T, 3, T, width), lambda i: (0, 0, 0, 0)),
        out_shape=jax.ShapeDtypeStruct((length // T, 3, T, width), BF16),
        scratch_shapes=[
            pltpu.VMEM((length, 2 * width), BF16),
            pltpu.VMEM((length, width), BF16),
            pltpu.VMEM((length, width), F32),
            pltpu.VMEM((length, width), F32),
            pltpu.VMEM((BLOCK, width), F32),
            pltpu.VMEM((width, BLOCK), F32),
        ],
        compiler_params=pltpu.CompilerParams(vmem_limit_bytes=32 << 20),
        cost_estimate=TINY,
    )(ends, qkv, wide, lse, up)


def layer_stats(rows):
    centred = rows - jnp.mean(rows, axis=-1, keepdims=True)
    inverse = lax.rsqrt(jnp.mean(centred * centred, axis=-1, keepdims=True) + EPSILON)
    return centred * inverse, inverse


def layer_back(upstream, normed, inverse, gain):
    scaled = upstream * gain
    return inverse * (
        scaled
        - jnp.mean(scaled, axis=-1, keepdims=True)
        - normed * jnp.mean(scaled * normed, axis=-1, keepdims=True)
    )


def full(shape):
    return pl.BlockSpec(shape, lambda *_: (0,) * len(shape))


def vmem(mib):
    return pltpu.CompilerParams(vmem_limit_bytes=mib << 20)


def origin(k, me, size):
    return lax.rem(me - k + size, size)


def at_rows(start, rows):
    return pl.ds(pl.multiple_of(start, rows), rows)


def project_kernel(dims, at_ref, own_ref, peer_ref, gain_ref, shift_ref, bias_ref, *refs):
    X, Y, Z, T, chunks, wd = dims
    a_refs, b_refs, refs = refs[: X * Y], refs[X * Y : 2 * X * Y], refs[2 * X * Y :]
    msg_ref, w_out_ref, first_ref, norm_ref, w_ref = refs
    rows, part = a_refs[0].shape[-2:]
    width = w_ref.shape[1] // (3 * X)

    @pl.when((pl.program_id(0) == 0) & (pl.program_id(1) == 0))
    def _():
        x_me, c_me, z_me, y_me = (at_ref[n] for n in range(4))
        for kx in range(X):
            for ky in range(Y):
                x, y = origin(kx, x_me, X), origin(ky, y_me, Y)
                for kz in range(Z):
                    z = origin(kz, z_me, Z)
                    for kc in range(2):
                        c = lax.rem(c_me + kc, 2)
                        spot = at_rows((((x * 2 + c) * Z + z) * Y + y) * rows, rows)
                        w_ref[spot, :part] = a_refs[ky * X + kx][kz, kc]
                        w_ref[spot, part:] = b_refs[kx * Y + ky][kz, kc]
        for r, ref in enumerate((own_ref, peer_ref)):
            normed, _ = layer_stats(ref[...].astype(F32))
            norm_ref[r * T : (r + 1) * T, :] = normed.astype(BF16)
            first_ref[r * T : (r + 1) * T, :] = (normed * gain_ref[...] + shift_ref[...]).astype(BF16)

    t, x = pl.program_id(0), pl.program_id(1)
    col = pl.multiple_of((t * X + x) * width, width)
    w = w_ref[:, pl.ds(col, width)]
    w_out_ref[...] = w
    out = dot_nn(first_ref[...], w) + bias_ref[:, pl.ds(col, width)]
    out = out.astype(BF16)
    per = width // wd
    for r in range(2):
        for k in range(per):
            msg_ref[r * chunks + x * per + k, 0] = out[r * T : (r + 1) * T, k * wd : (k + 1) * wd]


def project(dims, at, own, peer, gain, shift, bias, pieces):
    X, Y, Z, T, chunks, wd = dims
    D = own.shape[1]
    cols = 2 * pieces[0].shape[-1]
    return pl.pallas_call(
        functools.partial(project_kernel, dims),
        name="project",
        grid=(3, X),
        in_specs=[pl.BlockSpec(memory_space=pltpu.SMEM)]
        + [full(v.shape) for v in (own, peer, gain, shift, bias, *pieces)],
        out_specs=[
            pl.BlockSpec((2 * chunks, 1, T, wd), lambda t, x: (0, t, 0, 0)),
            pl.BlockSpec((D, cols // (3 * X)), lambda t, x: (0, t * X + x)),
            full((2 * T, D)), full((2 * T, D)),
        ],
        scratch_shapes=[pltpu.VMEM((D, cols), BF16)],
        out_shape=[
            jax.ShapeDtypeStruct((2 * chunks, 3, T, wd), BF16),
            jax.ShapeDtypeStruct((D, cols), BF16),
            jax.ShapeDtypeStruct((2 * T, D), BF16),
            jax.ShapeDtypeStruct((2 * T, D), BF16),
        ],
        compiler_params=vmem(60),
        cost_estimate=TINY,
    )(at, own, peer, gain, shift, bias, *pieces)


def expand_kernel(dims, at_ref, *refs):
    X, Y, Z, T, chunks, wd = dims
    own_ref, peer_ref, mine_ref, theirs_ref, out_b_ref, gain_ref, shift_ref, fc_b_ref = refs[:8]
    refs = refs[8:]
    n = X * Y
    own_w_refs, low_refs, high_refs, refs = refs[:n], refs[n : 2 * n], refs[2 * n : 3 * n], refs[3 * n :]
    peer_w_ref, resid_ref, second_ref, pre_ref, w_own_ref, fc_ref, w_peer = refs
    D = own_ref.shape[1]
    rows = own_w_refs[0].shape[1]
    f = pl.program_id(0)
    x_me, c_me, y_me = (at_ref[n] for n in (0, 1, 3))

    @pl.when(f == 0)
    def _():
        for kx in range(X):
            for ky in range(Y):
                for kz in range(Z):
                    x, y, z = origin(kx, x_me, X), origin(ky, y_me, Y), kz
                    spot = at_rows(((x * Z + z) * Y + y) * rows, rows)
                    w_own_ref[spot, :] = own_w_refs[kx * Y + ky][kz]
                    w_peer[spot, :] = peer_w_ref[kx * Y + ky, kz]
        per = chunks // X
        width = per * wd
        for r, x_ref in enumerate((own_ref, peer_ref)):
            resid = x_ref[...].astype(F32) + out_b_ref[...]
            for source, base, w in ((mine_ref, r, w_own_ref), (theirs_ref, 1 - r, w_peer)):
                for x in range(X):
                    parts = [source[base * chunks + x * per + k] for k in range(per)]
                    resid = resid + dot_nn(jnp.concatenate(parts, axis=1), w[x * width : (x + 1) * width, :])
            part = slice(r * T, (r + 1) * T)
            resid_ref[part, :] = resid
            normed, _ = layer_stats(resid)
            second_ref[part, :] = (normed * gain_ref[...] + shift_ref[...]).astype(BF16)

    def place(block, kx, ky, kz):
        x, y, z = origin(kx, x_me, X), origin(ky, y_me, Y), kz
        for kc in range(2):
            c = lax.rem(c_me + kc, 2)
            fc_ref[at_rows((((x * 2 + c) * Z + z) * Y + y) * rows, rows), :] = block[kc * rows : (kc + 1) * rows, :]

    steps = pl.num_programs(0)

    @pl.when(f * 2 < steps)
    def _():
        for kx in range(X):
            for ky in range(Y):
                for kz in range(Z):
                    place(low_refs[kx * Y + ky][kz], kx, ky, kz)

    @pl.when(f * 2 >= steps)
    def _():
        for kx in range(X):
            for ky in range(Y):
                for kz in range(Z):
                    place(high_refs[ky * X + kx][kz], kx, ky, kz)

    pre_ref[...] = dot_nn(second_ref[...], fc_ref[...]) + fc_b_ref[...]


def expand(dims, at, inputs, fc_b, low, w_peer, high):
    X, Y, Z, T, chunks, wd = dims
    D = inputs[0].shape[1]
    half, ffh = D // 2, fc_b.shape[1]
    rows = half // (X * Y * Z)
    steps = X * Z // DEPTH
    tile, per = ffh // steps, steps // 2
    return pl.pallas_call(
        functools.partial(expand_kernel, dims),
        name="expand",
        grid_spec=pltpu.PrefetchScalarGridSpec(
            num_scalar_prefetch=1,
            grid=(steps,),
            in_specs=[full(v.shape) for v in inputs]
            + [pl.BlockSpec((1, tile), lambda f, at: (0, f))]
            + [pl.BlockSpec((Z, rows, D), lambda f, at: (0, 4, 0))] * (X * Y)
            + [pl.BlockSpec((Z, 2 * rows, tile), lambda f, at: (0, 0, jnp.minimum(f, per - 1)))] * (X * Y)
            + [pl.BlockSpec((Z, 2 * rows, tile), lambda f, at: (0, 0, jnp.maximum(f - per, 0)))] * (X * Y)
            + [full(w_peer.shape)],
            out_specs=[
                full((2 * T, D)), full((2 * T, D)),
                pl.BlockSpec((2 * T, tile), lambda f, at: (0, f)),
                full((half, D)),
                pl.BlockSpec((D, tile), lambda f, at: (0, f)),
            ],
            scratch_shapes=[pltpu.VMEM((half, D), BF16)],
        ),
        out_shape=[
            jax.ShapeDtypeStruct((2 * T, D), F32),
            jax.ShapeDtypeStruct((2 * T, D), BF16),
            jax.ShapeDtypeStruct((2 * T, ffh), F32),
            jax.ShapeDtypeStruct((half, D), BF16),
            jax.ShapeDtypeStruct((D, ffh), BF16),
        ],
        compiler_params=vmem(60),
        cost_estimate=TINY,
    )(at, *inputs, fc_b, *low, *low, *high, w_peer)


def contract_kernel(dims, at_ref, *refs):
    X, Y, Z, T, chunks, wd = dims
    cot_own_ref, cot_peer_ref, second_ref, pre_ref, fc_ref = refs[:5]
    refs = refs[5:]
    low_refs, high_refs, refs = refs[: X * Y], refs[X * Y : 2 * X * Y], refs[2 * X * Y :]
    own_ref, give_ref, back_ref, back_low_ref, dy_ref, fc_sum_ref = refs[:6]
    refs = refs[6:]
    grad_ref, flipped, proj, grad, acc = refs
    D = cot_own_ref.shape[1]
    tile = pre_ref.shape[1]
    fr = tile // (Y * DEPTH)
    zs = Z // DEPTH
    cut = fr // 2
    rows = grad_ref.shape[3] // 8
    f = pl.program_id(0)
    x_me, y_me, place = at_ref[0], at_ref[3], at_ref[4]

    @pl.when(f == 0)
    def _():
        for r, cot_ref in enumerate((cot_own_ref, cot_peer_ref)):
            pos = place * T + lax.broadcasted_iota(jnp.int32, (T, D), 0)
            dy_ref[r * T : (r + 1) * T, :] = jnp.where(pos < at_ref[5 + r], cot_ref[...], BF16(0.0))
        flipped[...] = second_ref[...].T

    for ky in range(Y):
        for kx in range(X):

            @pl.when(origin(kx, x_me, X) == f // zs)
            def _():
                for z in range(DEPTH):
                    start = (z * Y + origin(ky, y_me, Y)) * fr
                    proj[at_rows(start, cut), :] = low_refs[kx * Y + ky][z]
                    proj[at_rows(start + cut, cut), :] = high_refs[ky * X + kx][z]

    pre = pre_ref[...]
    d_act = dot_nt(dy_ref[...], proj[...])
    k0, k1 = 0.7978845608028654, 0.044715
    square = pre * pre
    tanh = jnp.tanh(k0 * (pre + k1 * (square * pre)))
    left = 0.5 * (1.0 + tanh)
    act = (pre * left).astype(BF16)
    slope = left + 0.5 * pre * (1.0 - tanh * tanh) * (k0 * (1.0 + 3.0 * k1 * square))
    d_pre = (slope * d_act).astype(BF16)
    fc_sum_ref[...] = jnp.sum(d_pre.astype(F32), axis=0, keepdims=True)
    part = dot_nn(act, proj[...])
    back = dot_nt(d_pre, fc_ref[...])
    tall = dot_tn(act, dy_ref[...]).astype(BF16)
    for z in range(DEPTH):
        for y in range(Y):
            start = (z * Y + y) * fr
            grad_ref[f // zs, y, lax.rem(f, zs) * DEPTH + z, 4 * rows :, :] = tall[start : start + fr, :]
    grad[...] = dot_nn(flipped[...], d_pre).astype(BF16)
    n, lane = (f * tile) // D, pl.multiple_of(lax.rem(f * tile, D), tile)
    for x in range(X):
        for c in range(2):
            for z in range(Z):
                for y in range(Y):
                    start = (((x * 2 + c) * Z + z) * Y + y) * rows
                    value = grad[start : start + rows, :]
                    grad_ref[x, y, z, at_rows((c * 2 + n) * rows, rows), pl.ds(lane, tile)] = value

    @pl.when(f == 0)
    def _():
        acc[...] = part
        back_ref[...] = back

    @pl.when(f > 0)
    def _():
        acc[...] += part
        back_ref[...] += back

    @pl.when(f == pl.num_programs(0) - 1)
    def _():
        own_ref[...] = acc[:T, :]
        give_ref[...] = acc[T:, :].astype(BF16)
        back_low_ref[:T, :] = back_ref[T:, :].astype(BF16)
        back_low_ref[T:, :] = back_ref[:T, :].astype(BF16)


def contract(dims, at, cot_own, cot_peer, second, pre, fc, low, high):
    X, Y, Z, T, chunks, wd = dims
    D, ffh = fc.shape
    steps = X * Z // DEPTH
    tile = ffh // steps
    cut = tile // (2 * Y * DEPTH)
    rows = D // (2 * X * Y * Z)

    def block(f, at):
        return (f % (Z // DEPTH), 1, 0)

    return pl.pallas_call(
        functools.partial(contract_kernel, dims),
        name="contract",
        grid_spec=pltpu.PrefetchScalarGridSpec(
            num_scalar_prefetch=1,
            grid=(steps,),
            in_specs=[full(v.shape) for v in (cot_own, cot_peer, second)]
            + [
                pl.BlockSpec((2 * T, tile), lambda f, at: (0, f)),
                pl.BlockSpec((D, tile), lambda f, at: (0, f)),
            ]
            + [pl.BlockSpec((DEPTH, cut, D), block)] * (2 * X * Y),
            out_specs=[
                full((T, D)), full((T, D)), full((2 * T, D)), full((2 * T, D)), full((2 * T, D)),
                pl.BlockSpec((1, tile), lambda f, at: (0, f)),
            ]
            + [full((X, Y, Z, 8 * rows, D))],
            scratch_shapes=[
                pltpu.VMEM((D, 2 * T), BF16),
                pltpu.VMEM((tile, D), BF16),
                pltpu.VMEM((D, tile), BF16),
                pltpu.VMEM((2 * T, D), F32),
            ],
        ),
        out_shape=[
            jax.ShapeDtypeStruct((T, D), F32),
            jax.ShapeDtypeStruct((T, D), BF16),
            jax.ShapeDtypeStruct((2 * T, D), F32),
            jax.ShapeDtypeStruct((2 * T, D), BF16),
            jax.ShapeDtypeStruct((2 * T, D), BF16),
            jax.ShapeDtypeStruct((1, ffh), F32),
        ]
        + [jax.ShapeDtypeStruct((X, Y, Z, 8 * rows, D), BF16)],
        compiler_params=vmem(60),
        cost_estimate=TINY,
    )(at, cot_own, cot_peer, second, pre, fc, *low, *high)


def middle_kernel(
    dims, back_ref, got_ref, resid_ref, dy_ref, gain_ref, w_ref, low_ref, wide_ref, msg_ref, sums_ref
):
    X, Y, Z, T, chunks, wd = dims
    b = pl.program_id(0)
    rows, D = back_ref.shape
    steps = T // rows
    normed, inverse = layer_stats(resid_ref[...])
    d_second = back_ref[...] + got_ref[...].astype(F32)
    dy = dy_ref[...].astype(F32)
    d_resid = dy + layer_back(d_second, normed, inverse, gain_ref[...])
    low = d_resid.astype(BF16)
    low_ref[...] = low
    wide_ref[...] = d_resid
    per = chunks // X
    start = pl.multiple_of(lax.rem(b, steps) * rows, rows)
    for x in range(X):
        out = dot_nt(low, w_ref[x * per * wd : (x + 1) * per * wd, :]).astype(BF16)
        for k in range(per):
            msg_ref[(b // steps) * chunks + x * per + k, pl.ds(start, rows), :] = out[:, k * wd : (k + 1) * wd]

    @pl.when(b == 0)
    def _():
        sums_ref[...] = jnp.zeros_like(sums_ref)

    @pl.when(b < steps)
    def _():
        for n, value in enumerate((d_resid, d_second * normed, d_second, dy)):
            sums_ref[n : n + 1, :] += jnp.sum(value, axis=0, keepdims=True)


def middle(dims, back, got, resid, dy, gain, w_own):
    X, Y, Z, T, chunks, wd = dims
    D = back.shape[1]
    block = min(128, T)
    row = pl.BlockSpec((block, D), lambda b: (b, 0))
    return pl.pallas_call(
        functools.partial(middle_kernel, dims),
        name="middle",
        grid=(2 * T // block,),
        in_specs=[row, row, row, row, full(gain.shape), full(w_own.shape)],
        out_specs=[row, row, full((2 * chunks, T, wd)), full((8, D))],
        out_shape=[
            jax.ShapeDtypeStruct((2 * T, D), BF16),
            jax.ShapeDtypeStruct((2 * T, D), F32),
            jax.ShapeDtypeStruct((2 * chunks, T, wd), BF16),
            jax.ShapeDtypeStruct((8, D), F32),
        ],
        compiler_params=vmem(60),
        cost_estimate=TINY,
    )(back, got, resid, dy, gain, w_own)


def project_back_kernel(
    dims, at_ref, d_ref, w_ref, first_ref, norm_ref, mine_ref, low_ref, own_ref, give_ref, sum_ref, sums_ref, *refs
):
    X, Y, Z, T, chunks, wd = dims
    a_refs, b_refs, (joint, block) = refs[:X], refs[X : X + Y], refs[X + Y :]
    g = pl.program_id(0)
    x, c = g // 2, pl.multiple_of(lax.rem(g, 2), 1)
    half = chunks * wd

    @pl.when(g == 0)
    def _():
        for r in range(2):
            for t in range(3):
                for h in range(chunks):
                    at = t * half + h * wd
                    joint[r * T : (r + 1) * T, at : at + wd] = d_ref[r * chunks + h, t]
        sum_ref[...] = jnp.sum(joint[...].astype(F32), axis=0, keepdims=True)

    part = dot_nt(joint[...], w_ref[...])
    own_ref[...] = part[:T, :]
    give_ref[...] = part[T:, :].astype(BF16)
    sums_ref[0:1, :] = jnp.sum(part * norm_ref[...].astype(F32), axis=0, keepdims=True)
    sums_ref[1:2, :] = jnp.sum(part, axis=0, keepdims=True)
    block[...] = dot_tn(first_ref[...], joint[...]).astype(BF16)
    rows = block.shape[0] // (Z * Y)
    for k in range(X):

        @pl.when(x == lax.rem(at_ref[0] + k, X))
        def _():
            a_refs[k][:, :, at_rows(c * rows, rows), :] = block[:, : 2 * half].reshape(Z, Y, rows, 2 * half)

    def spots(k):
        y = lax.rem(at_ref[3] + k, Y)
        return [(z, at_rows((z * Y + y) * rows, rows)) for z in range(Z)]

    for k in range(Y):
        for z, spot in spots(k):
            b_refs[k][x, z, :rows, at_rows(c * half, half)] = block[spot, 2 * half :]

    @pl.when(c == 0)
    def _():
        per = chunks // X
        left = [jnp.concatenate([mine_ref[r * chunks + x * per + j] for r in range(2)], axis=0) for j in range(per)]
        block[:, : 2 * half] = dot_tn(jnp.concatenate(left, axis=1), low_ref[...]).astype(BF16)
        for k in range(Y):
            for z, spot in spots(k):
                b_refs[k][x, z, rows:, :] = block[spot, : 2 * half]


def project_back(dims, at, d_msg, w, first, norm, mine, low):
    X, Y, Z, T, chunks, wd = dims
    D, cols = w.shape
    block = D // (2 * X)
    rows = block // (Z * Y)
    a_shape, b_shape = (Z, Y, 2 * rows, D), (X, Z, 2 * rows, D)
    return pl.pallas_call(
        functools.partial(project_back_kernel, dims),
        name="project_back",
        grid=(2 * X,),
        in_specs=[
            pl.BlockSpec(memory_space=pltpu.SMEM),
            full(d_msg.shape),
            pl.BlockSpec((block, cols), lambda g: (g, 0)),
            pl.BlockSpec((2 * T, block), lambda g: (0, g)),
            pl.BlockSpec((2 * T, block), lambda g: (0, g)),
            full(mine.shape), full(low.shape),
        ],
        out_specs=[
            pl.BlockSpec((T, block), lambda g: (0, g)),
            pl.BlockSpec((T, block), lambda g: (0, g)),
            full((1, cols)),
            pl.BlockSpec((8, block), lambda g: (0, g)),
        ]
        + [full(a_shape)] * X
        + [full(b_shape)] * Y,
        out_shape=[
            jax.ShapeDtypeStruct((T, D), F32),
            jax.ShapeDtypeStruct((T, D), BF16),
            jax.ShapeDtypeStruct((1, cols), F32),
            jax.ShapeDtypeStruct((8, D), F32),
        ]
        + [jax.ShapeDtypeStruct(a_shape, BF16)] * X
        + [jax.ShapeDtypeStruct(b_shape, BF16)] * Y,
        scratch_shapes=[pltpu.VMEM((2 * T, cols), BF16), pltpu.VMEM((block, cols), BF16)],
        compiler_params=vmem(60),
        cost_estimate=TINY,
    )(at, d_msg, w, first, norm, mine, low)


def combine_kernel(streams, at_ref, *refs):
    step, taken = pl.program_id(0), []
    for counts in streams:
        groups = []
        for count in counts:
            groups.append(refs[:count])
            refs = refs[count:]
        taken.append(groups)
    size = len(refs) // len(streams)
    for n, groups in enumerate(taken):
        for k, out_ref in enumerate(refs[n * size : (n + 1) * size]):

            @pl.when(step == k)
            def _():
                start = 0
                for group in groups:
                    total = group[0][...].astype(F32)
                    for ref in group[1:]:
                        total = total + ref[...].astype(F32)
                    total = total.reshape(out_ref.shape[:-2] + total.shape[-2:]).astype(out_ref.dtype)
                    out_ref[..., start : start + total.shape[-2], :] = total
                    start += total.shape[-2]


def combine(at, *streams, wide=False, cost=None):
    specs, outs, values, out_specs, counts = [], [], [], [], []
    size = streams[0][2][0][0].shape[streams[0][1]]
    for axis, dim, groups in streams:
        shape = groups[0][0].shape
        rest = tuple(n for d, n in enumerate(shape) if d != dim)
        out = rest[:-2] + (sum(g[0].shape[-2] for g in groups), rest[-1])

        def spec(shape, axis=axis, dim=dim):
            return pl.BlockSpec(
                tuple(1 if d == dim else n for d, n in enumerate(shape)),
                lambda k, at: tuple(lax.rem(at[axis] + k, size) if d == dim else 0 for d in range(len(shape))),
            )

        specs += [spec(v.shape) for g in groups for v in g]
        values += [v for g in groups for v in g]
        out_specs += [full(out)] * size
        outs += [jax.ShapeDtypeStruct(out, F32 if wide and k == 0 else BF16) for k in range(size)]
        counts.append(tuple(len(g) for g in groups))
    out = pl.pallas_call(
        functools.partial(combine_kernel, tuple(counts)),
        name="combine",
        grid_spec=pltpu.PrefetchScalarGridSpec(
            num_scalar_prefetch=1, grid=(size,), in_specs=specs, out_specs=out_specs
        ),
        out_shape=outs,
        compiler_params=vmem(16),
        cost_estimate=cost or TINY,
    )(at, *values)
    return [out[n * size : (n + 1) * size] for n in range(len(streams))]


def pick(array, index, dim):
    return lax.dynamic_index_in_dim(array, index, dim, keepdims=False)


def swap(array):
    return lax.ppermute(array, "c", SWAP)


def shift(array, axis, size, k):
    return lax.ppermute(array, axis, [(i, (i + k) % size) for i in range(size)])


def spread(array, axis, size):
    return jnp.stack([array] + [shift(array, axis, size, k) for k in range(1, size)])


def gather(array, first, first_size, second, second_size):
    base = [array] + [shift(array, first, first_size, k) for k in range(1, first_size)]
    return base + [shift(v, second, second_size, j) for j in range(1, second_size) for v in base]


def sent(parts, axis):
    return [parts[0]] + [shift(parts[k], axis, len(parts), k) for k in range(1, len(parts))]


def scatter_sum(array, axis, dim):
    size, me = array.shape[dim], lax.axis_index(axis)
    return sum(sent([pick(array, (me + k) % size, dim) for k in range(size)], axis))


def per_device(sizes, *args):
    (
        hidden, group_sizes, prefix_lens, sol_lens, ln1_gain, ln1_shift, qkv_weight, qv_bias, out_weight, out_bias,
        ln2_gain, ln2_shift, fc_weight, fc_bias, proj_weight, proj_bias, cotangent,
    ) = args
    X, Z, Y = sizes
    S, ND = Z * Y, 2 * X * Z * Y
    _, T, D = hidden.shape
    FF = fc_weight.shape[1]
    heads = D // HD // S
    wd, chunks = heads * HD, S // 2
    half, ffh = D // 2, FF // 2
    rows = D // ND
    dims = (X, Y, Z, T, chunks, wd)
    c, place = lax.axis_index("c"), lax.axis_index(SEQ)

    local = qkv_weight.reshape(rows, 3, X, 2, half // X)
    kept = pick(local, c, 3).reshape(rows, 3 * half)
    given = pick(local, 1 - c, 3).reshape(rows, 3 * half)
    piece = jnp.stack([kept, swap(given)])
    cut = 3 * half // 2
    piece_a, piece_b = spread(piece[..., :cut], "z", Z), spread(piece[..., cut:], "z", Z)

    local = fc_weight.reshape(rows, X, 2, ffh // X)
    kept, given = (pick(local, n, 2).reshape(rows, ffh) for n in (c, 1 - c))
    wide = [slice(n, n + D) for n in range(0, ffh, D)]
    got = swap(jnp.concatenate([given[:, n] for n in wide], axis=0))
    fr = FF // ND
    low = jnp.concatenate([kept[:, wide[0]], got[:rows], proj_weight[: fr // 2], out_weight], axis=0)
    high = jnp.concatenate([kept[:, wide[1]], got[rows:], proj_weight[fr // 2 :]], axis=0)
    low, high, piece_a, piece_b = lax.optimization_barrier((low, high, piece_a, piece_b))
    low, high = (lax.all_gather(v, "z", axis=0, tiled=False) for v in (low, high))
    pieces = gather(piece_a, "x", X, "y", Y) + gather(piece_b, "y", Y, "x", X)

    small = (ln1_gain, ln1_shift, qv_bias, out_bias, ln2_gain, ln2_shift, fc_bias, proj_bias)
    cuts = [0]
    for part in small:
        cuts.append(cuts[-1] + part.shape[0])
    packed = jnp.broadcast_to(jnp.concatenate(small)[None, :], (ND, cuts[-1]))
    packed = lax.all_to_all(packed, ALL, split_axis=0, concat_axis=0, tiled=True).astype(F32)
    gain1, shift1, qv_all, out_b, gain2, shift2, fc_b, proj_b = (
        packed[:, cuts[n] : cuts[n + 1]].reshape(1, -1) for n in range(8)
    )

    slot = jnp.arange(sol_lens.shape[1], dtype=jnp.int32)
    used = jnp.where(slot < group_sizes[0], sol_lens[0], 0)
    ends = prefix_lens[0] + jnp.sum(jnp.where(slot[None, :] <= slot[:, None], used[None, :], 0), axis=1)
    meta = jnp.concatenate([prefix_lens, ends, jnp.zeros((15,), jnp.int32)])
    meta_peer = swap(meta)
    meta_here = jnp.where(place < chunks, meta, meta_peer)
    where = [lax.axis_index("x"), c, lax.axis_index("z"), lax.axis_index("y"), place, meta[16], meta_peer[16]]
    at = jnp.stack(where).astype(jnp.int32)

    own, cot = hidden[0], cotangent[0]
    peer, cot_peer = swap(own), swap(cot)

    qv_here = pick(qv_all.reshape(2, X, 2, half // X), c, 2).reshape(2, half)
    bias = jnp.concatenate([qv_here[:1], jnp.zeros_like(qv_here[:1]), qv_here[1:]], axis=1)
    msg, w_qkv, first, norm = project(dims, at, own, peer, gain1, shift1, bias, pieces)

    def exchange(array):
        return lax.all_to_all(array, SEQ, split_axis=0, concat_axis=0, tiled=True)

    qkv = exchange(msg)
    low, high = gather(low, "y", Y, "x", X), gather(high, "x", X, "y", Y)
    att, att_wide, lse = attend(qkv, meta_here, heads)
    w_peer = swap(jnp.stack([v[:, fr:] for v in low]))
    mine = exchange(att)
    theirs = swap(mine)

    fc_b_here = pick(fc_b.reshape(X, 2, ffh // X), c, 1).reshape(1, ffh)
    resid, second, pre, w_own, w_fc = expand(
        dims, at, [own, peer, mine, theirs, out_b, gain2, shift2], fc_b_here, low, w_peer, high
    )
    out = contract(dims, at, cot, cot_peer, second, pre, w_fc, low, high)
    ahead, give, back, back_low, dy, fc_sum = out[:6]
    grads = lax.psum_scatter(out[6].reshape(X * Y, Z, -1, D), ("x", "y"), scatter_dimension=0, tiled=True)
    d_low, d_wide, d_msg, sums_mid = middle(dims, back, swap(back_low), resid, dy, gain2, w_own)
    up = exchange(d_msg)
    position = place * T + jnp.arange(T, dtype=jnp.int32)
    valid = (position < meta[16]).astype(F32)[:, None]
    layer_out = valid * (resid[:T] + (ahead + swap(give).astype(F32)) + proj_b)

    d_msg = attend_back(qkv, att_wide, lse, up, meta_here, heads)
    d_qkv = exchange(d_msg)
    out = list(project_back(dims, at, d_qkv, w_qkv, first, norm, mine, d_low))
    part, part_peer, qkv_sum, sums_first = out[:4]
    given = swap(part_peer)
    part_a, part_b = sent(out[4 : 4 + X], "x"), sent(out[4 + X :], "y")

    grads, _ = lax.optimization_barrier((grads, part))
    grads = lax.psum_scatter(grads[0], "z", scatter_dimension=0, tiled=True)[0].astype(F32)

    def both_halves(grad, blocks):
        kept = pick(grad, c, 0)
        got = swap(pick(grad, 1 - c, 0).astype(BF16)).astype(F32)
        shape = (kept.shape[0],) + blocks
        kept, got = kept.reshape(shape), got.reshape(shape)
        low = jnp.where(c == 0, kept, got)
        high = jnp.where(c == 0, got, kept)
        return jnp.stack([low, high], axis=-2).reshape(kept.shape[0], -1)

    fc_rows = 2 * ffh // D * rows
    fc_grad = grads[:fc_rows].reshape(2, ffh // D, rows, D).transpose(0, 2, 1, 3).reshape(2, rows, ffh)
    proj_grad = grads[fc_rows:]
    fc_grad = both_halves(fc_grad, (X, ffh // X))

    def own_columns(vector, lead):
        cut = vector.reshape(lead, X, 1, -1)
        spot = lax.broadcasted_iota(jnp.int32, (lead, X, 2, cut.shape[-1]), 2)
        return jnp.where(spot == c, cut, 0.0).reshape(-1)

    qv_sum = jnp.concatenate([qkv_sum[0, :half], qkv_sum[0, 2 * half :]])
    sums = (
        sums_first[0],
        sums_first[1],
        own_columns(qv_sum, 2),
        sums_mid[0],
        sums_mid[1],
        sums_mid[2],
        own_columns(fc_sum, 1),
        sums_mid[3],
    )
    packed = jnp.concatenate([v.reshape(ND, -1) for v in sums], axis=1).reshape(X, 2, Z, Y, -1)
    packed = scatter_sum(packed, "x", 0)

    part_a, part_b = combine(at, (3, 1, [part_a]), (0, 0, [part_b]))
    packed, *_ = lax.optimization_barrier((packed, *part_a, *part_b))
    part_a, part_b, packed = sent(part_a, "y"), sent(part_b, "x"), scatter_sum(packed, "y", 2)
    packed = scatter_sum(scatter_sum(packed, "c", 0), "z", 0)
    d_first = part + given.astype(F32)
    norm, inverse = layer_stats(own.astype(F32))
    hidden_grad = d_wide[:T] + layer_back(d_first, norm, inverse, gain1)
    hidden_grad, layer_out = hidden_grad.astype(BF16), layer_out.astype(BF16)
    hidden_grad, layer_out, packed, fc_grad, proj_grad, *ordered = lax.optimization_barrier(
        (hidden_grad, layer_out, packed, fc_grad, proj_grad, *part_a, *part_b)
    )
    last = combine(at, (2, 0, [ordered[:Y], ordered[Y:]]), wide=True)[0]
    last = sent(last, "z")
    last = sum(v.astype(F32) for v in last)
    value = last[2 * rows : 3 * rows].reshape(rows, 2, half).transpose(1, 0, 2)
    qkv_grad = jnp.concatenate([last[: 2 * rows].reshape(2, rows, D), value], axis=2)
    out_grad = last[3 * rows :]
    qkv_grad = both_halves(qkv_grad, (3, X, half // X))

    gain1_g, shift1_g, qv_g, out_b_g, gain2_g, shift2_g, fc_b_g, proj_b_g = (
        packed[cuts[n] : cuts[n + 1]] for n in range(8)
    )
    return (
        layer_out[None], hidden_grad[None], gain1_g, shift1_g, qkv_grad, qv_g, out_grad,
        out_b_g, gain2_g, shift2_g, fc_grad, fc_b_g, proj_grad, proj_b_g,
    )


def solution(mesh):
    Z = 4
    X, Y = mesh.shape["dp"] // 2, mesh.shape["seq"] // Z
    split = Mesh(mesh.devices.reshape(X, 2, Z, Y), ALL)
    group, wide, flat = P(("x", "c"), SEQ, None), P(ALL, None), P(ALL)
    dp = P(("x", "c"))
    return jax.shard_map(
        functools.partial(per_device, (X, Z, Y)),
        mesh=split,
        in_specs=(
            group, dp, dp, P(("x", "c"), None), flat, flat, wide, flat, wide, flat, flat, flat, wide, flat, wide, flat,
            group,
        ),
        out_specs=(
            group, group, flat, flat, wide, flat, wide, flat, flat, flat, wide, flat, wide, flat,
        ),
        check_vma=False,
    )
```

```python
import functools

import jax
import jax.numpy as jnp
from jax import lax
from jax.experimental import pallas as pl
from jax.experimental.pallas import tpu as pltpu
from jax.sharding import Mesh
from jax.sharding import PartitionSpec as P

HD = 64
EPSILON = 1e-05
BIG = 1e30
BLOCK = 256
DEPTH = 2
F32 = jnp.float32
LONG = pl.CostEstimate(flops=10**11, bytes_accessed=1, transcendentals=0)
TINY = pl.CostEstimate(flops=1, bytes_accessed=1, transcendentals=0)
BF16 = jnp.bfloat16
ALL = ("x", "c", "z", "y")
SEQ = ("z", "y")
SWAP = [(0, 1), (1, 0)]


def dot_nt(a, b):
    return lax.dot_general(a, b, (((1,), (1,)), ((), ())), preferred_element_type=F32)


def dot_nn(a, b):
    return lax.dot_general(a, b, (((1,), (0,)), ((), ())), preferred_element_type=F32)


def dot_tn(a, b):
    return lax.dot_general(a, b, (((0,), (0,)), ((), ())), preferred_element_type=F32)


def segment_code(ends_ref, start, rows, lanes):
    pos = start + lax.broadcasted_iota(jnp.int32, (rows, lanes), 0)
    passed = jnp.ones((rows, lanes), jnp.int32)
    for t in range(16):
        passed = passed + jnp.where(pos >= ends_ref[1 + t], 1, 0)
    code = jnp.where(pos < ends_ref[16], passed, 17)
    return jnp.where(pos < ends_ref[0], 0, code)


def with_segments(keys, ends_ref, start):
    rows, lanes = keys.shape
    code = segment_code(ends_ref, start, rows, lanes)
    lane = lax.broadcasted_iota(jnp.int32, (rows, lanes), 1)
    key_mark = jnp.where((code == lane) & (code > 0), 1.0, 0.0).astype(BF16)
    query_mark = jnp.where(code == lane, 0.0, -BIG).astype(BF16)
    return jnp.concatenate([keys, key_mark], axis=1), query_mark


def head_part(array, head, heads):
    if heads == 1:
        return array
    lane = lax.broadcasted_iota(jnp.int32, array.shape, 1)
    return jnp.where((lane >= head * HD) & (lane < (head + 1) * HD), array, jnp.zeros_like(array))


def causal(rows, cols, transposed):
    row = lax.broadcasted_iota(jnp.int32, (rows, cols), 0)
    col = lax.broadcasted_iota(jnp.int32, (rows, cols), 1)
    return (row <= col) if transposed else (col <= row)


def attend_kernel(heads, ends_ref, qkv_ref, out_ref, wide_ref, lse_ref, keys, values):
    i = pl.program_id(0)
    width = heads * HD
    start = pl.multiple_of(i * BLOCK, BLOCK)
    query_in, keys_in, values_in = (qkv_ref[:, t].reshape(BLOCK, width) for t in range(3))
    tagged, query_mark = with_segments(keys_in, ends_ref, start)
    keys[pl.ds(start, BLOCK), :] = tagged
    values[pl.ds(start, BLOCK), :] = values_in
    scaled = query_in * BF16(HD**-0.5)
    for n in range(keys.shape[0] // BLOCK):

        @pl.when(i == n)
        def _():
            before = n * BLOCK

            def one_head(h, wide):
                query = jnp.concatenate([head_part(scaled, h, heads), query_mark], axis=1)
                score = jnp.where(causal(BLOCK, BLOCK, False), dot_nt(query, tagged), -BIG)
                top = jnp.max(score, axis=1, keepdims=True)
                if n:
                    wide_score = dot_nt(query, keys[:before, :])
                    top = jnp.maximum(top, jnp.max(wide_score, axis=1, keepdims=True))
                expo = jnp.exp(score - top)
                total = jnp.sum(expo, axis=1, keepdims=True)
                acc = dot_nn(expo.astype(BF16), values_in)
                if n:
                    expo = jnp.exp(wide_score - top)
                    total = total + jnp.sum(expo, axis=1, keepdims=True)
                    acc = acc + dot_nn(expo.astype(BF16), values[:before, :])
                lse = jnp.broadcast_to(top + jnp.log(total), (BLOCK, 128))
                lse_ref[pl.ds(h, 1), :] = lse.T[0:1, :]
                return head_part(acc / total, h, heads) + wide

            wide_ref[...] = lax.fori_loop(0, heads, one_head, jnp.zeros((BLOCK, width), F32))

    out_ref[...] = wide_ref[...].astype(BF16).reshape(out_ref.shape)


def attend(qkv, ends, heads):
    length, width = qkv.shape[0] * qkv.shape[2], heads * HD
    T = qkv.shape[2]
    per = BLOCK // T
    return pl.pallas_call(
        functools.partial(attend_kernel, heads),
        name="attend",
        grid=(length // BLOCK,),
        in_specs=[
            pl.BlockSpec(memory_space=pltpu.SMEM),
            pl.BlockSpec((per, 3, T, width), lambda i: (i, 0, 0, 0)),
        ],
        out_specs=[
            pl.BlockSpec((per, T, width), lambda i: (i, 0, 0)),
            pl.BlockSpec((BLOCK, width), lambda i: (i, 0)),
            pl.BlockSpec((8, BLOCK), lambda i: (0, i)),
        ],
        out_shape=[
            jax.ShapeDtypeStruct((length // T, T, width), BF16),
            jax.ShapeDtypeStruct((length, width), F32),
            jax.ShapeDtypeStruct((8, length), F32),
        ],
        scratch_shapes=[
            pltpu.VMEM((length, 2 * width), BF16),
            pltpu.VMEM((length, width), BF16),
        ],
        compiler_params=pltpu.CompilerParams(vmem_limit_bytes=32 << 20),
        cost_estimate=TINY,
    )(ends, qkv)


def attend_back_kernel(
    heads, ends_ref, qkv_ref, wide_ref, lse_ref, up_ref, out_ref, keys, values, key_acc, value_acc, query_acc, inner_all
):
    i = pl.program_id(0)
    width = heads * HD
    start = pl.multiple_of(i * BLOCK, BLOCK)
    query_in, keys_in, values_in = (qkv_ref[:, t].reshape(BLOCK, width) for t in range(3))
    tagged, query_mark = with_segments(keys_in, ends_ref, start)
    keys[pl.ds(start, BLOCK), :] = tagged
    values[pl.ds(start, BLOCK), :] = values_in
    key_acc[pl.ds(start, BLOCK), :] = jnp.zeros((BLOCK, width), F32)
    value_acc[pl.ds(start, BLOCK), :] = jnp.zeros((BLOCK, width), F32)
    scaled = query_in * BF16(HD**-0.5)
    up = up_ref[...].reshape(BLOCK, width)
    inner_all[...] = (up.astype(F32) * wide_ref[...]).T
    query_acc[...] = jnp.zeros((BLOCK, width), F32)

    def step(h, first, rows, diagonal):
        spot = slice(first, first + rows)
        block, value = keys[spot, :], values[spot, :]
        part, up_part = head_part(scaled, h, heads), head_part(up, h, heads)
        score = dot_nt(block, jnp.concatenate([part, query_mark], axis=1))
        if diagonal:
            score = jnp.where(causal(BLOCK, BLOCK, True), score, -BIG)
        inner = jnp.sum(inner_all[pl.ds(pl.multiple_of(h * HD, HD), HD), :], axis=0, keepdims=True)
        prob = jnp.exp(score - lse_ref[pl.ds(h, 1), :])
        d_prob = dot_nt(value, up_part)
        d_score = (prob * (d_prob - inner)).astype(BF16)
        value_acc[spot, :] += dot_nn(prob.astype(BF16), up_part)
        key_acc[spot, :] += dot_nn(d_score, part)
        query_acc[...] += head_part(dot_tn(d_score, block[:, :width]), h, heads)

    for n in range(keys.shape[0] // BLOCK):

        @pl.when(i == n)
        def _():
            def one_head(h, carry):
                step(h, n * BLOCK, BLOCK, True)
                if n:
                    step(h, 0, n * BLOCK, False)
                return carry

            lax.fori_loop(0, heads, one_head, 0)

    d_query = query_acc[...] * HD**-0.5
    T = out_ref.shape[2]
    per = BLOCK // T
    out_ref[pl.ds(i * per, per), 0] = d_query.astype(BF16).reshape(per, T, width)

    @pl.when(i == pl.num_programs(0) - 1)
    def _():
        for s in range(out_ref.shape[0]):
            out_ref[s, 1] = key_acc[s * T : (s + 1) * T, :].astype(BF16)
            out_ref[s, 2] = value_acc[s * T : (s + 1) * T, :].astype(BF16)


def attend_back(qkv, wide, lse, up, ends, heads):
    length, width = qkv.shape[0] * qkv.shape[2], heads * HD
    T = qkv.shape[2]
    per = BLOCK // T
    return pl.pallas_call(
        functools.partial(attend_back_kernel, heads),
        name="attend_back",
        grid=(length // BLOCK,),
        in_specs=[
            pl.BlockSpec(memory_space=pltpu.SMEM),
            pl.BlockSpec((per, 3, T, width), lambda i: (i, 0, 0, 0)),
            pl.BlockSpec((BLOCK, width), lambda i: (i, 0)),
            pl.BlockSpec((8, BLOCK), lambda i: (0, i)),
            pl.BlockSpec((per, T, width), lambda i: (i, 0, 0)),
        ],
        out_specs=pl.BlockSpec((length // T, 3, T, width), lambda i: (0, 0, 0, 0)),
        out_shape=jax.ShapeDtypeStruct((length // T, 3, T, width), BF16),
        scratch_shapes=[
            pltpu.VMEM((length, 2 * width), BF16),
            pltpu.VMEM((length, width), BF16),
            pltpu.VMEM((length, width), F32),
            pltpu.VMEM((length, width), F32),
            pltpu.VMEM((BLOCK, width), F32),
            pltpu.VMEM((width, BLOCK), F32),
        ],
        compiler_params=pltpu.CompilerParams(vmem_limit_bytes=32 << 20),
        cost_estimate=TINY,
    )(ends, qkv, wide, lse, up)


def layer_stats(rows):
    centred = rows - jnp.mean(rows, axis=-1, keepdims=True)
    inverse = lax.rsqrt(jnp.mean(centred * centred, axis=-1, keepdims=True) + EPSILON)
    return centred * inverse, inverse


def layer_back(upstream, normed, inverse, gain):
    scaled = upstream * gain
    return inverse * (
        scaled
        - jnp.mean(scaled, axis=-1, keepdims=True)
        - normed * jnp.mean(scaled * normed, axis=-1, keepdims=True)
    )


def full(shape):
    return pl.BlockSpec(shape, lambda *_: (0,) * len(shape))


def vmem(mib):
    return pltpu.CompilerParams(vmem_limit_bytes=mib << 20)


def origin(k, me, size):
    return lax.rem(me - k + size, size)


def at_rows(start, rows):
    return pl.ds(pl.multiple_of(start, rows), rows)


def project_kernel(dims, at_ref, own_ref, peer_ref, gain_ref, shift_ref, bias_ref, *refs):
    X, Y, Z, T, chunks, wd = dims
    a_refs, b_refs, refs = refs[: X * Y], refs[X * Y : 2 * X * Y], refs[2 * X * Y :]
    msg_ref, w_out_ref, first_ref, norm_ref, w_ref = refs
    rows, part = a_refs[0].shape[-2:]
    width = w_ref.shape[1] // (3 * X)

    @pl.when((pl.program_id(0) == 0) & (pl.program_id(1) == 0))
    def _():
        x_me, c_me, z_me, y_me = (at_ref[n] for n in range(4))
        for kx in range(X):
            for ky in range(Y):
                x, y = origin(kx, x_me, X), origin(ky, y_me, Y)
                for kz in range(Z):
                    z = origin(kz, z_me, Z)
                    for kc in range(2):
                        c = lax.rem(c_me + kc, 2)
                        spot = at_rows((((x * 2 + c) * Z + z) * Y + y) * rows, rows)
                        w_ref[spot, :part] = a_refs[ky * X + kx][kz, kc]
                        w_ref[spot, part:] = b_refs[kx * Y + ky][kz, kc]
        for r, ref in enumerate((own_ref, peer_ref)):
            normed, _ = layer_stats(ref[...].astype(F32))
            norm_ref[r * T : (r + 1) * T, :] = normed.astype(BF16)
            first_ref[r * T : (r + 1) * T, :] = (normed * gain_ref[...] + shift_ref[...]).astype(BF16)

    t, x = pl.program_id(0), pl.program_id(1)
    col = pl.multiple_of((t * X + x) * width, width)
    w = w_ref[:, pl.ds(col, width)]
    w_out_ref[...] = w
    out = dot_nn(first_ref[...], w) + bias_ref[:, pl.ds(col, width)]
    out = out.astype(BF16)
    per = width // wd
    for r in range(2):
        for k in range(per):
            msg_ref[r * chunks + x * per + k, 0] = out[r * T : (r + 1) * T, k * wd : (k + 1) * wd]


def project(dims, at, own, peer, gain, shift, bias, pieces):
    X, Y, Z, T, chunks, wd = dims
    D = own.shape[1]
    cols = 2 * pieces[0].shape[-1]
    return pl.pallas_call(
        functools.partial(project_kernel, dims),
        name="project",
        grid=(3, X),
        in_specs=[pl.BlockSpec(memory_space=pltpu.SMEM)]
        + [full(v.shape) for v in (own, peer, gain, shift, bias, *pieces)],
        out_specs=[
            pl.BlockSpec((2 * chunks, 1, T, wd), lambda t, x: (0, t, 0, 0)),
            pl.BlockSpec((D, cols // (3 * X)), lambda t, x: (0, t * X + x)),
            full((2 * T, D)), full((2 * T, D)),
        ],
        scratch_shapes=[pltpu.VMEM((D, cols), BF16)],
        out_shape=[
            jax.ShapeDtypeStruct((2 * chunks, 3, T, wd), BF16),
            jax.ShapeDtypeStruct((D, cols), BF16),
            jax.ShapeDtypeStruct((2 * T, D), BF16),
            jax.ShapeDtypeStruct((2 * T, D), BF16),
        ],
        compiler_params=vmem(60),
        cost_estimate=TINY,
    )(at, own, peer, gain, shift, bias, *pieces)


def expand_kernel(dims, at_ref, *refs):
    X, Y, Z, T, chunks, wd = dims
    own_ref, peer_ref, mine_ref, theirs_ref, out_b_ref, gain_ref, shift_ref, fc_b_ref = refs[:8]
    refs = refs[8:]
    n = X * Y
    own_w_refs, low_refs, high_refs, refs = refs[:n], refs[n : 2 * n], refs[2 * n : 3 * n], refs[3 * n :]
    peer_w_ref, resid_ref, second_ref, pre_ref, w_own_ref, fc_ref, w_peer = refs
    D = own_ref.shape[1]
    rows = own_w_refs[0].shape[1]
    f = pl.program_id(0)
    x_me, c_me, y_me = (at_ref[n] for n in (0, 1, 3))

    @pl.when(f == 0)
    def _():
        for kx in range(X):
            for ky in range(Y):
                for kz in range(Z):
                    x, y, z = origin(kx, x_me, X), origin(ky, y_me, Y), kz
                    spot = at_rows(((x * Z + z) * Y + y) * rows, rows)
                    w_own_ref[spot, :] = own_w_refs[kx * Y + ky][kz]
                    w_peer[spot, :] = peer_w_ref[kx * Y + ky, kz]
        per = chunks // X
        width = per * wd
        for r, x_ref in enumerate((own_ref, peer_ref)):
            resid = x_ref[...].astype(F32) + out_b_ref[...]
            for source, base, w in ((mine_ref, r, w_own_ref), (theirs_ref, 1 - r, w_peer)):
                for x in range(X):
                    parts = [source[base * chunks + x * per + k] for k in range(per)]
                    resid = resid + dot_nn(jnp.concatenate(parts, axis=1), w[x * width : (x + 1) * width, :])
            part = slice(r * T, (r + 1) * T)
            resid_ref[part, :] = resid
            normed, _ = layer_stats(resid)
            second_ref[part, :] = (normed * gain_ref[...] + shift_ref[...]).astype(BF16)

    def place(block, kx, ky, kz):
        x, y, z = origin(kx, x_me, X), origin(ky, y_me, Y), kz
        for kc in range(2):
            c = lax.rem(c_me + kc, 2)
            fc_ref[at_rows((((x * 2 + c) * Z + z) * Y + y) * rows, rows), :] = block[kc * rows : (kc + 1) * rows, :]

    steps = pl.num_programs(0)

    @pl.when(f * 2 < steps)
    def _():
        for kx in range(X):
            for ky in range(Y):
                for kz in range(Z):
                    place(low_refs[kx * Y + ky][kz], kx, ky, kz)

    @pl.when(f * 2 >= steps)
    def _():
        for kx in range(X):
            for ky in range(Y):
                for kz in range(Z):
                    place(high_refs[ky * X + kx][kz], kx, ky, kz)

    pre_ref[...] = dot_nn(second_ref[...], fc_ref[...]) + fc_b_ref[...]


def expand(dims, at, inputs, fc_b, low, w_peer, high):
    X, Y, Z, T, chunks, wd = dims
    D = inputs[0].shape[1]
    half, ffh = D // 2, fc_b.shape[1]
    rows = half // (X * Y * Z)
    steps = X * Z // DEPTH
    tile, per = ffh // steps, steps // 2
    return pl.pallas_call(
        functools.partial(expand_kernel, dims),
        name="expand",
        grid_spec=pltpu.PrefetchScalarGridSpec(
            num_scalar_prefetch=1,
            grid=(steps,),
            in_specs=[full(v.shape) for v in inputs]
            + [pl.BlockSpec((1, tile), lambda f, at: (0, f))]
            + [pl.BlockSpec((Z, rows, D), lambda f, at: (0, 4, 0))] * (X * Y)
            + [pl.BlockSpec((Z, 2 * rows, tile), lambda f, at: (0, 0, jnp.minimum(f, per - 1)))] * (X * Y)
            + [pl.BlockSpec((Z, 2 * rows, tile), lambda f, at: (0, 0, jnp.maximum(f - per, 0)))] * (X * Y)
            + [full(w_peer.shape)],
            out_specs=[
                full((2 * T, D)), full((2 * T, D)),
                pl.BlockSpec((2 * T, tile), lambda f, at: (0, f)),
                full((half, D)),
                pl.BlockSpec((D, tile), lambda f, at: (0, f)),
            ],
            scratch_shapes=[pltpu.VMEM((half, D), BF16)],
        ),
        out_shape=[
            jax.ShapeDtypeStruct((2 * T, D), F32),
            jax.ShapeDtypeStruct((2 * T, D), BF16),
            jax.ShapeDtypeStruct((2 * T, ffh), F32),
            jax.ShapeDtypeStruct((half, D), BF16),
            jax.ShapeDtypeStruct((D, ffh), BF16),
        ],
        compiler_params=vmem(60),
        cost_estimate=TINY,
    )(at, *inputs, fc_b, *low, *low, *high, w_peer)


def contract_kernel(dims, at_ref, *refs):
    X, Y, Z, T, chunks, wd = dims
    cot_own_ref, cot_peer_ref, second_ref, pre_ref, fc_ref = refs[:5]
    refs = refs[5:]
    low_refs, high_refs, refs = refs[: X * Y], refs[X * Y : 2 * X * Y], refs[2 * X * Y :]
    own_ref, give_ref, back_ref, back_low_ref, dy_ref, fc_sum_ref = refs[:6]
    refs = refs[6:]
    grad_ref, flipped, proj, grad, acc = refs
    D = cot_own_ref.shape[1]
    tile = pre_ref.shape[1]
    fr = tile // (Y * DEPTH)
    zs = Z // DEPTH
    cut = fr // 2
    rows = grad_ref.shape[3] // 8
    f = pl.program_id(0)
    x_me, y_me, place = at_ref[0], at_ref[3], at_ref[4]

    @pl.when(f == 0)
    def _():
        for r, cot_ref in enumerate((cot_own_ref, cot_peer_ref)):
            pos = place * T + lax.broadcasted_iota(jnp.int32, (T, D), 0)
            dy_ref[r * T : (r + 1) * T, :] = jnp.where(pos < at_ref[5 + r], cot_ref[...], BF16(0.0))
        flipped[...] = second_ref[...].T

    for ky in range(Y):
        for kx in range(X):

            @pl.when(origin(kx, x_me, X) == f // zs)
            def _():
                for z in range(DEPTH):
                    start = (z * Y + origin(ky, y_me, Y)) * fr
                    proj[at_rows(start, cut), :] = low_refs[kx * Y + ky][z]
                    proj[at_rows(start + cut, cut), :] = high_refs[ky * X + kx][z]

    pre = pre_ref[...]
    d_act = dot_nt(dy_ref[...], proj[...])
    k0, k1 = 0.7978845608028654, 0.044715
    square = pre * pre
    tanh = jnp.tanh(k0 * (pre + k1 * (square * pre)))
    left = 0.5 * (1.0 + tanh)
    act = (pre * left).astype(BF16)
    slope = left + 0.5 * pre * (1.0 - tanh * tanh) * (k0 * (1.0 + 3.0 * k1 * square))
    d_pre = (slope * d_act).astype(BF16)
    fc_sum_ref[...] = jnp.sum(d_pre.astype(F32), axis=0, keepdims=True)
    part = dot_nn(act, proj[...])
    back = dot_nt(d_pre, fc_ref[...])
    tall = dot_tn(act, dy_ref[...]).astype(BF16)
    for z in range(DEPTH):
        for y in range(Y):
            start = (z * Y + y) * fr
            grad_ref[f // zs, y, lax.rem(f, zs) * DEPTH + z, 4 * rows :, :] = tall[start : start + fr, :]
    grad[...] = dot_nn(flipped[...], d_pre).astype(BF16)
    n, lane = (f * tile) // D, pl.multiple_of(lax.rem(f * tile, D), tile)
    for x in range(X):
        for c in range(2):
            for z in range(Z):
                for y in range(Y):
                    start = (((x * 2 + c) * Z + z) * Y + y) * rows
                    value = grad[start : start + rows, :]
                    grad_ref[x, y, z, at_rows((c * 2 + n) * rows, rows), pl.ds(lane, tile)] = value

    @pl.when(f == 0)
    def _():
        acc[...] = part
        back_ref[...] = back

    @pl.when(f > 0)
    def _():
        acc[...] += part
        back_ref[...] += back

    @pl.when(f == pl.num_programs(0) - 1)
    def _():
        own_ref[...] = acc[:T, :]
        give_ref[...] = acc[T:, :].astype(BF16)
        back_low_ref[:T, :] = back_ref[T:, :].astype(BF16)
        back_low_ref[T:, :] = back_ref[:T, :].astype(BF16)


def contract(dims, at, cot_own, cot_peer, second, pre, fc, low, high):
    X, Y, Z, T, chunks, wd = dims
    D, ffh = fc.shape
    steps = X * Z // DEPTH
    tile = ffh // steps
    cut = tile // (2 * Y * DEPTH)
    rows = D // (2 * X * Y * Z)

    def block(f, at):
        return (f % (Z // DEPTH), 1, 0)

    return pl.pallas_call(
        functools.partial(contract_kernel, dims),
        name="contract",
        grid_spec=pltpu.PrefetchScalarGridSpec(
            num_scalar_prefetch=1,
            grid=(steps,),
            in_specs=[full(v.shape) for v in (cot_own, cot_peer, second)]
            + [
                pl.BlockSpec((2 * T, tile), lambda f, at: (0, f)),
                pl.BlockSpec((D, tile), lambda f, at: (0, f)),
            ]
            + [pl.BlockSpec((DEPTH, cut, D), block)] * (2 * X * Y),
            out_specs=[
                full((T, D)), full((T, D)), full((2 * T, D)), full((2 * T, D)), full((2 * T, D)),
                pl.BlockSpec((1, tile), lambda f, at: (0, f)),
            ]
            + [full((X, Y, Z, 8 * rows, D))],
            scratch_shapes=[
                pltpu.VMEM((D, 2 * T), BF16),
                pltpu.VMEM((tile, D), BF16),
                pltpu.VMEM((D, tile), BF16),
                pltpu.VMEM((2 * T, D), F32),
            ],
        ),
        out_shape=[
            jax.ShapeDtypeStruct((T, D), F32),
            jax.ShapeDtypeStruct((T, D), BF16),
            jax.ShapeDtypeStruct((2 * T, D), F32),
            jax.ShapeDtypeStruct((2 * T, D), BF16),
            jax.ShapeDtypeStruct((2 * T, D), BF16),
            jax.ShapeDtypeStruct((1, ffh), F32),
        ]
        + [jax.ShapeDtypeStruct((X, Y, Z, 8 * rows, D), BF16)],
        compiler_params=vmem(60),
        cost_estimate=TINY,
    )(at, cot_own, cot_peer, second, pre, fc, *low, *high)


def middle_kernel(
    dims, back_ref, got_ref, resid_ref, dy_ref, gain_ref, w_ref, low_ref, wide_ref, msg_ref, sums_ref
):
    X, Y, Z, T, chunks, wd = dims
    b = pl.program_id(0)
    rows, D = back_ref.shape
    steps = T // rows
    normed, inverse = layer_stats(resid_ref[...])
    d_second = back_ref[...] + got_ref[...].astype(F32)
    dy = dy_ref[...].astype(F32)
    d_resid = dy + layer_back(d_second, normed, inverse, gain_ref[...])
    low = d_resid.astype(BF16)
    low_ref[...] = low
    wide_ref[...] = d_resid
    per = chunks // X
    start = pl.multiple_of(lax.rem(b, steps) * rows, rows)
    for x in range(X):
        out = dot_nt(low, w_ref[x * per * wd : (x + 1) * per * wd, :]).astype(BF16)
        for k in range(per):
            msg_ref[(b // steps) * chunks + x * per + k, pl.ds(start, rows), :] = out[:, k * wd : (k + 1) * wd]

    @pl.when(b == 0)
    def _():
        sums_ref[...] = jnp.zeros_like(sums_ref)

    @pl.when(b < steps)
    def _():
        for n, value in enumerate((d_resid, d_second * normed, d_second, dy)):
            sums_ref[n : n + 1, :] += jnp.sum(value, axis=0, keepdims=True)


def middle(dims, back, got, resid, dy, gain, w_own):
    X, Y, Z, T, chunks, wd = dims
    D = back.shape[1]
    block = min(128, T)
    row = pl.BlockSpec((block, D), lambda b: (b, 0))
    return pl.pallas_call(
        functools.partial(middle_kernel, dims),
        name="middle",
        grid=(2 * T // block,),
        in_specs=[row, row, row, row, full(gain.shape), full(w_own.shape)],
        out_specs=[row, row, full((2 * chunks, T, wd)), full((8, D))],
        out_shape=[
            jax.ShapeDtypeStruct((2 * T, D), BF16),
            jax.ShapeDtypeStruct((2 * T, D), F32),
            jax.ShapeDtypeStruct((2 * chunks, T, wd), BF16),
            jax.ShapeDtypeStruct((8, D), F32),
        ],
        compiler_params=vmem(60),
        cost_estimate=TINY,
    )(back, got, resid, dy, gain, w_own)


def project_back_kernel(
    dims, at_ref, d_ref, w_ref, first_ref, norm_ref, mine_ref, low_ref, own_ref, give_ref, sum_ref, sums_ref, *refs
):
    X, Y, Z, T, chunks, wd = dims
    a_refs, b_refs, (joint, block) = refs[:X], refs[X : X + Y], refs[X + Y :]
    g = pl.program_id(0)
    x, c = g // 2, pl.multiple_of(lax.rem(g, 2), 1)
    half = chunks * wd

    @pl.when(g == 0)
    def _():
        for r in range(2):
            for t in range(3):
                for h in range(chunks):
                    at = t * half + h * wd
                    joint[r * T : (r + 1) * T, at : at + wd] = d_ref[r * chunks + h, t]
        sum_ref[...] = jnp.sum(joint[...].astype(F32), axis=0, keepdims=True)

    part = dot_nt(joint[...], w_ref[...])
    own_ref[...] = part[:T, :]
    give_ref[...] = part[T:, :].astype(BF16)
    sums_ref[0:1, :] = jnp.sum(part * norm_ref[...].astype(F32), axis=0, keepdims=True)
    sums_ref[1:2, :] = jnp.sum(part, axis=0, keepdims=True)
    block[...] = dot_tn(first_ref[...], joint[...]).astype(BF16)
    rows = block.shape[0] // (Z * Y)
    for k in range(X):

        @pl.when(x == lax.rem(at_ref[0] + k, X))
        def _():
            a_refs[k][:, :, at_rows(c * rows, rows), :] = block[:, : 2 * half].reshape(Z, Y, rows, 2 * half)

    def spots(k):
        y = lax.rem(at_ref[3] + k, Y)
        return [(z, at_rows((z * Y + y) * rows, rows)) for z in range(Z)]

    for k in range(Y):
        for z, spot in spots(k):
            b_refs[k][x, z, :rows, at_rows(c * half, half)] = block[spot, 2 * half :]

    @pl.when(c == 0)
    def _():
        per = chunks // X
        left = [jnp.concatenate([mine_ref[r * chunks + x * per + j] for r in range(2)], axis=0) for j in range(per)]
        block[:, : 2 * half] = dot_tn(jnp.concatenate(left, axis=1), low_ref[...]).astype(BF16)
        for k in range(Y):
            for z, spot in spots(k):
                b_refs[k][x, z, rows:, :] = block[spot, : 2 * half]


def project_back(dims, at, d_msg, w, first, norm, mine, low):
    X, Y, Z, T, chunks, wd = dims
    D, cols = w.shape
    block = D // (2 * X)
    rows = block // (Z * Y)
    a_shape, b_shape = (Z, Y, 2 * rows, D), (X, Z, 2 * rows, D)
    return pl.pallas_call(
        functools.partial(project_back_kernel, dims),
        name="project_back",
        grid=(2 * X,),
        in_specs=[
            pl.BlockSpec(memory_space=pltpu.SMEM),
            full(d_msg.shape),
            pl.BlockSpec((block, cols), lambda g: (g, 0)),
            pl.BlockSpec((2 * T, block), lambda g: (0, g)),
            pl.BlockSpec((2 * T, block), lambda g: (0, g)),
            full(mine.shape), full(low.shape),
        ],
        out_specs=[
            pl.BlockSpec((T, block), lambda g: (0, g)),
            pl.BlockSpec((T, block), lambda g: (0, g)),
            full((1, cols)),
            pl.BlockSpec((8, block), lambda g: (0, g)),
        ]
        + [full(a_shape)] * X
        + [full(b_shape)] * Y,
        out_shape=[
            jax.ShapeDtypeStruct((T, D), F32),
            jax.ShapeDtypeStruct((T, D), BF16),
            jax.ShapeDtypeStruct((1, cols), F32),
            jax.ShapeDtypeStruct((8, D), F32),
        ]
        + [jax.ShapeDtypeStruct(a_shape, BF16)] * X
        + [jax.ShapeDtypeStruct(b_shape, BF16)] * Y,
        scratch_shapes=[pltpu.VMEM((2 * T, cols), BF16), pltpu.VMEM((block, cols), BF16)],
        compiler_params=vmem(60),
        cost_estimate=TINY,
    )(at, d_msg, w, first, norm, mine, low)


def combine_kernel(streams, at_ref, *refs):
    step, taken = pl.program_id(0), []
    for counts in streams:
        groups = []
        for count in counts:
            groups.append(refs[:count])
            refs = refs[count:]
        taken.append(groups)
    size = len(refs) // len(streams)
    for n, groups in enumerate(taken):
        for k, out_ref in enumerate(refs[n * size : (n + 1) * size]):

            @pl.when(step == k)
            def _():
                start = 0
                for group in groups:
                    total = group[0][...].astype(F32)
                    for ref in group[1:]:
                        total = total + ref[...].astype(F32)
                    total = total.reshape(out_ref.shape[:-2] + total.shape[-2:]).astype(out_ref.dtype)
                    out_ref[..., start : start + total.shape[-2], :] = total
                    start += total.shape[-2]


def combine(at, *streams, wide=False, cost=None):
    specs, outs, values, out_specs, counts = [], [], [], [], []
    size = streams[0][2][0][0].shape[streams[0][1]]
    for axis, dim, groups in streams:
        shape = groups[0][0].shape
        rest = tuple(n for d, n in enumerate(shape) if d != dim)
        out = rest[:-2] + (sum(g[0].shape[-2] for g in groups), rest[-1])

        def spec(shape, axis=axis, dim=dim):
            return pl.BlockSpec(
                tuple(1 if d == dim else n for d, n in enumerate(shape)),
                lambda k, at: tuple(lax.rem(at[axis] + k, size) if d == dim else 0 for d in range(len(shape))),
            )

        specs += [spec(v.shape) for g in groups for v in g]
        values += [v for g in groups for v in g]
        out_specs += [full(out)] * size
        outs += [jax.ShapeDtypeStruct(out, F32 if wide and k == 0 else BF16) for k in range(size)]
        counts.append(tuple(len(g) for g in groups))
    out = pl.pallas_call(
        functools.partial(combine_kernel, tuple(counts)),
        name="combine",
        grid_spec=pltpu.PrefetchScalarGridSpec(
            num_scalar_prefetch=1, grid=(size,), in_specs=specs, out_specs=out_specs
        ),
        out_shape=outs,
        compiler_params=vmem(20),
        cost_estimate=cost or TINY,
    )(at, *values)
    return [out[n * size : (n + 1) * size] for n in range(len(streams))]


def pick(array, index, dim):
    return lax.dynamic_index_in_dim(array, index, dim, keepdims=False)


def swap(array):
    return lax.ppermute(array, "c", SWAP)


def shift(array, axis, size, k):
    return lax.ppermute(array, axis, [(i, (i + k) % size) for i in range(size)])


def spread(array, axis, size):
    return jnp.stack([array] + [shift(array, axis, size, k) for k in range(1, size)])


def gather(array, first, first_size, second, second_size):
    base = [array] + [shift(array, first, first_size, k) for k in range(1, first_size)]
    return base + [shift(v, second, second_size, j) for j in range(1, second_size) for v in base]


def sent(parts, axis):
    return [parts[0]] + [shift(parts[k], axis, len(parts), k) for k in range(1, len(parts))]


def scatter_sum(array, axis, dim):
    size, me = array.shape[dim], lax.axis_index(axis)
    return sum(sent([pick(array, (me + k) % size, dim) for k in range(size)], axis))


def per_device(sizes, *args):
    (
        hidden, group_sizes, prefix_lens, sol_lens, ln1_gain, ln1_shift, qkv_weight, qv_bias, out_weight, out_bias,
        ln2_gain, ln2_shift, fc_weight, fc_bias, proj_weight, proj_bias, cotangent,
    ) = args
    X, Z, Y = sizes
    S, ND = Z * Y, 2 * X * Z * Y
    _, T, D = hidden.shape
    FF = fc_weight.shape[1]
    heads = D // HD // S
    wd, chunks = heads * HD, S // 2
    half, ffh = D // 2, FF // 2
    rows = D // ND
    dims = (X, Y, Z, T, chunks, wd)
    c, place = lax.axis_index("c"), lax.axis_index(SEQ)

    local = qkv_weight.reshape(rows, 3, X, 2, half // X)
    kept = pick(local, c, 3).reshape(rows, 3 * half)
    given = pick(local, 1 - c, 3).reshape(rows, 3 * half)
    piece = jnp.stack([kept, swap(given)])
    cut = 3 * half // 2
    piece_a, piece_b = spread(piece[..., :cut], "z", Z), spread(piece[..., cut:], "z", Z)

    local = fc_weight.reshape(rows, X, 2, ffh // X)
    kept, given = (pick(local, n, 2).reshape(rows, ffh) for n in (c, 1 - c))
    wide = [slice(n, n + D) for n in range(0, ffh, D)]
    got = swap(jnp.concatenate([given[:, n] for n in wide], axis=0))
    fr = FF // ND
    low = jnp.concatenate([kept[:, wide[0]], got[:rows], proj_weight[: fr // 2], out_weight], axis=0)
    high = jnp.concatenate([kept[:, wide[1]], got[rows:], proj_weight[fr // 2 :]], axis=0)
    low, high, piece_a, piece_b = lax.optimization_barrier((low, high, piece_a, piece_b))
    low, high = (lax.all_gather(v, "z", axis=0, tiled=False) for v in (low, high))
    pieces = gather(piece_a, "x", X, "y", Y) + gather(piece_b, "y", Y, "x", X)

    small = (ln1_gain, ln1_shift, qv_bias, out_bias, ln2_gain, ln2_shift, fc_bias, proj_bias)
    cuts = [0]
    for part in small:
        cuts.append(cuts[-1] + part.shape[0])
    packed = jnp.broadcast_to(jnp.concatenate(small)[None, :], (ND, cuts[-1]))
    packed = lax.all_to_all(packed, ALL, split_axis=0, concat_axis=0, tiled=True).astype(F32)
    gain1, shift1, qv_all, out_b, gain2, shift2, fc_b, proj_b = (
        packed[:, cuts[n] : cuts[n + 1]].reshape(1, -1) for n in range(8)
    )
    fc_b_here = pick(fc_b.reshape(X, 2, ffh // X), c, 1).reshape(1, ffh)
    gain1, shift1, qv_all, out_b, gain2, shift2, fc_b_here, proj_b = lax.optimization_barrier(
        (gain1, shift1, qv_all, out_b, gain2, shift2, fc_b_here, proj_b)
    )

    slot = jnp.arange(sol_lens.shape[1], dtype=jnp.int32)
    used = jnp.where(slot < group_sizes[0], sol_lens[0], 0)
    ends = prefix_lens[0] + jnp.sum(jnp.where(slot[None, :] <= slot[:, None], used[None, :], 0), axis=1)
    meta = jnp.concatenate([prefix_lens, ends, jnp.zeros((15,), jnp.int32)])
    meta_peer = swap(meta)
    meta_here = jnp.where(place < chunks, meta, meta_peer)
    where = [lax.axis_index("x"), c, lax.axis_index("z"), lax.axis_index("y"), place, meta[16], meta_peer[16]]
    at = jnp.stack(where).astype(jnp.int32)

    own, cot = hidden[0], cotangent[0]
    peer, cot_peer = swap(own), swap(cot)

    qv_here = pick(qv_all.reshape(2, X, 2, half // X), c, 2).reshape(2, half)
    bias = jnp.concatenate([qv_here[:1], jnp.zeros_like(qv_here[:1]), qv_here[1:]], axis=1)
    msg, w_qkv, first, norm = project(dims, at, own, peer, gain1, shift1, bias, pieces)

    def exchange(array):
        return lax.all_to_all(array, SEQ, split_axis=0, concat_axis=0, tiled=True)

    qkv = exchange(msg)
    low, high = gather(low, "y", Y, "x", X), gather(high, "x", X, "y", Y)
    att, att_wide, lse = attend(qkv, meta_here, heads)
    w_peer = swap(jnp.stack([v[:, fr:] for v in low]))
    mine = exchange(att)
    theirs = swap(mine)

    resid, second, pre, w_own, w_fc = expand(
        dims, at, [own, peer, mine, theirs, out_b, gain2, shift2], fc_b_here, low, w_peer, high
    )
    out = contract(dims, at, cot, cot_peer, second, pre, w_fc, low, high)
    ahead, give, back, back_low, dy, fc_sum = out[:6]
    grads = lax.psum_scatter(out[6].reshape(X * Y, Z, -1, D), ("x", "y"), scatter_dimension=0, tiled=True)
    d_low, d_wide, d_msg, sums_mid = middle(dims, back, swap(back_low), resid, dy, gain2, w_own)
    up = exchange(d_msg)
    position = place * T + jnp.arange(T, dtype=jnp.int32)
    valid = (position < meta[16]).astype(F32)[:, None]
    layer_out = valid * (resid[:T] + (ahead + swap(give).astype(F32)) + proj_b)

    d_msg = attend_back(qkv, att_wide, lse, up, meta_here, heads)
    d_qkv = exchange(d_msg)
    out = list(project_back(dims, at, d_qkv, w_qkv, first, norm, mine, d_low))
    part, part_peer, qkv_sum, sums_first = out[:4]
    given = swap(part_peer)
    part_a, part_b = sent(out[4 : 4 + X], "x"), sent(out[4 + X :], "y")

    grads, _ = lax.optimization_barrier((grads, part))
    grads = lax.psum_scatter(grads[0], "z", scatter_dimension=0, tiled=True)[0].astype(F32)

    def both_halves(grad, blocks):
        kept = pick(grad, c, 0)
        got = swap(pick(grad, 1 - c, 0).astype(BF16)).astype(F32)
        shape = (kept.shape[0],) + blocks
        kept, got = kept.reshape(shape), got.reshape(shape)
        low = jnp.where(c == 0, kept, got)
        high = jnp.where(c == 0, got, kept)
        return jnp.stack([low, high], axis=-2).reshape(kept.shape[0], -1)

    fc_rows = 2 * ffh // D * rows
    fc_grad = grads[:fc_rows].reshape(2, ffh // D, rows, D).transpose(0, 2, 1, 3).reshape(2, rows, ffh)
    proj_grad = grads[fc_rows:]
    fc_grad = both_halves(fc_grad, (X, ffh // X))

    def own_columns(vector, lead):
        cut = vector.reshape(lead, X, 1, -1)
        spot = lax.broadcasted_iota(jnp.int32, (lead, X, 2, cut.shape[-1]), 2)
        return jnp.where(spot == c, cut, 0.0).reshape(-1)

    qv_sum = jnp.concatenate([qkv_sum[0, :half], qkv_sum[0, 2 * half :]])
    sums = (
        sums_first[0],
        sums_first[1],
        own_columns(qv_sum, 2),
        sums_mid[0],
        sums_mid[1],
        sums_mid[2],
        own_columns(fc_sum, 1),
        sums_mid[3],
    )
    packed = jnp.concatenate([v.reshape(ND, -1) for v in sums], axis=1).reshape(X, 2, Z, Y, -1)
    packed = scatter_sum(packed, "x", 0)

    part_a, part_b = combine(at, (3, 1, [part_a]), (0, 0, [part_b]))
    packed, *_ = lax.optimization_barrier((packed, *part_a, *part_b))
    part_a, part_b, packed = sent(part_a, "y"), sent(part_b, "x"), scatter_sum(packed, "y", 2)
    packed = scatter_sum(scatter_sum(packed, "c", 0), "z", 0)
    d_first = part + given.astype(F32)
    norm, inverse = layer_stats(own.astype(F32))
    hidden_grad = d_wide[:T] + layer_back(d_first, norm, inverse, gain1)
    hidden_grad, layer_out = hidden_grad.astype(BF16), layer_out.astype(BF16)
    hidden_grad, layer_out, packed, fc_grad, proj_grad, *ordered = lax.optimization_barrier(
        (hidden_grad, layer_out, packed, fc_grad, proj_grad, *part_a, *part_b)
    )
    last = combine(at, (2, 0, [ordered[:Y], ordered[Y:]]), wide=True)[0]
    last = sent(last, "z")
    last = sum(v.astype(F32) for v in last)
    value = last[2 * rows : 3 * rows].reshape(rows, 2, half).transpose(1, 0, 2)
    qkv_grad = jnp.concatenate([last[: 2 * rows].reshape(2, rows, D), value], axis=2)
    out_grad = last[3 * rows :]
    qkv_grad = both_halves(qkv_grad, (3, X, half // X))

    gain1_g, shift1_g, qv_g, out_b_g, gain2_g, shift2_g, fc_b_g, proj_b_g = (
        packed[cuts[n] : cuts[n + 1]] for n in range(8)
    )
    return (
        layer_out[None], hidden_grad[None], gain1_g, shift1_g, qkv_grad, qv_g, out_grad,
        out_b_g, gain2_g, shift2_g, fc_grad, fc_b_g, proj_grad, proj_b_g,
    )


def solution(mesh):
    Z = 4
    X, Y = mesh.shape["dp"] // 2, mesh.shape["seq"] // Z
    split = Mesh(mesh.devices.reshape(X, 2, Z, Y), ALL)
    group, wide, flat = P(("x", "c"), SEQ, None), P(ALL, None), P(ALL)
    dp = P(("x", "c"))
    return jax.shard_map(
        functools.partial(per_device, (X, Z, Y)),
        mesh=split,
        in_specs=(
            group, dp, dp, P(("x", "c"), None), flat, flat, wide, flat, wide, flat, flat, flat, wide, flat, wide, flat,
            group,
        ),
        out_specs=(
            group, group, flat, flat, wide, flat, wide, flat, flat, flat, wide, flat, wide, flat,
        ),
        check_vma=False,
    )
```

```python
import functools

import jax
import jax.numpy as jnp
from jax import lax
from jax.experimental import pallas as pl
from jax.experimental.pallas import tpu as pltpu
from jax.sharding import Mesh
from jax.sharding import PartitionSpec as P

HD = 64
EPSILON = 1e-05
BIG = 1e30
BLOCK = 256
DEPTH = 2
F32 = jnp.float32
LONG = pl.CostEstimate(flops=10**11, bytes_accessed=1, transcendentals=0)
TINY = pl.CostEstimate(flops=1, bytes_accessed=1, transcendentals=0)
BF16 = jnp.bfloat16
ALL = ("x", "c", "z", "y")
SEQ = ("z", "y")
SWAP = [(0, 1), (1, 0)]


def dot_nt(a, b):
    return lax.dot_general(a, b, (((1,), (1,)), ((), ())), preferred_element_type=F32)


def dot_nn(a, b):
    return lax.dot_general(a, b, (((1,), (0,)), ((), ())), preferred_element_type=F32)


def dot_tn(a, b):
    return lax.dot_general(a, b, (((0,), (0,)), ((), ())), preferred_element_type=F32)


def segment_code(ends_ref, start, rows, lanes):
    pos = start + lax.broadcasted_iota(jnp.int32, (rows, lanes), 0)
    passed = jnp.ones((rows, lanes), jnp.int32)
    for t in range(16):
        passed = passed + jnp.where(pos >= ends_ref[1 + t], 1, 0)
    code = jnp.where(pos < ends_ref[16], passed, 17)
    return jnp.where(pos < ends_ref[0], 0, code)


def with_segments(keys, ends_ref, start):
    rows, lanes = keys.shape
    code = segment_code(ends_ref, start, rows, lanes)
    lane = lax.broadcasted_iota(jnp.int32, (rows, lanes), 1)
    key_mark = jnp.where((code == lane) & (code > 0), 1.0, 0.0).astype(BF16)
    query_mark = jnp.where(code == lane, 0.0, -BIG).astype(BF16)
    return jnp.concatenate([keys, key_mark], axis=1), query_mark


def head_part(array, head, heads):
    if heads == 1:
        return array
    lane = lax.broadcasted_iota(jnp.int32, array.shape, 1)
    return jnp.where((lane >= head * HD) & (lane < (head + 1) * HD), array, jnp.zeros_like(array))


def merge_heads(parts):
    out = parts[0]
    if len(parts) > 1:
        lane = lax.broadcasted_iota(jnp.int32, out.shape, 1)
        for head in range(1, len(parts)):
            out = jnp.where(lane >= head * HD, parts[head], out)
    return out


def causal(rows, cols, transposed):
    row = lax.broadcasted_iota(jnp.int32, (rows, cols), 0)
    col = lax.broadcasted_iota(jnp.int32, (rows, cols), 1)
    return (row <= col) if transposed else (col <= row)


def attend_kernel(heads, ends_ref, qkv_ref, out_ref, wide_ref, lse_ref, keys, values, scores):
    i = pl.program_id(0)
    width = heads * HD
    start = pl.multiple_of(i * BLOCK, BLOCK)
    query_in, keys_in, values_in = (qkv_ref[:, t].reshape(BLOCK, width) for t in range(3))
    tagged, query_mark = with_segments(keys_in, ends_ref, start)
    keys[pl.ds(start, BLOCK), :] = tagged
    values[pl.ds(start, BLOCK), :] = values_in
    scaled = query_in * BF16(HD**-0.5)
    query = [
        jnp.concatenate([head_part(scaled, h, heads), query_mark], axis=1) for h in range(heads)
    ]

    def fold(array, op):
        out = array[:, :128]
        for at in range(128, BLOCK, 128):
            out = op(out, array[:, at : at + 128])
        return out

    def first(j, tops):
        block = keys[pl.ds(pl.multiple_of(j * BLOCK, BLOCK), BLOCK), :]
        new = []
        for h in range(heads):
            score = dot_nt(query[h], block)
            scores[h, j] = score
            new.append(jnp.maximum(tops[h], fold(score, jnp.maximum)))
        return tuple(new)

    tops = []
    for h in range(heads):
        score = jnp.where(causal(BLOCK, BLOCK, False), dot_nt(query[h], tagged), -BIG)
        scores[h, i] = score
        tops.append(fold(score, jnp.maximum))
    tops = lax.fori_loop(0, i, first, tuple(tops))
    tops = [jnp.max(t, axis=1, keepdims=True) for t in tops]

    def second(j, carry):
        sums, accs = carry
        block = values[pl.ds(pl.multiple_of(j * BLOCK, BLOCK), BLOCK), :]
        new_sums, new_accs = [], []
        for h in range(heads):
            expo = jnp.exp(scores[h, j] - tops[h])
            new_sums.append(sums[h] + fold(expo, jnp.add))
            new_accs.append(accs[h] + dot_nn(expo.astype(BF16), block))
        return tuple(new_sums), tuple(new_accs)

    zero = tuple(jnp.zeros((BLOCK, 128), F32) for _ in range(heads))
    zero_acc = tuple(jnp.zeros((BLOCK, width), F32) for _ in range(heads))
    sums, accs = lax.fori_loop(0, i + 1, second, (zero, zero_acc))
    sums = [jnp.sum(t, axis=1, keepdims=True) for t in sums]
    wide = merge_heads([accs[h] / sums[h] for h in range(heads)])
    wide_ref[...] = wide
    out_ref[...] = wide.astype(BF16).reshape(out_ref.shape)
    for h in range(heads):
        lse = jnp.broadcast_to(tops[h] + jnp.log(sums[h]), (BLOCK, 128))
        lse_ref[h : h + 1, :] = lse.T[0:1, :]


def attend(qkv, ends, heads):
    length, width = qkv.shape[0] * qkv.shape[2], heads * HD
    T = qkv.shape[2]
    per = BLOCK // T
    return pl.pallas_call(
        functools.partial(attend_kernel, heads),
        name="attend",
        grid=(length // BLOCK,),
        in_specs=[
            pl.BlockSpec(memory_space=pltpu.SMEM),
            pl.BlockSpec((per, 3, T, width), lambda i: (i, 0, 0, 0)),
        ],
        out_specs=[
            pl.BlockSpec((per, T, width), lambda i: (i, 0, 0)),
            pl.BlockSpec((BLOCK, width), lambda i: (i, 0)),
            pl.BlockSpec((8, BLOCK), lambda i: (0, i)),
        ],
        out_shape=[
            jax.ShapeDtypeStruct((length // T, T, width), BF16),
            jax.ShapeDtypeStruct((length, width), F32),
            jax.ShapeDtypeStruct((8, length), F32),
        ],
        scratch_shapes=[
            pltpu.VMEM((length, 2 * width), BF16),
            pltpu.VMEM((length, width), BF16),
            pltpu.VMEM((heads, length // BLOCK, BLOCK, BLOCK), F32),
        ],
        compiler_params=pltpu.CompilerParams(vmem_limit_bytes=32 << 20),
        cost_estimate=TINY,
    )(ends, qkv)


def attend_back_kernel(
    heads, ends_ref, qkv_ref, wide_ref, lse_ref, up_ref, out_ref, keys, values, key_acc, value_acc, query_acc, inner_all
):
    i = pl.program_id(0)
    width = heads * HD
    start = pl.multiple_of(i * BLOCK, BLOCK)
    query_in, keys_in, values_in = (qkv_ref[:, t].reshape(BLOCK, width) for t in range(3))
    tagged, query_mark = with_segments(keys_in, ends_ref, start)
    keys[pl.ds(start, BLOCK), :] = tagged
    values[pl.ds(start, BLOCK), :] = values_in
    key_acc[pl.ds(start, BLOCK), :] = jnp.zeros((BLOCK, width), F32)
    value_acc[pl.ds(start, BLOCK), :] = jnp.zeros((BLOCK, width), F32)
    scaled = query_in * BF16(HD**-0.5)
    up = up_ref[...].reshape(BLOCK, width)
    inner_all[...] = (up.astype(F32) * wide_ref[...]).T
    query_acc[...] = jnp.zeros((BLOCK, width), F32)

    def step(h, first, rows, diagonal):
        spot = slice(first, first + rows)
        block, value = keys[spot, :], values[spot, :]
        part, up_part = head_part(scaled, h, heads), head_part(up, h, heads)
        score = dot_nt(block, jnp.concatenate([part, query_mark], axis=1))
        if diagonal:
            score = jnp.where(causal(BLOCK, BLOCK, True), score, -BIG)
        inner = jnp.sum(inner_all[pl.ds(pl.multiple_of(h * HD, HD), HD), :], axis=0, keepdims=True)
        prob = jnp.exp(score - lse_ref[pl.ds(h, 1), :])
        d_prob = dot_nt(value, up_part)
        d_score = (prob * (d_prob - inner)).astype(BF16)
        value_acc[spot, :] += dot_nn(prob.astype(BF16), up_part)
        key_acc[spot, :] += dot_nn(d_score, part)
        query_acc[...] += head_part(dot_tn(d_score, block[:, :width]), h, heads)

    for n in range(keys.shape[0] // BLOCK):

        @pl.when(i == n)
        def _():
            def one_head(h, carry):
                step(h, n * BLOCK, BLOCK, True)
                if n:
                    step(h, 0, n * BLOCK, False)
                return carry

            lax.fori_loop(0, heads, one_head, 0)

    d_query = query_acc[...] * HD**-0.5
    T = out_ref.shape[2]
    per = BLOCK // T
    out_ref[pl.ds(i * per, per), 0] = d_query.astype(BF16).reshape(per, T, width)

    @pl.when(i == pl.num_programs(0) - 1)
    def _():
        for s in range(out_ref.shape[0]):
            out_ref[s, 1] = key_acc[s * T : (s + 1) * T, :].astype(BF16)
            out_ref[s, 2] = value_acc[s * T : (s + 1) * T, :].astype(BF16)


def attend_back(qkv, wide, lse, up, ends, heads):
    length, width = qkv.shape[0] * qkv.shape[2], heads * HD
    T = qkv.shape[2]
    per = BLOCK // T
    return pl.pallas_call(
        functools.partial(attend_back_kernel, heads),
        name="attend_back",
        grid=(length // BLOCK,),
        in_specs=[
            pl.BlockSpec(memory_space=pltpu.SMEM),
            pl.BlockSpec((per, 3, T, width), lambda i: (i, 0, 0, 0)),
            pl.BlockSpec((BLOCK, width), lambda i: (i, 0)),
            pl.BlockSpec((8, BLOCK), lambda i: (0, i)),
            pl.BlockSpec((per, T, width), lambda i: (i, 0, 0)),
        ],
        out_specs=pl.BlockSpec((length // T, 3, T, width), lambda i: (0, 0, 0, 0)),
        out_shape=jax.ShapeDtypeStruct((length // T, 3, T, width), BF16),
        scratch_shapes=[
            pltpu.VMEM((length, 2 * width), BF16),
            pltpu.VMEM((length, width), BF16),
            pltpu.VMEM((length, width), F32),
            pltpu.VMEM((length, width), F32),
            pltpu.VMEM((BLOCK, width), F32),
            pltpu.VMEM((width, BLOCK), F32),
        ],
        compiler_params=pltpu.CompilerParams(vmem_limit_bytes=32 << 20),
        cost_estimate=TINY,
    )(ends, qkv, wide, lse, up)


def layer_stats(rows):
    centred = rows - jnp.mean(rows, axis=-1, keepdims=True)
    inverse = lax.rsqrt(jnp.mean(centred * centred, axis=-1, keepdims=True) + EPSILON)
    return centred * inverse, inverse


def layer_back(upstream, normed, inverse, gain):
    scaled = upstream * gain
    return inverse * (
        scaled
        - jnp.mean(scaled, axis=-1, keepdims=True)
        - normed * jnp.mean(scaled * normed, axis=-1, keepdims=True)
    )


def full(shape):
    return pl.BlockSpec(shape, lambda *_: (0,) * len(shape))


def vmem(mib):
    return pltpu.CompilerParams(vmem_limit_bytes=mib << 20)


def origin(k, me, size):
    return lax.rem(me - k + size, size)


def at_rows(start, rows):
    return pl.ds(pl.multiple_of(start, rows), rows)


def project_kernel(dims, at_ref, own_ref, peer_ref, gain_ref, shift_ref, bias_ref, *refs):
    X, Y, Z, T, chunks, wd = dims
    a_refs, b_refs, refs = refs[: X * Y], refs[X * Y : 2 * X * Y], refs[2 * X * Y :]
    msg_ref, w_out_ref, first_ref, norm_ref, w_ref = refs
    rows, part = a_refs[0].shape[-2:]
    width = w_ref.shape[1] // (3 * X)

    @pl.when((pl.program_id(0) == 0) & (pl.program_id(1) == 0))
    def _():
        x_me, c_me, z_me, y_me = (at_ref[n] for n in range(4))
        for kx in range(X):
            for ky in range(Y):
                x, y = origin(kx, x_me, X), origin(ky, y_me, Y)
                for kz in range(Z):
                    z = origin(kz, z_me, Z)
                    for kc in range(2):
                        c = lax.rem(c_me + kc, 2)
                        spot = at_rows((((x * 2 + c) * Z + z) * Y + y) * rows, rows)
                        w_ref[spot, :part] = a_refs[ky * X + kx][kz, kc]
                        w_ref[spot, part:] = b_refs[kx * Y + ky][kz, kc]
        for r, ref in enumerate((own_ref, peer_ref)):
            normed, _ = layer_stats(ref[...].astype(F32))
            norm_ref[r * T : (r + 1) * T, :] = normed.astype(BF16)
            first_ref[r * T : (r + 1) * T, :] = (normed * gain_ref[...] + shift_ref[...]).astype(BF16)

    t, x = pl.program_id(0), pl.program_id(1)
    col = pl.multiple_of((t * X + x) * width, width)
    w = w_ref[:, pl.ds(col, width)]
    w_out_ref[...] = w
    out = dot_nn(first_ref[...], w) + bias_ref[:, pl.ds(col, width)]
    out = out.astype(BF16)
    per = width // wd
    for r in range(2):
        for k in range(per):
            msg_ref[r * chunks + x * per + k, 0] = out[r * T : (r + 1) * T, k * wd : (k + 1) * wd]


def project(dims, at, own, peer, gain, shift, bias, pieces):
    X, Y, Z, T, chunks, wd = dims
    D = own.shape[1]
    cols = 2 * pieces[0].shape[-1]
    return pl.pallas_call(
        functools.partial(project_kernel, dims),
        name="project",
        grid=(3, X),
        in_specs=[pl.BlockSpec(memory_space=pltpu.SMEM)]
        + [full(v.shape) for v in (own, peer, gain, shift, bias, *pieces)],
        out_specs=[
            pl.BlockSpec((2 * chunks, 1, T, wd), lambda t, x: (0, t, 0, 0)),
            pl.BlockSpec((D, cols // (3 * X)), lambda t, x: (0, t * X + x)),
            full((2 * T, D)), full((2 * T, D)),
        ],
        scratch_shapes=[pltpu.VMEM((D, cols), BF16)],
        out_shape=[
            jax.ShapeDtypeStruct((2 * chunks, 3, T, wd), BF16),
            jax.ShapeDtypeStruct((D, cols), BF16),
            jax.ShapeDtypeStruct((2 * T, D), BF16),
            jax.ShapeDtypeStruct((2 * T, D), BF16),
        ],
        compiler_params=vmem(60),
        cost_estimate=TINY,
    )(at, own, peer, gain, shift, bias, *pieces)


def expand_kernel(dims, at_ref, *refs):
    X, Y, Z, T, chunks, wd = dims
    own_ref, peer_ref, mine_ref, theirs_ref, out_b_ref, gain_ref, shift_ref, fc_b_ref = refs[:8]
    refs = refs[8:]
    n = X * Y
    own_w_refs, low_refs, high_refs, refs = refs[:n], refs[n : 2 * n], refs[2 * n : 3 * n], refs[3 * n :]
    peer_w_ref, resid_ref, second_ref, pre_ref, w_own_ref, fc_ref, w_peer = refs
    D = own_ref.shape[1]
    rows = own_w_refs[0].shape[1]
    f = pl.program_id(0)
    x_me, c_me, y_me = (at_ref[n] for n in (0, 1, 3))

    @pl.when(f == 0)
    def _():
        for kx in range(X):
            for ky in range(Y):
                for kz in range(Z):
                    x, y, z = origin(kx, x_me, X), origin(ky, y_me, Y), kz
                    spot = at_rows(((x * Z + z) * Y + y) * rows, rows)
                    w_own_ref[spot, :] = own_w_refs[kx * Y + ky][kz]
                    w_peer[spot, :] = peer_w_ref[kx * Y + ky, kz]
        per = chunks // X
        width = per * wd
        for r, x_ref in enumerate((own_ref, peer_ref)):
            resid = x_ref[...].astype(F32) + out_b_ref[...]
            for source, base, w in ((mine_ref, r, w_own_ref), (theirs_ref, 1 - r, w_peer)):
                for x in range(X):
                    parts = [source[base * chunks + x * per + k] for k in range(per)]
                    resid = resid + dot_nn(jnp.concatenate(parts, axis=1), w[x * width : (x + 1) * width, :])
            part = slice(r * T, (r + 1) * T)
            resid_ref[part, :] = resid
            normed, _ = layer_stats(resid)
            second_ref[part, :] = (normed * gain_ref[...] + shift_ref[...]).astype(BF16)

    def place(block, kx, ky, kz):
        x, y, z = origin(kx, x_me, X), origin(ky, y_me, Y), kz
        for kc in range(2):
            c = lax.rem(c_me + kc, 2)
            fc_ref[at_rows((((x * 2 + c) * Z + z) * Y + y) * rows, rows), :] = block[kc * rows : (kc + 1) * rows, :]

    steps = pl.num_programs(0)

    @pl.when(f * 2 < steps)
    def _():
        for kx in range(X):
            for ky in range(Y):
                for kz in range(Z):
                    place(low_refs[kx * Y + ky][kz], kx, ky, kz)

    @pl.when(f * 2 >= steps)
    def _():
        for kx in range(X):
            for ky in range(Y):
                for kz in range(Z):
                    place(high_refs[ky * X + kx][kz], kx, ky, kz)

    pre_ref[...] = dot_nn(second_ref[...], fc_ref[...]) + fc_b_ref[...]


def expand(dims, at, inputs, fc_b, low, w_peer, high):
    X, Y, Z, T, chunks, wd = dims
    D = inputs[0].shape[1]
    half, ffh = D // 2, fc_b.shape[1]
    rows = half // (X * Y * Z)
    steps = X * Z // DEPTH
    tile, per = ffh // steps, steps // 2
    return pl.pallas_call(
        functools.partial(expand_kernel, dims),
        name="expand",
        grid_spec=pltpu.PrefetchScalarGridSpec(
            num_scalar_prefetch=1,
            grid=(steps,),
            in_specs=[full(v.shape) for v in inputs]
            + [pl.BlockSpec((1, tile), lambda f, at: (0, f))]
            + [pl.BlockSpec((Z, rows, D), lambda f, at: (0, 4, 0))] * (X * Y)
            + [pl.BlockSpec((Z, 2 * rows, tile), lambda f, at: (0, 0, jnp.minimum(f, per - 1)))] * (X * Y)
            + [pl.BlockSpec((Z, 2 * rows, tile), lambda f, at: (0, 0, jnp.maximum(f - per, 0)))] * (X * Y)
            + [full(w_peer.shape)],
            out_specs=[
                full((2 * T, D)), full((2 * T, D)),
                pl.BlockSpec((2 * T, tile), lambda f, at: (0, f)),
                full((half, D)),
                pl.BlockSpec((D, tile), lambda f, at: (0, f)),
            ],
            scratch_shapes=[pltpu.VMEM((half, D), BF16)],
        ),
        out_shape=[
            jax.ShapeDtypeStruct((2 * T, D), F32),
            jax.ShapeDtypeStruct((2 * T, D), BF16),
            jax.ShapeDtypeStruct((2 * T, ffh), F32),
            jax.ShapeDtypeStruct((half, D), BF16),
            jax.ShapeDtypeStruct((D, ffh), BF16),
        ],
        compiler_params=vmem(60),
        cost_estimate=TINY,
    )(at, *inputs, fc_b, *low, *low, *high, w_peer)


def contract_kernel(dims, at_ref, *refs):
    X, Y, Z, T, chunks, wd = dims
    cot_own_ref, cot_peer_ref, second_ref, pre_ref, fc_ref = refs[:5]
    refs = refs[5:]
    low_refs, high_refs, refs = refs[: X * Y], refs[X * Y : 2 * X * Y], refs[2 * X * Y :]
    own_ref, give_ref, back_ref, back_low_ref, dy_ref, fc_sum_ref = refs[:6]
    refs = refs[6:]
    grad_ref, flipped, proj, grad, acc = refs
    D = cot_own_ref.shape[1]
    tile = pre_ref.shape[1]
    fr = tile // (Y * DEPTH)
    zs = Z // DEPTH
    cut = fr // 2
    rows = grad_ref.shape[3] // 8
    f = pl.program_id(0)
    x_me, y_me, place = at_ref[0], at_ref[3], at_ref[4]

    @pl.when(f == 0)
    def _():
        for r, cot_ref in enumerate((cot_own_ref, cot_peer_ref)):
            pos = place * T + lax.broadcasted_iota(jnp.int32, (T, D), 0)
            dy_ref[r * T : (r + 1) * T, :] = jnp.where(pos < at_ref[5 + r], cot_ref[...], BF16(0.0))
        flipped[...] = second_ref[...].T

    for ky in range(Y):
        for kx in range(X):

            @pl.when(origin(kx, x_me, X) == f // zs)
            def _():
                for z in range(DEPTH):
                    start = (z * Y + origin(ky, y_me, Y)) * fr
                    proj[at_rows(start, cut), :] = low_refs[kx * Y + ky][z]
                    proj[at_rows(start + cut, cut), :] = high_refs[ky * X + kx][z]

    pre = pre_ref[...]
    d_act = dot_nt(dy_ref[...], proj[...])
    k0, k1 = 0.7978845608028654, 0.044715
    square = pre * pre
    tanh = jnp.tanh(k0 * (pre + k1 * (square * pre)))
    left = 0.5 * (1.0 + tanh)
    act = (pre * left).astype(BF16)
    slope = left + 0.5 * pre * (1.0 - tanh * tanh) * (k0 * (1.0 + 3.0 * k1 * square))
    d_pre = (slope * d_act).astype(BF16)
    fc_sum_ref[...] = jnp.sum(d_pre.astype(F32), axis=0, keepdims=True)
    part = dot_nn(act, proj[...])
    back = dot_nt(d_pre, fc_ref[...])
    tall = dot_tn(act, dy_ref[...]).astype(BF16)
    for z in range(DEPTH):
        for y in range(Y):
            start = (z * Y + y) * fr
            grad_ref[f // zs, y, lax.rem(f, zs) * DEPTH + z, 4 * rows :, :] = tall[start : start + fr, :]
    grad[...] = dot_nn(flipped[...], d_pre).astype(BF16)
    n, lane = (f * tile) // D, pl.multiple_of(lax.rem(f * tile, D), tile)
    for x in range(X):
        for c in range(2):
            for z in range(Z):
                for y in range(Y):
                    start = (((x * 2 + c) * Z + z) * Y + y) * rows
                    value = grad[start : start + rows, :]
                    grad_ref[x, y, z, at_rows((c * 2 + n) * rows, rows), pl.ds(lane, tile)] = value

    @pl.when(f == 0)
    def _():
        acc[...] = part
        back_ref[...] = back

    @pl.when(f > 0)
    def _():
        acc[...] += part
        back_ref[...] += back

    @pl.when(f == pl.num_programs(0) - 1)
    def _():
        own_ref[...] = acc[:T, :]
        give_ref[...] = acc[T:, :].astype(BF16)
        back_low_ref[:T, :] = back_ref[T:, :].astype(BF16)
        back_low_ref[T:, :] = back_ref[:T, :].astype(BF16)


def contract(dims, at, cot_own, cot_peer, second, pre, fc, low, high):
    X, Y, Z, T, chunks, wd = dims
    D, ffh = fc.shape
    steps = X * Z // DEPTH
    tile = ffh // steps
    cut = tile // (2 * Y * DEPTH)
    rows = D // (2 * X * Y * Z)

    def block(f, at):
        return (f % (Z // DEPTH), 1, 0)

    return pl.pallas_call(
        functools.partial(contract_kernel, dims),
        name="contract",
        grid_spec=pltpu.PrefetchScalarGridSpec(
            num_scalar_prefetch=1,
            grid=(steps,),
            in_specs=[full(v.shape) for v in (cot_own, cot_peer, second)]
            + [
                pl.BlockSpec((2 * T, tile), lambda f, at: (0, f)),
                pl.BlockSpec((D, tile), lambda f, at: (0, f)),
            ]
            + [pl.BlockSpec((DEPTH, cut, D), block)] * (2 * X * Y),
            out_specs=[
                full((T, D)), full((T, D)), full((2 * T, D)), full((2 * T, D)), full((2 * T, D)),
                pl.BlockSpec((1, tile), lambda f, at: (0, f)),
            ]
            + [full((X, Y, Z, 8 * rows, D))],
            scratch_shapes=[
                pltpu.VMEM((D, 2 * T), BF16),
                pltpu.VMEM((tile, D), BF16),
                pltpu.VMEM((D, tile), BF16),
                pltpu.VMEM((2 * T, D), F32),
            ],
        ),
        out_shape=[
            jax.ShapeDtypeStruct((T, D), F32),
            jax.ShapeDtypeStruct((T, D), BF16),
            jax.ShapeDtypeStruct((2 * T, D), F32),
            jax.ShapeDtypeStruct((2 * T, D), BF16),
            jax.ShapeDtypeStruct((2 * T, D), BF16),
            jax.ShapeDtypeStruct((1, ffh), F32),
        ]
        + [jax.ShapeDtypeStruct((X, Y, Z, 8 * rows, D), BF16)],
        compiler_params=vmem(60),
        cost_estimate=TINY,
    )(at, cot_own, cot_peer, second, pre, fc, *low, *high)


def middle_kernel(
    dims, back_ref, got_ref, resid_ref, dy_ref, gain_ref, w_ref, low_ref, wide_ref, msg_ref, sums_ref
):
    X, Y, Z, T, chunks, wd = dims
    b = pl.program_id(0)
    rows, D = back_ref.shape
    steps = T // rows
    normed, inverse = layer_stats(resid_ref[...])
    d_second = back_ref[...] + got_ref[...].astype(F32)
    dy = dy_ref[...].astype(F32)
    d_resid = dy + layer_back(d_second, normed, inverse, gain_ref[...])
    low = d_resid.astype(BF16)
    low_ref[...] = low
    wide_ref[...] = d_resid
    per = chunks // X
    start = pl.multiple_of(lax.rem(b, steps) * rows, rows)
    for x in range(X):
        out = dot_nt(low, w_ref[x * per * wd : (x + 1) * per * wd, :]).astype(BF16)
        for k in range(per):
            msg_ref[(b // steps) * chunks + x * per + k, pl.ds(start, rows), :] = out[:, k * wd : (k + 1) * wd]

    @pl.when(b == 0)
    def _():
        sums_ref[...] = jnp.zeros_like(sums_ref)

    @pl.when(b < steps)
    def _():
        for n, value in enumerate((d_resid, d_second * normed, d_second, dy)):
            sums_ref[n : n + 1, :] += jnp.sum(value, axis=0, keepdims=True)


def middle(dims, back, got, resid, dy, gain, w_own):
    X, Y, Z, T, chunks, wd = dims
    D = back.shape[1]
    block = min(128, T)
    row = pl.BlockSpec((block, D), lambda b: (b, 0))
    return pl.pallas_call(
        functools.partial(middle_kernel, dims),
        name="middle",
        grid=(2 * T // block,),
        in_specs=[row, row, row, row, full(gain.shape), full(w_own.shape)],
        out_specs=[row, row, full((2 * chunks, T, wd)), full((8, D))],
        out_shape=[
            jax.ShapeDtypeStruct((2 * T, D), BF16),
            jax.ShapeDtypeStruct((2 * T, D), F32),
            jax.ShapeDtypeStruct((2 * chunks, T, wd), BF16),
            jax.ShapeDtypeStruct((8, D), F32),
        ],
        compiler_params=vmem(60),
        cost_estimate=TINY,
    )(back, got, resid, dy, gain, w_own)


def project_back_kernel(
    dims, at_ref, d_ref, w_ref, first_ref, norm_ref, mine_ref, low_ref, own_ref, give_ref, sum_ref, sums_ref, *refs
):
    X, Y, Z, T, chunks, wd = dims
    a_refs, b_refs, (joint, block) = refs[:X], refs[X : X + Y], refs[X + Y :]
    g = pl.program_id(0)
    x, c = g // 2, pl.multiple_of(lax.rem(g, 2), 1)
    half = chunks * wd

    @pl.when(g == 0)
    def _():
        for r in range(2):
            for t in range(3):
                for h in range(chunks):
                    at = t * half + h * wd
                    joint[r * T : (r + 1) * T, at : at + wd] = d_ref[r * chunks + h, t]
        sum_ref[...] = jnp.sum(joint[...].astype(F32), axis=0, keepdims=True)

    part = dot_nt(joint[...], w_ref[...])
    own_ref[...] = part[:T, :]
    give_ref[...] = part[T:, :].astype(BF16)
    sums_ref[0:1, :] = jnp.sum(part * norm_ref[...].astype(F32), axis=0, keepdims=True)
    sums_ref[1:2, :] = jnp.sum(part, axis=0, keepdims=True)
    block[...] = dot_tn(first_ref[...], joint[...]).astype(BF16)
    rows = block.shape[0] // (Z * Y)
    for k in range(X):

        @pl.when(x == lax.rem(at_ref[0] + k, X))
        def _():
            a_refs[k][:, :, at_rows(c * rows, rows), :] = block[:, : 2 * half].reshape(Z, Y, rows, 2 * half)

    def spots(k):
        y = lax.rem(at_ref[3] + k, Y)
        return [(z, at_rows((z * Y + y) * rows, rows)) for z in range(Z)]

    for k in range(Y):
        for z, spot in spots(k):
            b_refs[k][x, z, :rows, at_rows(c * half, half)] = block[spot, 2 * half :]

    @pl.when(c == 0)
    def _():
        per = chunks // X
        left = [jnp.concatenate([mine_ref[r * chunks + x * per + j] for r in range(2)], axis=0) for j in range(per)]
        block[:, : 2 * half] = dot_tn(jnp.concatenate(left, axis=1), low_ref[...]).astype(BF16)
        for k in range(Y):
            for z, spot in spots(k):
                b_refs[k][x, z, rows:, :] = block[spot, : 2 * half]


def project_back(dims, at, d_msg, w, first, norm, mine, low):
    X, Y, Z, T, chunks, wd = dims
    D, cols = w.shape
    block = D // (2 * X)
    rows = block // (Z * Y)
    a_shape, b_shape = (Z, Y, 2 * rows, D), (X, Z, 2 * rows, D)
    return pl.pallas_call(
        functools.partial(project_back_kernel, dims),
        name="project_back",
        grid=(2 * X,),
        in_specs=[
            pl.BlockSpec(memory_space=pltpu.SMEM),
            full(d_msg.shape),
            pl.BlockSpec((block, cols), lambda g: (g, 0)),
            pl.BlockSpec((2 * T, block), lambda g: (0, g)),
            pl.BlockSpec((2 * T, block), lambda g: (0, g)),
            full(mine.shape), full(low.shape),
        ],
        out_specs=[
            pl.BlockSpec((T, block), lambda g: (0, g)),
            pl.BlockSpec((T, block), lambda g: (0, g)),
            full((1, cols)),
            pl.BlockSpec((8, block), lambda g: (0, g)),
        ]
        + [full(a_shape)] * X
        + [full(b_shape)] * Y,
        out_shape=[
            jax.ShapeDtypeStruct((T, D), F32),
            jax.ShapeDtypeStruct((T, D), BF16),
            jax.ShapeDtypeStruct((1, cols), F32),
            jax.ShapeDtypeStruct((8, D), F32),
        ]
        + [jax.ShapeDtypeStruct(a_shape, BF16)] * X
        + [jax.ShapeDtypeStruct(b_shape, BF16)] * Y,
        scratch_shapes=[pltpu.VMEM((2 * T, cols), BF16), pltpu.VMEM((block, cols), BF16)],
        compiler_params=vmem(60),
        cost_estimate=TINY,
    )(at, d_msg, w, first, norm, mine, low)


def combine_kernel(streams, at_ref, *refs):
    step, taken = pl.program_id(0), []
    for counts in streams:
        groups = []
        for count in counts:
            groups.append(refs[:count])
            refs = refs[count:]
        taken.append(groups)
    size = len(refs) // len(streams)
    for n, groups in enumerate(taken):
        for k, out_ref in enumerate(refs[n * size : (n + 1) * size]):

            @pl.when(step == k)
            def _():
                start = 0
                for group in groups:
                    total = group[0][...].astype(F32)
                    for ref in group[1:]:
                        total = total + ref[...].astype(F32)
                    total = total.reshape(out_ref.shape[:-2] + total.shape[-2:]).astype(out_ref.dtype)
                    out_ref[..., start : start + total.shape[-2], :] = total
                    start += total.shape[-2]


def combine(at, *streams, wide=False, cost=None):
    specs, outs, values, out_specs, counts = [], [], [], [], []
    size = streams[0][2][0][0].shape[streams[0][1]]
    for axis, dim, groups in streams:
        shape = groups[0][0].shape
        rest = tuple(n for d, n in enumerate(shape) if d != dim)
        out = rest[:-2] + (sum(g[0].shape[-2] for g in groups), rest[-1])

        def spec(shape, axis=axis, dim=dim):
            return pl.BlockSpec(
                tuple(1 if d == dim else n for d, n in enumerate(shape)),
                lambda k, at: tuple(lax.rem(at[axis] + k, size) if d == dim else 0 for d in range(len(shape))),
            )

        specs += [spec(v.shape) for g in groups for v in g]
        values += [v for g in groups for v in g]
        out_specs += [full(out)] * size
        outs += [jax.ShapeDtypeStruct(out, F32 if wide and k == 0 else BF16) for k in range(size)]
        counts.append(tuple(len(g) for g in groups))
    out = pl.pallas_call(
        functools.partial(combine_kernel, tuple(counts)),
        name="combine",
        grid_spec=pltpu.PrefetchScalarGridSpec(
            num_scalar_prefetch=1, grid=(size,), in_specs=specs, out_specs=out_specs
        ),
        out_shape=outs,
        compiler_params=vmem(20),
        cost_estimate=cost or TINY,
    )(at, *values)
    return [out[n * size : (n + 1) * size] for n in range(len(streams))]


def pick(array, index, dim):
    return lax.dynamic_index_in_dim(array, index, dim, keepdims=False)


def swap(array):
    return lax.ppermute(array, "c", SWAP)


def shift(array, axis, size, k):
    return lax.ppermute(array, axis, [(i, (i + k) % size) for i in range(size)])


def spread(array, axis, size):
    return jnp.stack([array] + [shift(array, axis, size, k) for k in range(1, size)])


def gather(array, first, first_size, second, second_size):
    base = [array] + [shift(array, first, first_size, k) for k in range(1, first_size)]
    return base + [shift(v, second, second_size, j) for j in range(1, second_size) for v in base]


def sent(parts, axis):
    return [parts[0]] + [shift(parts[k], axis, len(parts), k) for k in range(1, len(parts))]


def scatter_sum(array, axis, dim):
    size, me = array.shape[dim], lax.axis_index(axis)
    return sum(sent([pick(array, (me + k) % size, dim) for k in range(size)], axis))


def per_device(sizes, *args):
    (
        hidden, group_sizes, prefix_lens, sol_lens, ln1_gain, ln1_shift, qkv_weight, qv_bias, out_weight, out_bias,
        ln2_gain, ln2_shift, fc_weight, fc_bias, proj_weight, proj_bias, cotangent,
    ) = args
    X, Z, Y = sizes
    S, ND = Z * Y, 2 * X * Z * Y
    _, T, D = hidden.shape
    FF = fc_weight.shape[1]
    heads = D // HD // S
    wd, chunks = heads * HD, S // 2
    half, ffh = D // 2, FF // 2
    rows = D // ND
    dims = (X, Y, Z, T, chunks, wd)
    c, place = lax.axis_index("c"), lax.axis_index(SEQ)

    local = qkv_weight.reshape(rows, 3, X, 2, half // X)
    kept = pick(local, c, 3).reshape(rows, 3 * half)
    given = pick(local, 1 - c, 3).reshape(rows, 3 * half)
    piece = jnp.stack([kept, swap(given)])
    cut = 3 * half // 2
    piece_a, piece_b = spread(piece[..., :cut], "z", Z), spread(piece[..., cut:], "z", Z)

    local = fc_weight.reshape(rows, X, 2, ffh // X)
    kept, given = (pick(local, n, 2).reshape(rows, ffh) for n in (c, 1 - c))
    wide = [slice(n, n + D) for n in range(0, ffh, D)]
    got = swap(jnp.concatenate([given[:, n] for n in wide], axis=0))
    fr = FF // ND
    low = jnp.concatenate([kept[:, wide[0]], got[:rows], proj_weight[: fr // 2], out_weight], axis=0)
    high = jnp.concatenate([kept[:, wide[1]], got[rows:], proj_weight[fr // 2 :]], axis=0)
    low, high, piece_a, piece_b = lax.optimization_barrier((low, high, piece_a, piece_b))
    low, high = (lax.all_gather(v, "z", axis=0, tiled=False) for v in (low, high))
    pieces = gather(piece_a, "x", X, "y", Y) + gather(piece_b, "y", Y, "x", X)

    small = (ln1_gain, ln1_shift, qv_bias, out_bias, ln2_gain, ln2_shift, fc_bias, proj_bias)
    cuts = [0]
    for part in small:
        cuts.append(cuts[-1] + part.shape[0])
    packed = jnp.broadcast_to(jnp.concatenate(small)[None, :], (ND, cuts[-1]))
    packed = lax.all_to_all(packed, ALL, split_axis=0, concat_axis=0, tiled=True).astype(F32)
    gain1, shift1, qv_all, out_b, gain2, shift2, fc_b, proj_b = (
        packed[:, cuts[n] : cuts[n + 1]].reshape(1, -1) for n in range(8)
    )
    fc_b_here = pick(fc_b.reshape(X, 2, ffh // X), c, 1).reshape(1, ffh)
    gain1, shift1, qv_all, out_b, gain2, shift2, fc_b_here, proj_b = lax.optimization_barrier(
        (gain1, shift1, qv_all, out_b, gain2, shift2, fc_b_here, proj_b)
    )

    slot = jnp.arange(sol_lens.shape[1], dtype=jnp.int32)
    used = jnp.where(slot < group_sizes[0], sol_lens[0], 0)
    ends = prefix_lens[0] + jnp.sum(jnp.where(slot[None, :] <= slot[:, None], used[None, :], 0), axis=1)
    meta = jnp.concatenate([prefix_lens, ends, jnp.zeros((15,), jnp.int32)])
    meta_peer = swap(meta)
    meta_here = jnp.where(place < chunks, meta, meta_peer)
    where = [lax.axis_index("x"), c, lax.axis_index("z"), lax.axis_index("y"), place, meta[16], meta_peer[16]]
    at = jnp.stack(where).astype(jnp.int32)

    own, cot = hidden[0], cotangent[0]
    peer, cot_peer = swap(own), swap(cot)

    qv_here = pick(qv_all.reshape(2, X, 2, half // X), c, 2).reshape(2, half)
    bias = jnp.concatenate([qv_here[:1], jnp.zeros_like(qv_here[:1]), qv_here[1:]], axis=1)
    msg, w_qkv, first, norm = project(dims, at, own, peer, gain1, shift1, bias, pieces)

    def exchange(array):
        return lax.all_to_all(array, SEQ, split_axis=0, concat_axis=0, tiled=True)

    qkv = exchange(msg)
    low, high = gather(low, "y", Y, "x", X), gather(high, "x", X, "y", Y)
    att, att_wide, lse = attend(qkv, meta_here, heads)
    w_peer = swap(jnp.stack([v[:, fr:] for v in low]))
    mine = exchange(att)
    theirs = swap(mine)

    resid, second, pre, w_own, w_fc = expand(
        dims, at, [own, peer, mine, theirs, out_b, gain2, shift2], fc_b_here, low, w_peer, high
    )
    out = contract(dims, at, cot, cot_peer, second, pre, w_fc, low, high)
    ahead, give, back, back_low, dy, fc_sum = out[:6]
    grads = lax.psum_scatter(out[6].reshape(X * Y, Z, -1, D), ("x", "y"), scatter_dimension=0, tiled=True)
    d_low, d_wide, d_msg, sums_mid = middle(dims, back, swap(back_low), resid, dy, gain2, w_own)
    up = exchange(d_msg)
    position = place * T + jnp.arange(T, dtype=jnp.int32)
    valid = (position < meta[16]).astype(F32)[:, None]
    layer_out = valid * (resid[:T] + (ahead + swap(give).astype(F32)) + proj_b)

    d_msg = attend_back(qkv, att_wide, lse, up, meta_here, heads)
    d_qkv = exchange(d_msg)
    out = list(project_back(dims, at, d_qkv, w_qkv, first, norm, mine, d_low))
    part, part_peer, qkv_sum, sums_first = out[:4]
    given = swap(part_peer)
    part_a, part_b = sent(out[4 : 4 + X], "x"), sent(out[4 + X :], "y")

    grads, _ = lax.optimization_barrier((grads, part))
    grads = lax.psum_scatter(grads[0], "z", scatter_dimension=0, tiled=True)[0].astype(F32)

    def both_halves(grad, blocks):
        kept = pick(grad, c, 0)
        got = swap(pick(grad, 1 - c, 0).astype(BF16)).astype(F32)
        shape = (kept.shape[0],) + blocks
        kept, got = kept.reshape(shape), got.reshape(shape)
        low = jnp.where(c == 0, kept, got)
        high = jnp.where(c == 0, got, kept)
        return jnp.stack([low, high], axis=-2).reshape(kept.shape[0], -1)

    fc_rows = 2 * ffh // D * rows
    fc_grad = grads[:fc_rows].reshape(2, ffh // D, rows, D).transpose(0, 2, 1, 3).reshape(2, rows, ffh)
    proj_grad = grads[fc_rows:]
    fc_grad = both_halves(fc_grad, (X, ffh // X))

    def own_columns(vector, lead):
        cut = vector.reshape(lead, X, 1, -1)
        spot = lax.broadcasted_iota(jnp.int32, (lead, X, 2, cut.shape[-1]), 2)
        return jnp.where(spot == c, cut, 0.0).reshape(-1)

    qv_sum = jnp.concatenate([qkv_sum[0, :half], qkv_sum[0, 2 * half :]])
    sums = (
        sums_first[0],
        sums_first[1],
        own_columns(qv_sum, 2),
        sums_mid[0],
        sums_mid[1],
        sums_mid[2],
        own_columns(fc_sum, 1),
        sums_mid[3],
    )
    packed = jnp.concatenate([v.reshape(ND, -1) for v in sums], axis=1).reshape(X, 2, Z, Y, -1)
    packed = scatter_sum(packed, "x", 0)

    part_a, part_b = combine(at, (3, 1, [part_a]), (0, 0, [part_b]))
    packed, *_ = lax.optimization_barrier((packed, *part_a, *part_b))
    part_a, part_b, packed = sent(part_a, "y"), sent(part_b, "x"), scatter_sum(packed, "y", 2)
    packed = scatter_sum(scatter_sum(packed, "c", 0), "z", 0)
    d_first = part + given.astype(F32)
    norm, inverse = layer_stats(own.astype(F32))
    hidden_grad = d_wide[:T] + layer_back(d_first, norm, inverse, gain1)
    hidden_grad, layer_out = hidden_grad.astype(BF16), layer_out.astype(BF16)
    hidden_grad, layer_out, packed, fc_grad, proj_grad, *ordered = lax.optimization_barrier(
        (hidden_grad, layer_out, packed, fc_grad, proj_grad, *part_a, *part_b)
    )
    last = combine(at, (2, 0, [ordered[:Y], ordered[Y:]]), wide=True)[0]
    last = sent(last, "z")
    last = sum(v.astype(F32) for v in last)
    value = last[2 * rows : 3 * rows].reshape(rows, 2, half).transpose(1, 0, 2)
    qkv_grad = jnp.concatenate([last[: 2 * rows].reshape(2, rows, D), value], axis=2)
    out_grad = last[3 * rows :]
    qkv_grad = both_halves(qkv_grad, (3, X, half // X))

    gain1_g, shift1_g, qv_g, out_b_g, gain2_g, shift2_g, fc_b_g, proj_b_g = (
        packed[cuts[n] : cuts[n + 1]] for n in range(8)
    )
    return (
        layer_out[None], hidden_grad[None], gain1_g, shift1_g, qkv_grad, qv_g, out_grad,
        out_b_g, gain2_g, shift2_g, fc_grad, fc_b_g, proj_grad, proj_b_g,
    )


def solution(mesh):
    Z = 4
    X, Y = mesh.shape["dp"] // 2, mesh.shape["seq"] // Z
    split = Mesh(mesh.devices.reshape(X, 2, Z, Y), ALL)
    group, wide, flat = P(("x", "c"), SEQ, None), P(ALL, None), P(ALL)
    dp = P(("x", "c"))
    return jax.shard_map(
        functools.partial(per_device, (X, Z, Y)),
        mesh=split,
        in_specs=(
            group, dp, dp, P(("x", "c"), None), flat, flat, wide, flat, wide, flat, flat, flat, wide, flat, wide, flat,
            group,
        ),
        out_specs=(
            group, group, flat, flat, wide, flat, wide, flat, flat, flat, wide, flat, wide, flat,
        ),
        check_vma=False,
    )
```
